32 devices in a mesh: dp: 2 (over x), row: 4 (over y, core), col: 4 (over z).
Axes of the slice: x: 2, y: 2, z: 4, core: 2. Of those that a mesh axis runs over, the one named last changes fastest.
Arguments:
- tokens: bfloat16 [768, 8192], P('col', ('dp', 'row')), may hold values from -6 to 6
- cotangent: bfloat16 [768, 8192], P('col', ('dp', 'row')), may hold values from -6 to 6
- segment_ids: int32 [8192], P('dp'), may hold values from 0 to 5, as said below
- doc_times: int32 [8, 7], P('dp'), may hold values from 0 to 255
- time_table: float32 [256, 128], replicated, may hold values from -6 to 6
- attn_gain: bfloat16 [768], P('col'), may hold values from 0.5 to 1.5
- mlp_gain: bfloat16 [768], P('col'), may hold values from 0.5 to 1.5
- mod_weight: bfloat16 [6, 768, 128], P(None, 'col'), may hold values from -0.25 to 0.25
- mod_bias: bfloat16 [6, 768], P(None, 'col'), may hold values from -4 to 4
- qkv_weight: bfloat16 [768, 3, 768], P('col', None, 'row'), may hold values from -0.21875 to 0.21875
- proj_weight: bfloat16 [768, 768], P('row', 'col'), may hold values from -3 to 3
- up_weight: bfloat16 [768, 3072], P('col', 'row'), may hold values from -2 to 2
- up_bias: bfloat16 [3072], P('row'), may hold values from -4 to 4
- down_weight: bfloat16 [768, 3072], P('col', 'row'), may hold values from -0.109375 to 0.109375
- down_bias: bfloat16 [768], P('col'), may hold values from -4 to 4
Outputs:
- block_output: bfloat16 [768, 8192], P('col', ('dp', 'row'))
- tokens_grad: bfloat16 [768, 8192], P('col', ('dp', 'row'))
- table_grad: float32 [256, 128], replicated
- attn_gain_grad: float32 [768], P('col')
- mlp_gain_grad: float32 [768], P('col')
- mod_weight_grad: float32 [6, 768, 128], P(None, 'col')
- mod_bias_grad: float32 [6, 768], P(None, 'col')
- qkv_weight_grad: float32 [768, 3, 768], P('col', None, 'row')
- proj_weight_grad: float32 [768, 768], P('row', 'col')
- up_weight_grad: float32 [768, 3072], P('col', 'row')
- up_bias_grad: float32 [3072], P('row')
- down_weight_grad: float32 [768, 3072], P('col', 'row')
- down_bias_grad: float32 [768], P('col')
- stream_rms: float32 [3], replicated
The draws below stay inside these ranges and needn't reach their ends.
Inputs may be any that keep to these rules, and one draw needn't show every extreme that they name: `segment_ids`: each sequence of 1024 tokens holds whole documents of 200 to min(2000, 1024) tokens with ids 1, 2, 3, ... in order, each a contiguous run, followed by padding with id 0; the first document always fits.
All inputs are finite; a program needn't handle non-finite values.
Results may differ from the reference program's by a relative error of at most 0.023.
Values may be sent and summed in bfloat16 or wider, within the bound.
No kernel may reach another device: no remote copies, remote signals or barrier semaphores. Data moves between devices by JAX's collectives and lax.ppermute only.
A program may use at most 192 MiB of HBM per device.

```python
import jax
import jax.numpy as jnp
from jax import lax

D = 768
H = 12
HEAD_DIM = 64
FF = 3072
COND = 128
SEQ = 1024
TIME_STEPS = 256
DOCS = 7
TOKENS = 8192
SEQS = 8


def draw_segment_ids(key, part):
    seq_total = TOKENS // SEQ
    longest = min(2000, SEQ)
    lengths = jax.random.randint(key, (seq_total, DOCS - 1), 200, longest + 1)
    first_row = (jnp.arange(seq_total, dtype=jnp.int32) == 0)[:, None]
    lengths = jnp.where(first_row, 200, lengths).astype(jnp.int32)
    doc_ends = jnp.cumsum(lengths, axis=1)
    positions = jnp.arange(SEQ, dtype=jnp.int32)
    before = jnp.sum((doc_ends[:, None, :] <= positions[None, :, None]).astype(jnp.int32), axis=2)
    own_end = jnp.take_along_axis(doc_ends, jnp.minimum(before, DOCS - 2), axis=1)
    seg_values = jnp.where(own_end <= SEQ, before + 1, 0)
    return seg_values.reshape(-1).astype(jnp.int32)


def draw_up_weight(key, part):
    base = jnp.clip(jax.random.normal(jax.random.fold_in(key, 11), (D, FF), jnp.float32), -6.0, 6.0)
    offset = jnp.clip(jax.random.normal(jax.random.fold_in(key, 23), (FF,), jnp.float32), -4.0, 4.0)
    return ((base + offset[None, :]) * D ** (-0.5)).astype(jnp.bfloat16)


def plant(array, stream_key, least, high):
    spot = [jax.random.randint(jax.random.fold_in(stream_key, axis), (), 0, length) for axis, length in enumerate(array.shape)]
    main_axis = array.shape.index(max(array.shape))
    next_to = spot[:main_axis] + [(spot[main_axis] + 1) % array.shape[main_axis]] + spot[main_axis + 1:]
    return array.at[tuple(spot)].set(least).at[tuple(next_to)].set(high)


def block_levels(rng, extent, cuts, smallest, high):
    level = 1.0
    for axis_at, shards_of in cuts:
        draws = jax.random.uniform(jax.random.fold_in(jax.random.fold_in(rng, 6), axis_at), (shards_of,), jnp.float32, smallest / len(cuts), high / len(cuts))
        level = level * jnp.repeat(jnp.exp(draws), extent[axis_at] // shards_of).reshape((-1,) + (1,) * (len(extent) - 1 - axis_at))
    return level


def noise(stream_key, extent, deviation, bound, split=(), kind=jnp.bfloat16):
    drawn = deviation * jax.random.normal(stream_key, extent, jnp.float32)
    if split:
        drawn = drawn * block_levels(stream_key, extent, split, -0.22, 0.18)
    return jnp.clip(drawn, -bound, bound).astype(kind)


def setup_inputs(seed: int = 0) -> dict:
    key_list = jax.random.split(jax.random.key(seed), 16)
    return {
        "tokens": noise(key_list[0], (D, TOKENS), 1.0, 6.0, ((0, 4), (1, 8))),
        "cotangent": noise(key_list[1], (D, TOKENS), 1.0, 6.0, ((0, 4), (1, 8))),
        "segment_ids": draw_segment_ids(jax.random.fold_in(key_list[15], 71), 0),
        "doc_times": plant(jax.random.randint(key_list[3], (SEQS, DOCS), 0, TIME_STEPS), jax.random.fold_in(key_list[3], 1), 0, TIME_STEPS - 1).astype(jnp.int32),
        "time_table": noise(key_list[4], (TIME_STEPS, COND), 1.0, 6.0, (), jnp.float32),
        "attn_gain": jnp.clip(1.0 + 0.1 * jax.random.normal(key_list[5], (D,), jnp.float32), 0.5, 1.5).astype(jnp.bfloat16),
        "mlp_gain": jnp.clip(1.0 + 0.1 * jax.random.normal(key_list[6], (D,), jnp.float32), 0.5, 1.5).astype(jnp.bfloat16),
        "mod_weight": noise(key_list[7], (6, D, COND), (4 * COND) ** -0.5, 0.25, ((1, 4),)),
        "mod_bias": noise(key_list[8], (6, D), 0.3, 4.0, ((1, 4),)),
        "qkv_weight": noise(key_list[9], (D, 3, D), D ** -0.5, 0.21875, ((0, 4), (2, 4))),
        "proj_weight": noise(key_list[10], (D, D), (max(1, D // 192)) ** -0.5, 3.0, ((0, 4), (1, 4))),
        "up_weight": draw_up_weight(jax.random.fold_in(key_list[15], 71), 0),
        "up_bias": noise(key_list[12], (FF,), 0.3, 4.0, ((0, 4),)),
        "down_weight": noise(key_list[13], (D, FF), FF ** -0.5, 0.109375, ((0, 4), (1, 4))),
        "down_bias": noise(key_list[14], (D,), 0.3, 4.0, ((0, 4),)),
    }


PRECISE = lax.Precision.HIGHEST
EPSILON = 1e-05
MASK_FILL = -1e+30

@jax.custom_vjp
def low(v):
    return lax.optimization_barrier(v.astype(jnp.bfloat16)).astype(jnp.float32)

@jax.custom_vjp
def low_back(v):
    return v

def low_keep(v):
    return (low(v), None)

def low_pass(kept, grad):
    return (grad,)

def back_keep(v):
    return (v, None)

def back_low(kept, grad):
    return (low(grad),)
low.defvjp(low_keep, low_pass)
low_back.defvjp(back_keep, back_low)

def matmul(left, right):
    return jnp.dot(left, right, precision=PRECISE)

def doc_positions(seg_rows):
    length = seg_rows.shape[1]
    places = jnp.broadcast_to(jnp.arange(length, dtype=jnp.int32)[None, :], seg_rows.shape)
    fresh_start = (places == 0) | (seg_rows != jnp.roll(seg_rows, 1, axis=1))
    starts = lax.cummax(jnp.where(fresh_start, places, 0), axis=1)
    return (places - starts).astype(jnp.float32)

def rope_tables(positions, head_size):
    half_size = head_size // 2
    inverse_freq = 1.0 / 10000.0 ** (jnp.arange(half_size, dtype=jnp.float32) * 2.0 / head_size)
    angles = positions[:, None] * inverse_freq[None, :]
    cosine_table = jnp.cos(angles)
    sine_table = jnp.sin(angles)
    return (jnp.concatenate([cosine_table, cosine_table], 1), jnp.concatenate([sine_table, sine_table], 1))

def rotate(vectors, cosine_table, sine_table):
    half_size = vectors.shape[-1] // 2
    turned = jnp.concatenate([-vectors[..., half_size:], vectors[..., :half_size]], -1)
    return vectors * cosine_table[:, None, :] + turned * sine_table[:, None, :]

def attend_block(queries, key_vecs, value_vecs, seg_query, seg_keys):
    score_scale = HEAD_DIM ** (-0.5)
    scores = low_back(jnp.einsum('qhd,khd->hqk', queries, key_vecs, precision=PRECISE) * score_scale)
    allowed = (seg_query[:, None] == seg_keys[None, :]) & (seg_keys[None, :] != 0)
    masked = jnp.where(allowed[None], scores, MASK_FILL)
    largest = lax.optimization_barrier(jnp.max(masked, axis=-1))
    exponent = jnp.where(allowed[None], jnp.exp(masked - largest[..., None]), 0.0)
    padding = (seg_query == 0).astype(jnp.float32)
    denominator = lax.optimization_barrier(jnp.sum(exponent, axis=-1)) + padding[None, :]
    probability = exponent / denominator[..., None]
    return jnp.einsum('hqk,khd->qhd', low(probability), value_vecs, precision=PRECISE)

def layer_norm(values, gain):
    center = lax.optimization_barrier(jnp.mean(values, axis=1, keepdims=True))
    spread = lax.optimization_barrier(jnp.mean((values - center) ** 2, axis=1, keepdims=True))
    return (values - center) * lax.rsqrt(spread + EPSILON) * gain

def layer_forward(weights, stream, doc_embed, seg_rows):
    attn_gain, mlp_gain, mod_weight, mod_bias, qkv_weight, proj_weight, up_weight, up_bias, down_weight, down_bias = weights
    length = stream.shape[0]
    width = stream.shape[1]
    doc_mods = jnp.einsum('jc,sdc->jsd', doc_embed, mod_weight, precision=PRECISE) + mod_bias[None]
    token_mods = jnp.take(doc_mods, seg_rows, axis=0)
    normed_attn = layer_norm(stream, attn_gain)
    input_attn = low(normed_attn * (1.0 + token_mods[:, 1]) + token_mods[:, 0])
    projected = low_back(matmul(input_attn, qkv_weight.reshape(width, 3 * width)))
    projected = projected.reshape(length, 3, H, HEAD_DIM)
    cosine_table, sine_table = rope_tables(doc_positions(seg_rows[None])[0], HEAD_DIM)
    queries = low(rotate(projected[:, 0], cosine_table, sine_table))
    key_vecs = low(rotate(projected[:, 1], cosine_table, sine_table))
    value_vecs = low(projected[:, 2])
    block_rows = min(512, length)

    def one_block(block_index):
        query_rows = lax.dynamic_slice_in_dim(queries, block_index * block_rows, block_rows, 0)
        seg_query = lax.dynamic_slice_in_dim(seg_rows, block_index * block_rows, block_rows, 0)
        return attend_block(query_rows, key_vecs, value_vecs, seg_query, seg_rows)
    mixed_out = lax.map(jax.checkpoint(one_block), jnp.arange(length // block_rows))
    mixed_out = low_back(low(mixed_out.reshape(length, width)))
    attn_out = low_back(matmul(mixed_out, proj_weight))
    attn_term = token_mods[:, 2] * attn_out
    middle = stream + attn_term
    normed_mlp = layer_norm(middle, mlp_gain)
    input_mlp = low(normed_mlp * (1.0 + token_mods[:, 4]) + token_mods[:, 3])
    hidden_pre = low_back(matmul(input_mlp, up_weight) + up_bias)
    hidden_low = low(jax.nn.gelu(hidden_pre, approximate=True))
    mlp_out = low_back(matmul(hidden_low, down_weight.T) + down_bias)
    mlp_term = token_mods[:, 5] * mlp_out
    return (middle + mlp_term, attn_term, mlp_term)

def reference(tokens, cotangent, segment_ids, doc_times, time_table, attn_gain, mlp_gain, mod_weight, mod_bias, qkv_weight, proj_weight, up_weight, up_bias, down_weight, down_bias):
    weights = tuple((weight_item.astype(jnp.float32) for weight_item in (attn_gain, mlp_gain, mod_weight, mod_bias, qkv_weight, proj_weight, up_weight, up_bias, down_weight, down_bias)))
    seq_total = segment_ids.shape[0] // SEQ
    stream_all = tokens.astype(jnp.float32).T.reshape(seq_total, SEQ, D)
    grads_all = cotangent.astype(jnp.float32).T.reshape(seq_total, SEQ, D)
    segs_all = segment_ids.reshape(seq_total, SEQ)
    table_float = time_table.astype(jnp.float32)

    def seq_step(running, packed):
        weight_sums, table_sum, stat_sums = running
        stream, grad_out, seg_rows, doc_slots = packed
        doc_embed = jnp.take(table_float, doc_slots, axis=0)

        def forward_part(weight_list, values, embedding):
            return layer_forward(weight_list, values, embedding, seg_rows)
        outputs, pullback = jax.vjp(forward_part, weights, stream, doc_embed)
        result, attn_term, mlp_term = outputs
        zero_term = jnp.zeros_like(result)
        weight_grads, stream_grad, embed_grad = pullback((grad_out, zero_term, zero_term))
        table_sum = table_sum.at[doc_slots].add(embed_grad)
        valid_rows = (seg_rows != 0).astype(jnp.float32)[:, None]
        stat_terms = jnp.stack([jnp.sum(valid_rows * result ** 2), jnp.sum(valid_rows * attn_term ** 2), jnp.sum(valid_rows * mlp_term ** 2), jnp.sum(valid_rows) * D])
        weight_sums = jax.tree.map(jnp.add, weight_sums, weight_grads)
        return ((weight_sums, table_sum, stat_sums + stat_terms), (result.astype(jnp.bfloat16), stream_grad.astype(jnp.bfloat16)))
    initial = (jax.tree.map(jnp.zeros_like, weights), jnp.zeros_like(table_float), jnp.zeros((4,), jnp.float32))
    finals, stacked = lax.scan(seq_step, initial, (stream_all, grads_all, segs_all, doc_times))
    weight_sums, table_sum, stat_sums = finals
    results, stream_grads = stacked
    stream_rms = jnp.sqrt(stat_sums[:3] / stat_sums[3])
    return (results.reshape(-1, D).T, stream_grads.reshape(-1, D).T, table_sum, weight_sums[0], weight_sums[1], weight_sums[2], weight_sums[3], weight_sums[4], weight_sums[5], weight_sums[6], weight_sums[7], weight_sums[8], weight_sums[9], stream_rms)
```

```python
import jax
import jax.numpy as jnp
from jax import lax
from jax.sharding import PartitionSpec as P

HEAD_DIM = 64
SEQ = 1024

PRECISE = lax.Precision.HIGHEST
EPSILON = 1e-05
MASK_FILL = -1e30
LOW = jnp.bfloat16
FULL = jnp.float32


def swap(values, axis, bit):
    count = lax.axis_size(axis)
    return lax.ppermute(values, axis, [(i, i ^ bit) for i in range(count)])


def row_bits():
    count = lax.axis_size("row")
    bits = []
    bit = 1
    while bit < count:
        bits.append(bit)
        bit *= 2
    return bits


def gather_rows(values):
    for bit in reversed(row_bits()):
        values = jnp.concatenate([values, swap(values, "row", bit)], 0)
    return values


def xor_order():
    order = [0]
    for bit in reversed(row_bits()):
        order = order + [o ^ bit for o in order]
    return order


def scatter_rows(values):
    for bit in row_bits():
        half = values.shape[0] // 2
        received = swap(values[half:], "row", bit)
        values = (values[:half].astype(FULL) + received.astype(FULL)).astype(LOW)
    return values.astype(FULL)


def col_of_row(row_count):
    if row_count == 4:
        return [0, 2, 1, 3]
    return list(range(row_count))


def relayout_pairs(step):
    row_count = lax.axis_size("row")
    col_count = lax.axis_size("col")
    per_row = col_count // row_count
    table = col_of_row(row_count)
    pairs = []
    for r in range(row_count):
        for c in range(col_count):
            j, q = divmod((c + step) % col_count, row_count)
            pairs.append((r * col_count + c, q * col_count + table[r] * per_row + j))
    return pairs


def relayout_in(values):
    row_count = lax.axis_size("row")
    col_count = lax.axis_size("col")
    col_index = lax.axis_index("col")
    row_index = lax.axis_index("row")
    per_row = col_count // row_count
    width_local = values.shape[0]
    own = values.shape[1] // col_count
    table = jnp.array(col_of_row(row_count), jnp.int32)
    chunks = values.reshape(width_local, col_count, own)
    result = jnp.zeros((width_local * col_count, own), values.dtype)
    mine = col_index % per_row * row_count + row_index
    for step in range(col_count):
        piece = lax.dynamic_index_in_dim(chunks, (col_index + step) % col_count, 1, False)
        got = lax.ppermute(piece, ("row", "col"), relayout_pairs(step))
        source = (mine - step) % col_count
        result = lax.dynamic_update_slice(result, got, (source * width_local, 0))
    return result


def relayout_out(values):
    row_count = lax.axis_size("row")
    col_count = lax.axis_size("col")
    col_index = lax.axis_index("col")
    row_index = lax.axis_index("row")
    per_row = col_count // row_count
    width_local = values.shape[0] // col_count
    own = values.shape[1]
    result = jnp.zeros((width_local, col_count, own), values.dtype)
    mine = col_index % per_row * row_count + row_index
    for step in range(col_count):
        source = (mine - step) % col_count
        piece = lax.dynamic_slice_in_dim(values, source * width_local, width_local, 0)
        got = lax.ppermute(
            piece, ("row", "col"), [(b, a) for a, b in relayout_pairs(step)]
        )
        result = lax.dynamic_update_slice(
            result, got[:, None, :], (0, (col_index + step) % col_count, 0)
        )
    return result.reshape(width_local, col_count * own)


def rope_tables(positions, head_size):
    half_size = head_size // 2
    inverse_freq = 1.0 / 10000.0 ** (jnp.arange(half_size, dtype=FULL) * 2.0 / head_size)
    angles = positions[:, None] * inverse_freq[None, :]
    cosine_table = jnp.cos(angles)
    sine_table = jnp.sin(angles)
    return (
        jnp.concatenate([cosine_table, cosine_table], 1),
        jnp.concatenate([sine_table, sine_table], 1),
    )


def rotate(vectors, cosine_table, sine_table):
    half_size = vectors.shape[-1] // 2
    turned = jnp.concatenate([-vectors[..., half_size:], vectors[..., :half_size]], -1)
    return vectors * cosine_table[:, None, :] + turned * sine_table[:, None, :]


def rotate_back(grads, cosine_table, sine_table):
    half_size = grads.shape[-1] // 2
    scaled = grads * sine_table[:, None, :]
    turned_back = jnp.concatenate([scaled[..., half_size:], -scaled[..., :half_size]], -1)
    return grads * cosine_table[:, None, :] + turned_back


def gelu_back(hidden_pre, hidden_grad):

    def activation(inner):
        return jax.nn.gelu(inner, approximate=True)

    return jax.vjp(activation, hidden_pre)[1](hidden_grad)[0]


def normalize(stream):
    center = jnp.mean(stream, axis=1, keepdims=True)
    offset = stream - center
    inverse = lax.rsqrt(jnp.mean(offset * offset, axis=1, keepdims=True) + EPSILON)
    return offset * inverse, inverse


def normalize_back(grad_normed, normed, inverse):
    center = jnp.mean(grad_normed, axis=1, keepdims=True)
    along = jnp.mean(grad_normed * normed, axis=1, keepdims=True)
    return inverse * (grad_normed - center - normed * along)


def dot(left, right, left_dim, right_dim):
    return lax.dot_general(
        left, right, (((left_dim,), (right_dim,)), ((), ())), preferred_element_type=FULL
    )


def attention_forward(queries, key_vecs, value_vecs, segs):
    score_scale = HEAD_DIM ** (-0.5)
    scores = jnp.einsum("qhd,khd->hqk", queries, key_vecs, preferred_element_type=FULL) * score_scale
    allowed = (segs[:, None] == segs[None, :]) & (segs[None, :] != 0)
    masked = jnp.where(allowed[None], scores, MASK_FILL)
    largest = jnp.max(masked, axis=-1)
    exponent = jnp.where(allowed[None], jnp.exp(masked - largest[..., None]), 0.0)
    padding = (segs == 0).astype(FULL)
    denominator = jnp.sum(exponent, axis=-1) + padding[None, :]
    probability = exponent / denominator[..., None]
    mixed_out = jnp.einsum(
        "hqk,khd->qhd", probability.astype(LOW), value_vecs, preferred_element_type=FULL
    )
    return mixed_out, largest + jnp.log(denominator)


def attention_backward(queries, key_vecs, value_vecs, segs, logsum, grad_mixed):
    score_scale = HEAD_DIM ** (-0.5)
    scores = jnp.einsum("qhd,khd->hqk", queries, key_vecs, preferred_element_type=FULL) * score_scale
    allowed = (segs[:, None] == segs[None, :]) & (segs[None, :] != 0)
    masked = jnp.where(allowed[None], scores, MASK_FILL)
    probability = jnp.where(allowed[None], jnp.exp(masked - logsum[..., None]), 0.0)
    grad_probs = jnp.einsum("qhd,khd->hqk", grad_mixed, value_vecs, preferred_element_type=FULL)
    value_grad = jnp.einsum(
        "hqk,qhd->khd", probability.astype(LOW), grad_mixed, preferred_element_type=FULL
    )
    inner_sum = jnp.sum(probability * grad_probs, axis=-1)
    score_grad = (probability * (grad_probs - inner_sum[..., None])).astype(LOW)
    query_grad = (
        jnp.einsum("hqk,khd->qhd", score_grad, key_vecs, preferred_element_type=FULL) * score_scale
    )
    key_grad = (
        jnp.einsum("hqk,qhd->khd", score_grad, queries, preferred_element_type=FULL) * score_scale
    )
    return query_grad, key_grad, value_grad


def per_device(
    tokens,
    cotangent,
    segment_ids,
    doc_times,
    time_table,
    attn_gain,
    mlp_gain,
    mod_weight,
    mod_bias,
    qkv_weight,
    proj_weight,
    up_weight,
    up_bias,
    down_weight,
    down_bias,
):
    row_count = lax.axis_size("row")
    col_count = lax.axis_size("col")
    row_index = lax.axis_index("row")
    col_index = lax.axis_index("col")
    per_row = col_count // row_count
    width_local = tokens.shape[0]
    width = width_local * col_count
    own = tokens.shape[1] // col_count
    head_width = qkv_weight.shape[2]
    heads_local = head_width // HEAD_DIM
    slot_count = doc_times.shape[1]
    cond_width = mod_weight.shape[2]
    if segment_ids.shape[0] != col_count * SEQ or own * row_count != SEQ:
        raise ValueError("sequence split")

    table = col_of_row(row_count)
    seq_of_col = [0] * col_count
    for r in range(row_count):
        for j in range(per_row):
            seq_of_col[table[r] * per_row + j] = r * per_row + j
    seq_segs = segment_ids.reshape(col_count, SEQ)[jnp.array(seq_of_col)]
    seq_times = doc_times[jnp.array(seq_of_col)]

    segs_natural = lax.dynamic_index_in_dim(seq_segs, col_index, 0, False)
    places = jnp.arange(SEQ, dtype=jnp.int32)
    slots = jnp.arange(slot_count, dtype=jnp.int32)
    starts = jnp.min(
        jnp.where(segs_natural[None, :] == slots[:, None], places[None, :], SEQ), axis=1
    )
    start_of = jnp.sum(jnp.where(segs_natural[None, :] == slots[:, None], starts[:, None], 0), axis=0)
    positions_natural = (places - start_of).astype(FULL)
    order = jnp.array(xor_order(), jnp.int32) ^ row_index
    segs = segs_natural.reshape(row_count, own)[order].reshape(-1)
    positions = positions_natural.reshape(row_count, own)[order].reshape(-1)
    own_segs = segs[:own]

    doc_embed = jnp.take(time_table, seq_times.reshape(-1), axis=0)
    mod_full = mod_weight.astype(FULL).transpose(2, 0, 1).reshape(cond_width, 6 * width_local)
    doc_mods_part = jnp.dot(doc_embed, mod_full, precision=PRECISE) + mod_bias.astype(FULL).reshape(-1)
    doc_mods_part = doc_mods_part.reshape(col_count, slot_count * 6, width_local)
    vectors = jnp.stack([attn_gain, mlp_gain, down_bias]).astype(FULL)
    mods_send = jnp.concatenate(
        [doc_mods_part, jnp.broadcast_to(vectors[None], (col_count,) + vectors.shape)], 1
    )
    mods_got = lax.all_to_all(mods_send, "col", 0, 2, tiled=True).reshape(-1, width)
    doc_mods = mods_got[: slot_count * 6].reshape(slot_count, 6 * width)
    gain_one, gain_two, down_bias_full = mods_got[-3], mods_got[-2], mods_got[-1]
    selector = (own_segs[:, None] == slots[None, :]).astype(FULL)
    token_mods = jnp.dot(selector, doc_mods, precision=PRECISE).reshape(own, 6, width)
    shift_one, scale_one, gate_one, shift_two, scale_two, gate_two = [
        token_mods[:, i] for i in range(6)
    ]

    def gather_cols(values):
        return lax.all_gather(values, "col", axis=0, tiled=True)

    qkv_full = gather_cols(qkv_weight.reshape(width_local, 3 * head_width))
    proj_full = gather_cols(proj_weight.T)
    up_full = gather_cols(up_weight)
    down_full = gather_cols(down_weight)

    stream = relayout_in(tokens).T.astype(FULL)
    normed_one, inverse_one = normalize(stream)
    scaled_one = normed_one * gain_one
    input_one = (scaled_one * (1.0 + scale_one) + shift_one).astype(LOW)
    rows_one = gather_rows(input_one)
    projected = dot(rows_one, qkv_full, 1, 0)
    cosine_table, sine_table = rope_tables(positions, HEAD_DIM)
    split_heads = projected.reshape(SEQ, 3, heads_local, HEAD_DIM)
    queries = rotate(split_heads[:, 0], cosine_table, sine_table).astype(LOW)
    key_vecs = rotate(split_heads[:, 1], cosine_table, sine_table).astype(LOW)
    value_vecs = split_heads[:, 2].astype(LOW)
    mixed_out, logsum = attention_forward(queries, key_vecs, value_vecs, segs)
    mixed = mixed_out.reshape(SEQ, head_width).astype(LOW)
    attn_out = scatter_rows(dot(mixed, proj_full, 1, 1).astype(LOW))

    grad_result = relayout_in(cotangent).T.astype(FULL)
    grad_branch = (grad_result * gate_two).astype(LOW)
    branch_rows = gather_rows(grad_branch)

    middle = stream + gate_one * attn_out
    normed_two, inverse_two = normalize(middle)
    scaled_two = normed_two * gain_two
    input_two = (scaled_two * (1.0 + scale_two) + shift_two).astype(LOW)
    rows_two = gather_rows(input_two)
    hidden_pre = dot(rows_two, up_full, 1, 0) + up_bias.astype(FULL)
    hidden = jax.nn.gelu(hidden_pre, approximate=True).astype(LOW)
    mlp_out = scatter_rows(dot(hidden, down_full, 1, 1).astype(LOW)) + down_bias_full

    hidden_grad = dot(branch_rows, down_full, 1, 0)
    pre_grad = gelu_back(hidden_pre, hidden_grad).astype(LOW)
    input_grad_two = scatter_rows(dot(pre_grad, up_full, 1, 1).astype(LOW))
    down_grad_part = dot(branch_rows, hidden, 0, 0)
    up_grad_part = dot(rows_two, pre_grad, 0, 0)
    up_bias_part = jnp.sum(pre_grad.astype(FULL), axis=0)

    result = middle + gate_two * mlp_out
    block_output = relayout_out(result.astype(LOW).T)
    valid_rows = (own_segs != 0).astype(FULL)[:, None]
    attn_term = gate_one * attn_out
    mlp_term = gate_two * mlp_out
    stat_terms = jnp.stack(
        [
            jnp.sum(valid_rows * result * result),
            jnp.sum(valid_rows * attn_term * attn_term),
            jnp.sum(valid_rows * mlp_term * mlp_term),
            jnp.sum(valid_rows) * width,
        ]
    )
    grad_gate_two = grad_result * mlp_out
    down_bias_part = jnp.sum(grad_branch.astype(FULL), axis=0)

    grad_scaled_two = input_grad_two * (1.0 + scale_two)
    gain_two_part = jnp.sum(grad_scaled_two * normed_two, axis=0)
    grad_middle = grad_result + normalize_back(grad_scaled_two * gain_two, normed_two, inverse_two)
    grad_gate_one = grad_middle * attn_out
    grad_attn = (grad_middle * gate_one).astype(LOW)
    attn_rows = gather_rows(grad_attn)
    proj_grad_part = dot(attn_rows, mixed, 0, 0)
    grad_mixed = dot(attn_rows, proj_full, 1, 0).astype(LOW)
    query_grad, key_grad, value_grad = attention_backward(
        queries, key_vecs, value_vecs, segs, logsum, grad_mixed.reshape(SEQ, heads_local, HEAD_DIM)
    )
    query_back = rotate_back(query_grad, cosine_table, sine_table)
    key_back = rotate_back(key_grad, cosine_table, sine_table)
    qkv_grad = (
        jnp.stack([query_back, key_back, value_grad], axis=1).reshape(SEQ, 3 * head_width).astype(LOW)
    )
    qkv_grad_part = dot(rows_one, qkv_grad, 0, 0)
    input_grad_one = scatter_rows(dot(qkv_grad, qkv_full, 1, 1).astype(LOW))
    grad_scaled_one = input_grad_one * (1.0 + scale_one)
    gain_one_part = jnp.sum(grad_scaled_one * normed_one, axis=0)
    grad_stream = grad_middle + normalize_back(grad_scaled_one * gain_one, normed_one, inverse_one)
    tokens_grad = relayout_out(grad_stream.astype(LOW).T)

    def sum_weight(part):
        part = lax.psum_scatter(part.astype(LOW), "col", scatter_dimension=0, tiled=True)
        return sum_dp(part)

    def sum_dp(part):
        total = part.astype(FULL)
        bit = 1
        while bit < lax.axis_size("dp"):
            total = total + swap(total.astype(LOW), "dp", bit).astype(FULL)
            bit *= 2
        return total

    qkv_out = sum_weight(qkv_grad_part).reshape(width_local, 3, head_width)
    proj_out = sum_weight(proj_grad_part).T
    up_out = sum_weight(up_grad_part)
    down_out = sum_weight(down_grad_part)
    up_bias_out = lax.psum(up_bias_part.astype(LOW), ("dp", "col")).astype(FULL)

    token_mod_grads = jnp.stack(
        [
            input_grad_one,
            input_grad_one * scaled_one,
            grad_gate_one,
            input_grad_two,
            input_grad_two * scaled_two,
            grad_gate_two,
        ],
        axis=1,
    ).reshape(own, 6 * width)
    doc_grads = lax.dot_general(
        selector, token_mod_grads, (((0,), (0,)), ((), ())), precision=PRECISE
    )
    small = jnp.concatenate(
        [
            doc_grads.reshape(slot_count * 6, width),
            jnp.stack([gain_one_part, gain_two_part, down_bias_part]),
        ],
        0,
    )
    small = lax.psum(small, "row")
    small = lax.all_to_all(
        small.reshape(1, -1, col_count, width_local).transpose(2, 1, 0, 3), "col", 0, 0, tiled=True
    )[:, :, 0]
    small = lax.all_gather(small, "dp", axis=0, tiled=True)
    all_embed = lax.all_gather(doc_embed, "dp", axis=0, tiled=True)
    all_times = lax.all_gather(seq_times, "dp", axis=0, tiled=True)
    vector_out = jnp.sum(small[:, slot_count * 6 :], axis=0)
    slot_grads = small[:, : slot_count * 6].reshape(-1, 6 * width_local)
    mod_bias_out = jnp.sum(slot_grads, axis=0).reshape(6, width_local)
    mod_weight_out = (
        lax.dot_general(slot_grads, all_embed, (((0,), (0,)), ((), ())), precision=PRECISE)
    ).reshape(6, width_local, cond_width)
    embed_grads = lax.dot_general(slot_grads, mod_full, (((1,), (1,)), ((), ())), precision=PRECISE)
    time_select = (
        all_times.reshape(-1)[:, None] == jnp.arange(time_table.shape[0], dtype=jnp.int32)[None, :]
    ).astype(FULL)
    embed_grads = lax.psum(embed_grads, "col")
    table_out = lax.dot_general(
        time_select, embed_grads, (((0,), (0,)), ((), ())), precision=PRECISE
    )
    stats = lax.psum(stat_terms, ("dp", "row", "col"))
    stream_rms = jnp.sqrt(stats[:3] / stats[3])
    return (
        block_output,
        tokens_grad,
        table_out,
        vector_out[0],
        vector_out[1],
        mod_weight_out,
        mod_bias_out,
        qkv_out,
        proj_out,
        up_out,
        up_bias_out,
        down_out,
        vector_out[2],
        stream_rms,
    )


def solution(mesh):
    return jax.shard_map(
        per_device,
        mesh=mesh,
        in_specs=(
            P("col", ("dp", "row")),
            P("col", ("dp", "row")),
            P("dp"),
            P("dp", None),
            P(),
            P("col"),
            P("col"),
            P(None, "col", None),
            P(None, "col"),
            P("col", None, "row"),
            P("row", "col"),
            P("col", "row"),
            P("row"),
            P("col", "row"),
            P("col"),
        ),
        out_specs=(
            P("col", ("dp", "row")),
            P("col", ("dp", "row")),
            P(),
            P("col"),
            P("col"),
            P(None, "col", None),
            P(None, "col"),
            P("col", None, "row"),
            P("row", "col"),
            P("col", "row"),
            P("row"),
            P("col", "row"),
            P("col"),
            P(),
        ),
        check_vma=False,
    )
```

```python
import functools

import jax
import jax.numpy as jnp
from jax import lax
from jax.experimental import pallas as pl
from jax.experimental.pallas import tpu as pltpu
from jax.sharding import PartitionSpec as P

HEAD_DIM = 64
SEQ = 1024

PRECISE = lax.Precision.HIGHEST
EPSILON = 1e-05
MASK_FILL = -1e30
MASK_FLOOR = -1e29
LOW = jnp.bfloat16
FULL = jnp.float32
SLOTS = 8
LANES = 64
GAIN_ONE, GAIN_TWO, DOWN_BIAS = 48, 49, 50
STATS = 51
VMEM_SMALL = 12 * 1024 * 1024
VMEM_LARGE = 56 * 1024 * 1024
VMEM_LIMIT = {
    name: VMEM_LARGE
    for name in ("attend", "feed_first", "feed_grads", "feed_out", "attend_back", "attend_weights")
}


def swap(values, axis, bit):
    count = lax.axis_size(axis)
    return lax.ppermute(values, axis, [(i, i ^ bit) for i in range(count)])


def gather_rows(values, filler=None, deps=()):
    far = swap(values, "row", 2)
    near = swap(values, "row", 1)
    filled = None
    if filler is not None:
        filled = filler(near)
        deps = list(deps) + list(filled[:1])
    if deps:
        [far] = after(deps, [far])
    last = swap(far, "row", 1)
    pieces = [values, near, far, last]
    return pieces if filler is None else (pieces, after([last], filled))


def scatter_rows(parts, filler=None, hold=False):
    width = parts[0].shape[0]
    near = swap(parts[2], "row", 1)
    total = (parts[1].astype(FULL) + near[width:].astype(FULL)).astype(LOW)
    far = swap(total, "row", 2)
    if filler is None:
        return [parts[0], near, far]
    filled = filler(total)
    [far] = after(filled[:1], [far])
    return [parts[0], near, far], after([far], filled) if hold else filled


def col_of_row(row_count):
    if row_count == 4:
        return [0, 2, 1, 3]
    return list(range(row_count))


def relayout_pairs(step):
    row_count = lax.axis_size("row")
    col_count = lax.axis_size("col")
    per_row = col_count // row_count
    table = col_of_row(row_count)
    pairs = []
    for r in range(row_count):
        for c in range(col_count):
            j, q = divmod((c + step) % col_count, row_count)
            pairs.append((r * col_count + c, q * col_count + table[r] * per_row + j))
    return pairs


def relayout(pieces, back=False):
    got = []
    for step, piece in enumerate(pieces):
        pairs = relayout_pairs(step)
        if back:
            pairs = [(b, a) for a, b in pairs]
        got.append(lax.ppermute(piece, ("row", "col"), pairs))
    return got


def after(deps, values):
    return lax.optimization_barrier((list(values), list(deps)))[0]


class Grid:
    def __init__(self):
        self.rows = lax.axis_size("row")
        self.cols = lax.axis_size("col")
        self.per_row = self.cols // self.rows
        table = col_of_row(self.rows)
        self.seq_of_col = [0] * self.cols
        for r in range(self.rows):
            for j in range(self.per_row):
                self.seq_of_col[table[r] * self.per_row + j] = r * self.per_row + j

    def row(self):
        return lax.axis_index("row")

    def col(self):
        return lax.axis_index("col")

    def sequence(self):
        return sum(jnp.where(self.col() == c, s, 0) for c, s in enumerate(self.seq_of_col))

    def half(self):
        return lax.axis_index("dp") % 2

    def half_start(self, block, which, size):
        return pl.multiple_of((2 * block + which) * size, size)

    def source(self, step):
        mine = self.col() % self.per_row * self.rows + self.row()
        return (mine + self.cols - step) % self.cols

    def place(self, step):
        return (self.col() + step) % self.cols


def whole(memory_space=pltpu.VMEM):
    return pl.BlockSpec(memory_space=memory_space)


class Far:
    def __init__(self, value):
        self.value = value


class FarIn:
    def __init__(self, source, buffer, sem):
        self.copy = pltpu.make_async_copy(source, buffer, sem)
        self.buffer, self.waiting = buffer, True
        self.copy.start()

    @property
    def shape(self):
        return self.buffer.shape

    @property
    def ref(self):
        if self.waiting:
            self.copy.wait()
            self.waiting = False
        return self.buffer

    @property
    def at(self):
        return self.ref.at

    def __getitem__(self, index):
        return self.ref[index]


class FarOut:
    def __init__(self, buffer, target, sem):
        self.copy = pltpu.make_async_copy(buffer, target, sem)
        self.ref, self.shipped = buffer, False

    @property
    def shape(self):
        return self.ref.shape

    @property
    def at(self):
        return self.ref.at

    def __getitem__(self, index):
        return self.ref[index]

    def __setitem__(self, index, value):
        self.ref[index] = value

    def ship(self):
        if not self.shipped:
            self.copy.start()
            self.shipped = True


def ship(*refs):
    for ref in refs:
        if isinstance(ref, FarOut):
            ref.ship()


def run(body, name, outs, args, scratch=(), smem=0, flops=0):
    far_args = [isinstance(a, Far) for a in args]
    far_outs = [isinstance(o, Far) for o in outs]
    args = [a.value if isinstance(a, Far) else a for a in args]
    outs = [o.value if isinstance(o, Far) else o for o in outs]
    buffers = [pltpu.VMEM(a.shape, a.dtype) for a, far in zip(args + outs, far_args + far_outs) if far]
    moved = sum(a.size * a.dtype.itemsize for a in args + outs)

    def kernel(*refs):
        ins, rest = list(refs[: len(args)]), refs[len(args) :]
        results, rest = list(rest[: len(outs)]), rest[len(outs) :]
        own, rest = rest[: len(scratch)], list(rest[len(scratch) :])
        count = 0
        for i, far in enumerate(far_args):
            if far:
                ins[i] = FarIn(ins[i], rest[count], rest[-1].at[count])
                count += 1
        for i, far in enumerate(far_outs):
            if far:
                results[i] = FarOut(rest[count], results[i], rest[-1].at[count])
                count += 1
        body(*ins, *results, *own)
        for ref in results:
            ship(ref)
        for ref in ins:
            if isinstance(ref, FarIn):
                ref.ref
        for ref in results:
            if isinstance(ref, FarOut):
                ref.copy.wait()

    def spec(far):
        return whole(pl.ANY) if far else whole()

    found = pl.pallas_call(
        kernel if buffers else body,
        out_shape=outs,
        in_specs=[whole(pltpu.SMEM)] * smem + [spec(far) for far in far_args[smem:]],
        out_specs=[spec(far) for far in far_outs],
        scratch_shapes=list(scratch) + buffers
        + ([pltpu.SemaphoreType.DMA((len(buffers),))] if buffers else []),
        compiler_params=pltpu.CompilerParams(vmem_limit_bytes=VMEM_LIMIT.get(name, VMEM_SMALL)),
        cost_estimate=pl.CostEstimate(flops=flops, bytes_accessed=moved, transcendentals=0),
        name=name,
    )(*args)
    return list(found)


def far_all(values):
    return [Far(v) for v in values]


def shape(dims, dtype):
    return jax.ShapeDtypeStruct(dims, dtype)


def dot(left, right, dims, precision=None):
    return lax.dot_general(
        left, right, (((dims[0],), (dims[1],)), ((), ())),
        preferred_element_type=FULL, precision=precision,
    )


def split(values, terms):
    found = []
    for _ in range(terms):
        term = values.astype(LOW).astype(FULL)
        found.append(term)
        values = values - term
    return found


def block_start(index, size):
    return pl.multiple_of(index * size, size)


def token_mods_of(mods, segs):
    terms = jnp.concatenate(split(mods, 2), 1).astype(LOW)
    rows = lax.broadcasted_iota(jnp.int32, (2 * LANES, segs.shape[1]), 0) % LANES

    def pick(k):
        chosen = (rows == segs + k * SLOTS).astype(LOW)
        return dot(terms, chosen, (1, 0))

    return pick


def part_of(parts, e):
    if e % 2 == 0:
        return parts[e // 2]
    width = parts[0].shape[0]
    return parts[2].at[(e // 2) * width : (e // 2 + 1) * width]


def ship_part(parts, e):
    if e != 3:
        ship({1: parts[2], 2: parts[1], 0: parts[0]}[e])


def three_terms(part, near, far):
    return (
        part[...].astype(FULL) + near[: part.shape[0], :].astype(FULL) + far[...].astype(FULL)
    )


def normalize(stream):
    count = 1.0 / stream.shape[0]
    center = jnp.sum(stream, axis=0, keepdims=True) * count
    offset = stream - center
    inverse = lax.rsqrt(jnp.sum(offset * offset, axis=0, keepdims=True) * count + EPSILON)
    return offset * inverse, inverse


def normalize_back(grad_normed, normed, inverse):
    count = 1.0 / normed.shape[0]
    center = jnp.sum(grad_normed, axis=0, keepdims=True) * count
    along = jnp.sum(grad_normed * normed, axis=0, keepdims=True) * count
    return inverse * (grad_normed - center - normed * along)


def prepare(grid, slot_count, times, table, weight, bias, gain_one, gain_two, down_bias, tokens, cot, *rest):
    outs, (embed, rows, blocks) = rest[: grid.cols], rest[grid.cols :]
    own = (outs[0].shape[1] - 2 * LANES) // 2
    rows[...] = jnp.zeros_like(rows)
    for k in range(6):
        rows[k * SLOTS : (k + 1) * SLOTS, :] = jnp.broadcast_to(
            bias[k : k + 1, :].astype(FULL), (SLOTS, rows.shape[1])
        )
    rows[GAIN_ONE : GAIN_ONE + 1, :] = gain_one[...].astype(FULL)[None]
    rows[GAIN_TWO : GAIN_TWO + 1, :] = gain_two[...].astype(FULL)[None]
    rows[DOWN_BIAS : DOWN_BIAS + 1, :] = down_bias[...].astype(FULL)[None]
    fixed = rows[...].T
    cond = weight.shape[2]
    flat = jnp.concatenate([weight[k] for k in range(6)], 1)
    row = lax.broadcasted_iota(jnp.int32, (LANES, 6 * cond), 0)
    lane = lax.broadcasted_iota(jnp.int32, (LANES, 6 * cond), 1)
    match = row // SLOTS == lane // cond
    for j in range(grid.per_row):
        embed[...] = jnp.zeros_like(embed)
        for slot in range(slot_count):
            time = times[grid.row() * grid.per_row + j, slot]
            embed[slot : slot + 1, :] = table[pl.ds(time, 1), :]
        tiled = jnp.concatenate([embed[...]] * (LANES // SLOTS), 0)
        tiled = jnp.concatenate([tiled] * 6, 1)
        total = fixed
        for term in split(jnp.where(match, tiled, 0.0), 3):
            total = total + dot(flat, term.astype(LOW), (1, 1))
        blocks[j] = jnp.concatenate(split(total, 2), 1).astype(LOW)
    for step in range(grid.cols):
        place = grid.place(step)
        outs[step][:, :own] = tokens[:, pl.ds(block_start(place, own), own)]
        outs[step][:, own : 2 * own] = cot[:, pl.ds(block_start(place, own), own)]
        outs[step][:, 2 * own :] = blocks[place // grid.rows]


def unbundle(grid, *rest):
    bundles, (grad_out, result_out, small_out) = rest[: grid.cols], rest[grid.cols :]
    size = grad_out.shape[0]
    own = grad_out.shape[1] // grid.cols
    small_out[...] = jnp.zeros_like(small_out)
    for step in range(grid.cols):
        place = grid.place(step)
        span = pl.ds(block_start(place, own), own)
        grad_out[:, span] = bundles[step][:size, :own]
        result_out[:, span] = bundles[step][:size, own : 2 * own]
        terms = bundles[step][:, 2 * own :].astype(FULL)
        small_out[place // grid.rows] += (terms[:, :LANES] + terms[:, LANES:]).T


def pack(qkv, proj, attn_out):
    width = qkv.shape[2]
    for i in range(3):
        attn_out[:, i * width : (i + 1) * width] = qkv[i]
    attn_out[:, 3 * width :] = proj[...].T


def places(grid, slot_count, segs, segs_row, segs_col, segs_own, cosine, sine):
    own = segs_own.shape[1]
    base = grid.sequence() * grid.rows
    lane = lax.broadcasted_iota(jnp.int32, (1, own), 1)

    def segs_of(q):
        return segs[pl.ds(base + q, 1), :]

    starts = []
    for slot in range(slot_count):
        start = jnp.full((1, 1), SEQ, jnp.int32)
        for q in range(grid.rows):
            there = jnp.where(segs_of(q) == slot, lane + q * own, SEQ)
            start = jnp.minimum(start, jnp.min(there, axis=1, keepdims=True))
        starts.append(start)
    half = cosine.shape[0]
    step = lax.broadcasted_iota(jnp.int32, (half, own), 0).astype(FULL)
    inverse_freq = 1.0 / jnp.exp(step * (2.0 / HEAD_DIM) * jnp.log(FULL(10000.0)))
    for e in range(grid.rows):
        q = grid.row() ^ e
        span = slice(e * own, (e + 1) * own)
        row = segs_of(q)
        position = lane + q * own
        for slot in range(slot_count):
            position = position - jnp.where(row == slot, starts[slot], 0)
        angle = position.astype(FULL) * inverse_freq
        cosine[:, span] = jnp.cos(angle)
        sine[:, span] = jnp.sin(angle)
        segs_row[:, span] = row
        segs_col[span, :] = jnp.broadcast_to(row.astype(FULL), (8, own)).T[:, :1].astype(jnp.int32)
    segs_own[...] = segs_row[:, :own]


def first_norm(grid, segs, *rest):
    bundles, (input_out, stream_out, cot_out, mods_out) = rest[: grid.cols], rest[grid.cols :]
    size, own = bundles[0].shape[0], input_out.shape[1]
    for step in range(grid.cols):
        place = pl.ds(block_start(grid.source(step), size), size)
        stream_out[place, :] = bundles[step][:, :own]
        cot_out[place, :] = bundles[step][:, own : 2 * own]
        terms = bundles[step][:, 2 * own :].astype(FULL)
        mods_out[place, :] = terms[:, :LANES] + terms[:, LANES:]
    stream = stream_out[...].astype(FULL)
    mods = mods_out[...]
    pick = token_mods_of(mods, segs[...])
    normed, _ = normalize(stream)
    scaled = normed * mods[:, GAIN_ONE : GAIN_ONE + 1]
    input_out[...] = (scaled * (1.0 + pick(1)) + pick(0)).astype(LOW)


def branch_grad(segs, mods, cot, branch_out):
    pick = token_mods_of(mods[...], segs[...])
    branch_out[...] = (cot[...].astype(FULL) * pick(5)).astype(LOW)


def attend(segs_row, segs_col, cosine, sine, weight_all, *rest):
    pieces, outs = rest[:4], rest[4:]
    parts, (query, key, value, mixed, logsum, inputs_all, key_rows) = outs[:3], outs[3:]
    own = pieces[0].shape[1]
    head_width = query.shape[0]
    weight, proj = weight_all[:, : 3 * head_width], weight_all[:, 3 * head_width :]
    half = HEAD_DIM // 2
    scale = HEAD_DIM ** (-0.5)
    for e in range(4):
        span = slice(e * own, (e + 1) * own)
        cos, sin = cosine[:, span], sine[:, span]
        inputs_all[:, span] = pieces[e][...]
        found = dot(weight, inputs_all[:, span], (0, 0))
        for h in range(head_width // HEAD_DIM):
            for out, base, factor in ((query, 0, scale), (key, head_width, 1.0)):
                at = h * HEAD_DIM
                one = found[base + at : base + at + half]
                two = found[base + at + half : base + at + HEAD_DIM]
                out[at : at + half, span] = ((one * cos - two * sin) * factor).astype(LOW)
                out[at + half : at + HEAD_DIM, span] = ((two * cos + one * sin) * factor).astype(LOW)
        value[:, span] = found[2 * head_width :].astype(LOW)
    ship(query, key, value, inputs_all)
    key_segs = jnp.where(segs_col[...] == 0, -1, segs_col[...])
    for h in range(head_width // HEAD_DIM):
        rows = slice(h * HEAD_DIM, (h + 1) * HEAD_DIM)
        key_rows[h] = key[rows, :].astype(FULL).T.astype(LOW)
    for e in (3, 1, 2, 0):
        span = slice(e * own, (e + 1) * own)
        query_segs = segs_row[:, span]
        allowed = key_segs == query_segs
        padding = (query_segs == 0).astype(FULL)
        for h in range(head_width // HEAD_DIM):
            rows = slice(h * HEAD_DIM, (h + 1) * HEAD_DIM)
            scores = dot(key_rows[h], query[rows, span], (1, 0))
            scores = jnp.where(allowed, scores, MASK_FILL)
            largest = jnp.maximum(jnp.max(scores, axis=0, keepdims=True), MASK_FLOOR)
            exponent = jnp.exp(scores - largest)
            total = jnp.sum(exponent, axis=0, keepdims=True) + padding
            found = dot(value[rows, :], exponent.astype(LOW), (1, 0))
            mixed[rows, span] = (found / total).astype(LOW)
            logsum[h : h + 1, span] = largest + jnp.log(total)
        part_of(parts, e)[...] = dot(proj, mixed[:, span], (1, 0)).astype(LOW)
        ship_part(parts, e)


def second_norm(segs, mods, stream, part, near, far, input_out, middle_out, attn_out):
    pick = token_mods_of(mods[...], segs[...])
    attn = three_terms(part, near, far)
    attn_out[...] = attn.astype(LOW)
    middle = stream[...].astype(FULL) + pick(2) * attn
    middle_out[...] = middle
    normed, _ = normalize(middle)
    scaled = normed * mods[:, GAIN_TWO : GAIN_TWO + 1]
    input_out[...] = (scaled * (1.0 + pick(4)) + pick(3)).astype(LOW)


GELU_SCALE = 0.7978845608028654
GELU_CUBE = 0.044715


def feed_first(weights, up_bias, *rest):
    pieces, branches, outs = rest[:4], rest[4:8], rest[8:]
    parts, (hidden, pre_grad, inputs_all, branch_all) = outs[:3], outs[3:]
    own = pieces[0].shape[1]
    count = hidden.shape[0]
    up, down = weights[:, :count], weights[:, count:]
    bias = jnp.broadcast_to(up_bias[...].astype(FULL)[None], (8, count)).T[:, :1]
    for e in (3, 1, 2, 0):
        span = slice(e * own, (e + 1) * own)
        inputs_all[:, span] = pieces[e][...]
        branch_all[:, span] = branches[e][...]
        pre = dot(up, pieces[e][...], (0, 0)) + bias
        square = pre * pre
        curve = jnp.tanh(GELU_SCALE * (pre + GELU_CUBE * square * pre))
        hidden[:, span] = (0.5 * pre * (1.0 + curve)).astype(LOW)
        slope = 0.5 * (1.0 + curve) + 0.5 * pre * (1.0 - curve * curve) * (
            GELU_SCALE * (1.0 + 3.0 * GELU_CUBE * square)
        )
        grad = dot(down, branches[e][...], (0, 0))
        pre_grad[:, span] = (grad * slope).astype(LOW)
        part_of(parts, e)[...] = dot(up, pre_grad[:, span], (1, 0)).astype(LOW)
        ship_part(parts, e)


def feed_grads_of(hidden, pre_grad, inputs_all, branch_all, grads):
    count = hidden.shape[0]
    blocks = grads.shape[0]
    size = inputs_all.shape[0] // blocks
    ones = jnp.ones((16, hidden.shape[1]), LOW)
    bias = dot(ones, pre_grad[...], (1, 1)).astype(LOW)
    for j in range(blocks):
        grads[j, size:, :count] = bias
        grads[j, size:, count:] = jnp.zeros_like(bias)
    up_total = dot(inputs_all[...], pre_grad[...], (1, 1)).astype(LOW)
    for j in range(blocks):
        grads[j, :size, :count] = up_total[j * size : (j + 1) * size]
    down_total = dot(branch_all[...], hidden[...], (1, 1)).astype(LOW)
    for j in range(blocks):
        grads[j, :size, count:] = down_total[j * size : (j + 1) * size]


def feed_out(weights, hidden, *parts):
    count = hidden.shape[0]
    own = parts[0].shape[1]
    for e in (3, 1, 2, 0):
        part_of(parts, e)[...] = dot(
            weights[:, count:], hidden[:, e * own : (e + 1) * own], (1, 0)
        ).astype(LOW)
        ship_part(parts, e)


def middle_grad(segs, mods, middle, cot, part, near, far, grad_out, attn_grad_out, input_grad_out):
    pick = token_mods_of(mods[...], segs[...])
    input_grad = three_terms(part, near, far)
    input_grad_out[...] = input_grad.astype(LOW)
    normed, inverse = normalize(middle[...])
    grad_scaled = input_grad * (1.0 + pick(4)) * mods[:, GAIN_TWO : GAIN_TWO + 1]
    grad = cot[...].astype(FULL) + normalize_back(grad_scaled, normed, inverse)
    grad_out[...] = grad
    attn_grad_out[...] = (grad * pick(2)).astype(LOW)


def doc_sums(values, chosen):
    terms = jnp.concatenate(split(values, 2), 1).astype(LOW)
    return dot(jnp.concatenate([chosen, chosen], 1), terms, (1, 1))


def slot_rows(segs):
    return (lax.broadcasted_iota(jnp.int32, (16, segs.shape[1]), 0) == segs).astype(LOW)


def finish_forward(segs, mods, middle, cot, attn, grad_middle, input_grad, part, near, far, result_out, small):
    pick = token_mods_of(mods[...], segs[...])
    chosen = slot_rows(segs[...])
    ones = jnp.ones(chosen.shape, LOW)
    valid = (segs[...] != 0).astype(FULL)
    mlp = (
        three_terms(part, near, far)
        + mods[:, DOWN_BIAS : DOWN_BIAS + 1]
    )
    gate = pick(5)
    mlp_term = gate * mlp
    result = middle[...] + mlp_term
    result_out[...] = result.astype(LOW)
    small[...] = jnp.zeros_like(small)
    cot_full = cot[...].astype(FULL)
    attn_all = attn[...].astype(FULL)
    input_all = input_grad[...].astype(FULL)
    normed, _ = normalize(middle[...])
    along = input_all * normed
    terms = (
        (2, grad_middle[...] * attn_all),
        (3, input_all),
        (4, along * mods[:, GAIN_TWO : GAIN_TWO + 1]),
        (5, cot_full * mlp),
    )
    for k, values in terms:
        small[k * SLOTS : (k + 1) * SLOTS, :] = doc_sums(values, chosen)[:SLOTS]
    small[GAIN_TWO : GAIN_TWO + 1, :] = doc_sums(along * (1.0 + pick(4)), ones)[:1]
    branch = (cot_full * gate).astype(LOW)
    small[DOWN_BIAS : DOWN_BIAS + 1, :] = dot(ones, branch, (1, 1))[:1]
    attn_term = pick(2) * attn_all
    squares = [
        jnp.sum(jnp.sum(v * v, axis=0, keepdims=True) * valid, axis=1, keepdims=True)
        for v in (result, attn_term, mlp_term)
    ]
    squares.append(jnp.sum(valid, axis=1, keepdims=True) * middle.shape[0])
    lane = lax.broadcasted_iota(jnp.int32, (1, small.shape[1]), 1)
    total = jnp.zeros(lane.shape, FULL)
    for i, value in enumerate(squares):
        total = jnp.where(lane == i, value, total)
    small[STATS : STATS + 1, :] = total


def attend_back(segs_row, segs_col, cosine, sine, weight_all, query, key, value, mixed, logsum, *rest):
    pieces, outs = rest[:4], rest[4:]
    parts, (grads, pieces_all, key_rows, value_rows, out_grad, key_grad, value_grad) = outs[:3], outs[3:]
    own = pieces[0].shape[1]
    head_width = query.shape[0]
    heads = head_width // HEAD_DIM
    weight, proj = weight_all[:, : 3 * head_width], weight_all[:, 3 * head_width :]
    half = HEAD_DIM // 2
    scale = HEAD_DIM ** (-0.5)
    for h in range(heads):
        rows = slice(h * HEAD_DIM, (h + 1) * HEAD_DIM)
        key_rows[h] = key[rows, :].astype(FULL).T.astype(LOW)
        value_rows[h] = value[rows, :].astype(FULL).T.astype(LOW)
    key_segs = jnp.where(segs_col[...] == 0, -1, segs_col[...])
    key_grad[...] = jnp.zeros_like(key_grad)
    value_grad[...] = jnp.zeros_like(value_grad)

    def turn_back(grad, span, base, at):
        cos, sin = cosine[:, span], sine[:, span]
        one, two = grad[:half], grad[half:]
        grads[base + at : base + at + half, span] = (one * cos + two * sin).astype(LOW)
        grads[base + at + half : base + at + HEAD_DIM, span] = (two * cos - one * sin).astype(LOW)

    for e in range(4):
        span = slice(e * own, (e + 1) * own)
        allowed = key_segs == segs_row[:, span]
        pieces_all[:, span] = pieces[e][...]
        out_grad[...] = dot(proj, pieces[e][...], (0, 0)).astype(LOW)
        for h in range(heads):
            rows = slice(h * HEAD_DIM, (h + 1) * HEAD_DIM)
            back = out_grad[rows, :]
            inner = jnp.sum(
                back.astype(FULL) * mixed[rows, span].astype(FULL), axis=0, keepdims=True
            )
            scores = dot(key_rows[h], query[rows, span], (1, 0))
            scores = jnp.where(allowed, scores, MASK_FILL)
            probability = jnp.exp(scores - logsum[h : h + 1, span])
            grad_probs = dot(value_rows[h], back, (1, 0))
            score_grad = (probability * (grad_probs - inner)).astype(LOW)
            value_grad[rows, :] += dot(back, probability.astype(LOW), (1, 1))
            key_grad[rows, :] += dot(query[rows, span], score_grad, (1, 1))
            turn_back(dot(key[rows, :], score_grad, (1, 0)) * scale, span, 0, h * HEAD_DIM)
    ship(pieces_all)
    for e in (3, 1, 2, 0):
        span = slice(e * own, (e + 1) * own)
        for h in range(heads):
            turn_back(key_grad[h * HEAD_DIM : (h + 1) * HEAD_DIM, span], span, head_width, h * HEAD_DIM)
        grads[2 * head_width :, span] = value_grad[:, span].astype(LOW)
        part_of(parts, e)[...] = dot(weight, grads[:, span], (1, 0)).astype(LOW)
        ship_part(parts, e)


def attend_weights(grid, grads, mixed, inputs_all, pieces_all, *rest):
    blocks, total = rest[: grid.cols], rest[grid.cols]
    count = grads.shape[0]
    total[:, :count] = dot(inputs_all[...], grads[...], (1, 1)).astype(LOW)
    total[:, count:] = dot(pieces_all[...], mixed[...], (1, 1)).astype(LOW)
    size = blocks[0].shape[0]
    for j in range(grid.cols):
        blocks[j][...] = total[pl.ds(block_start(grid.col() ^ j, size), size), :]


def block_sum(*rest):
    total = rest[0][...].astype(FULL)
    for piece in rest[1:-1]:
        total = total + piece[...].astype(FULL)
    rest[-1][...] = total.astype(LOW)


def attn_weight_out(*rest):
    parts, (qkv_out, proj_out) = rest[:-2], rest[-2:]
    total = parts[0][...].astype(FULL)
    for part in parts[1:]:
        total = total + part[...].astype(FULL)
    width = qkv_out.shape[2]
    for i in range(3):
        qkv_out[i] = total[:, i * width : (i + 1) * width]
    proj_out[...] = total[:, 3 * width :].T


def feed_weight_out(*rest):
    parts, (up_out, bias_out, down_out) = rest[:-3], rest[-3:]
    total = parts[0][...].astype(FULL)
    for part in parts[1:]:
        total = total + part[...].astype(FULL)
    size, count = up_out.shape
    up_out[...] = total[:size, :count]
    down_out[...] = total[:size, count:]
    bias_out[...] = total[size, :count]


def finish_backward(grid, segs, mods, stream, grad_middle, result, small_in, part, near, far, *rest):
    outs, (grad_low, blocks) = rest[: grid.cols], rest[grid.cols :]
    pick = token_mods_of(mods[...], segs[...])
    chosen = slot_rows(segs[...])
    ones = jnp.ones(chosen.shape, LOW)
    input_grad = three_terms(part, near, far)
    normed, inverse = normalize(stream[...].astype(FULL))
    gain = mods[:, GAIN_ONE : GAIN_ONE + 1]
    grown = input_grad * (1.0 + pick(1))
    grad = grad_middle[...] + normalize_back(grown * gain, normed, inverse)
    grad_low[...] = grad.astype(LOW)
    size = grad.shape[0] // grid.cols
    own = grad.shape[1]
    for step in range(grid.cols):
        place = pl.ds(block_start(grid.source(step), size), size)
        outs[step][:size, :own] = grad_low[place, :]
        outs[step][:size, own : 2 * own] = result[place, :]
    shift = doc_sums(input_grad, chosen)[:SLOTS]
    scale = doc_sums(input_grad * normed * gain, chosen)[:SLOTS]
    norm_gain = doc_sums(grown * normed, ones)[:1]
    for c in range(grid.cols):
        span = slice(c * size, (c + 1) * size)
        blocks[c, :, :size] = small_in[:, span]
        blocks[c, :SLOTS, :size] = shift[:, span]
        blocks[c, SLOTS : 2 * SLOTS, :size] = scale[:, span]
        blocks[c, GAIN_ONE : GAIN_ONE + 1, :size] = norm_gain[:, span]
        blocks[c, STATS : STATS + 1, :size] = small_in[STATS : STATS + 1, :size]
    for step in range(grid.cols):
        terms = split(blocks[grid.source(step)].T, 2)
        outs[step][:, 2 * own :] = jnp.concatenate(terms, 1).astype(LOW)


def modulation_back(grid, slot_count, dp_count, *rest):
    times, (table, weight), rest = rest[:dp_count], rest[dp_count : dp_count + 2], rest[dp_count + 2 :]
    pieces, outs = rest[: 2 * dp_count], rest[2 * dp_count :]
    weight_out, bias_out, gain_one_out, gain_two_out, down_bias_out, stats_out, embed_out = outs[:7]
    embed, grads = outs[7:]
    per = grid.per_row
    embed[...] = jnp.zeros_like(embed)
    size = grads.shape[2]
    total = jnp.zeros((LANES - 6 * SLOTS, size), FULL)
    for d in range(dp_count):
        for far in range(2):
            piece = pieces[2 * d + far]
            for s in range(2 * per):
                sequence = (grid.row() ^ (2 * far + s // per)) * per + s % per
                first = block_start(d * per * grid.rows + sequence, SLOTS)
                for slot in range(slot_count):
                    time = times[d][sequence, slot]
                    embed[pl.ds(first + slot, 1), :] = table[pl.ds(time, 1), :]
                for k in range(6):
                    grads[k, pl.ds(first, SLOTS), :] = piece[s, k * SLOTS : (k + 1) * SLOTS, :]
                total = total + piece[s, 6 * SLOTS :, :]
    for k in range(6):
        rows = grads[k]
        weight_out[k] = dot(rows, embed[...], (0, 0), PRECISE)
        bias_out[k : k + 1, :] = jnp.sum(rows, axis=0, keepdims=True)
        part = dot(rows, weight[k].astype(FULL), (1, 0), PRECISE)
        embed_out[...] = part if k == 0 else embed_out[...] + part
    gain_one_out[...] = total[GAIN_ONE - 6 * SLOTS]
    gain_two_out[...] = total[GAIN_TWO - 6 * SLOTS]
    down_bias_out[...] = total[DOWN_BIAS - 6 * SLOTS]
    squares = total[STATS - 6 * SLOTS : STATS - 6 * SLOTS + 1, :]
    stats_out[...] = jnp.sqrt(squares / squares[:, 3:4])[0, :3]


def table_sum(grid, slot_count, dp_count, *rest):
    times, parts, (table_out, total) = rest[:dp_count], rest[dp_count:-2], rest[-2:]
    found = parts[0][...]
    for part in parts[1:]:
        found = found + part[...]
    total[...] = found
    table_out[...] = jnp.zeros_like(table_out)
    for d in range(dp_count):
        for sequence in range(grid.cols):
            for slot in range(slot_count):
                time = times[d][sequence, slot]
                at = (d * grid.cols + sequence) * SLOTS + slot
                table_out[pl.ds(time, 1), :] += total[at : at + 1, :]


def per_device(
    tokens,
    cotangent,
    segment_ids,
    doc_times,
    time_table,
    attn_gain,
    mlp_gain,
    mod_weight,
    mod_bias,
    qkv_weight,
    proj_weight,
    up_weight,
    up_bias,
    down_weight,
    down_bias,
):
    grid = Grid()
    dp_count = lax.axis_size("dp")
    width_local = tokens.shape[0]
    width = width_local * grid.cols
    own = tokens.shape[1] // grid.cols
    head_width = qkv_weight.shape[2]
    hidden_local = up_weight.shape[1]
    slot_count = doc_times.shape[1]
    cond_width = mod_weight.shape[2]
    if segment_ids.shape[0] != grid.cols * SEQ or own * grid.rows != SEQ or grid.rows != 4:
        raise ValueError("sequence split")
    low_tile = shape((width, own), LOW)
    full_tile = shape((width, own), FULL)
    low_piece = shape((width_local, own), LOW)
    part_tiles = [low_tile, low_tile, shape((2 * width, own), LOW)]

    part_rows = width_local // dp_count
    part_start = lax.axis_index("dp") * part_rows

    def gather_weight(parts):
        parts = [lax.dynamic_slice_in_dim(p, part_start, part_rows, 0) for p in parts]
        part = jnp.concatenate(parts, 1) if len(parts) > 1 else parts[0]
        return lax.all_gather(part, ("col", "dp"), axis=0, tiled=True)

    attn_block = run(
        pack, "pack", [shape((width_local, 4 * head_width), LOW)],
        [qkv_weight.transpose(1, 0, 2), proj_weight],
    )
    attn_weights = gather_weight(attn_block)

    bundles = run(
        functools.partial(prepare, grid, slot_count), "prepare",
        [shape((width_local, 2 * own + 2 * LANES), LOW)] * grid.cols,
        [doc_times, time_table, mod_weight, mod_bias, attn_gain, mlp_gain,
         down_bias, tokens, cotangent],
        [pltpu.VMEM((SLOTS, cond_width), FULL), pltpu.VMEM((LANES, width_local), FULL),
         pltpu.VMEM((grid.per_row, width_local, 2 * LANES), LOW)],
        smem=1,
    )
    bundles = relayout(bundles)
    segs_row, segs_col, segs_own, cosine, sine = run(
        functools.partial(places, grid, slot_count), "places",
        [shape((1, SEQ), jnp.int32), shape((SEQ, 1), jnp.int32), shape((1, own), jnp.int32)]
        + [shape((HEAD_DIM // 2, SEQ), FULL)] * 2,
        [segment_ids.reshape(-1, own)],
    )
    input_one, stream, cot, mods = run(
        functools.partial(first_norm, grid), "first_norm",
        [low_tile] + far_all([low_tile] * 2) + [shape((width, LANES), FULL)], [segs_own] + bundles,
    )

    def branch_filler(ready):
        [late] = after([ready], [cot])
        return run(branch_grad, "branch_grad", [low_tile], [segs_own, mods, Far(late)])

    rows_one, [branch] = gather_rows(input_one, branch_filler)
    branch_rows = gather_rows(branch)
    times = [doc_times] + [swap(doc_times, "dp", d) for d in range(1, dp_count)]
    rows_one[3:] = after([branch_rows[1]] + times[1:], rows_one[3:])

    feed_weights = gather_weight(after(rows_one[2:3] + [attn_weights], [up_weight, down_weight]))
    *parts, query, key, value, mixed, logsum, inputs_one = run(
        attend, "attend",
        far_all(part_tiles + [shape((head_width, SEQ), LOW)] * 4) + [shape((8, SEQ), FULL)]
        + [Far(shape((width, SEQ), LOW))],
        [segs_row] + far_all([segs_col, cosine, sine, attn_weights] + rows_one),
        [pltpu.VMEM((head_width // HEAD_DIM, SEQ, HEAD_DIM), LOW)],
    )
    attn_terms = scatter_rows(parts)
    input_two, middle, attn = run(
        second_norm, "second_norm", [low_tile] + far_all([full_tile, low_tile]),
        [segs_own, mods, Far(stream), Far(attn_terms[0])] + attn_terms[1:],
    )
    rows_two = gather_rows(input_two)
    hidden_tile = shape((hidden_local, SEQ), LOW)
    *parts, hidden, pre_grad, inputs_two, branch_all = run(
        feed_first, "feed_first",
        far_all(part_tiles + [hidden_tile] * 2 + [shape((width, SEQ), LOW)] * 2),
        [Far(feed_weights), up_bias] + far_all(rows_two + branch_rows),
    )
    def grads_filler(ready):
        [late] = after([ready], [hidden])
        return run(
            feed_grads_of, "feed_grads",
            [Far(shape((grid.cols, width_local + 16, 2 * hidden_local), LOW))],
            far_all([late, pre_grad, inputs_two, branch_all]),
        )

    input_terms, [feed_grads] = scatter_rows(parts, grads_filler, True)
    feed_grads = lax.psum_scatter(
        feed_grads.reshape(-1, 2 * hidden_local), "col", scatter_dimension=0, tiled=True
    )
    grad_middle, grad_attn, input_grad = run(
        middle_grad, "middle_grad", [Far(full_tile), low_tile, Far(low_tile)],
        [segs_own, mods, Far(middle), Far(cot), Far(input_terms[0])] + input_terms[1:],
    )

    def feed_filler(ready):
        [late] = after([ready], [hidden])
        return run(feed_out, "feed_out", far_all(part_tiles), far_all([feed_weights, late]))

    attn_rows, parts = gather_rows(grad_attn, feed_filler)
    mlp_terms = scatter_rows(parts)
    *parts, qkv_grads, attn_all = run(
        attend_back, "attend_back",
        far_all(part_tiles + [shape((3 * head_width, SEQ), LOW), shape((width, SEQ), LOW)]),
        [segs_row] + far_all([segs_col, cosine, sine, attn_weights, query, key, value, mixed])
        + [logsum] + far_all(attn_rows),
        [pltpu.VMEM((head_width // HEAD_DIM, SEQ, HEAD_DIM), LOW)] * 2
        + [pltpu.VMEM((head_width, own), LOW)] + [pltpu.VMEM((head_width, SEQ), FULL)] * 2,
    )

    def back_filler(ready):
        [late] = after([ready], [qkv_grads])
        blocks = run(
            functools.partial(attend_weights, grid), "attend_weights",
            far_all([shape((width_local, 4 * head_width), LOW)] * grid.cols),
            far_all([late, mixed, inputs_one, attn_all]), [pltpu.VMEM((width, 4 * head_width), LOW)],
        )
        [first] = after(blocks[:1], mlp_terms[:1])
        found = run(
            finish_forward, "finish_forward", [low_tile, shape((LANES, width), FULL)],
            [segs_own, mods] + far_all([middle, cot, attn, grad_middle, input_grad, first])
            + mlp_terms[1:],
        )
        return found + blocks

    back_terms, (result, small, *attn_grads) = scatter_rows(parts, back_filler)
    wide = width_local
    bundles = run(
        functools.partial(finish_backward, grid), "finish_backward",
        [shape((wide, 2 * own + 2 * LANES), LOW)] * grid.cols,
        [segs_own, mods, Far(stream), Far(grad_middle), result, small, Far(back_terms[0])]
        + back_terms[1:],
        [pltpu.VMEM((width, own), LOW), pltpu.VMEM((grid.cols, LANES, wide), FULL)],
    )
    out_tile = shape((width_local, grid.cols * own), LOW)
    tokens_grad, block_output, small = run(
        functools.partial(unbundle, grid), "unbundle",
        [out_tile, out_tile, shape((grid.per_row, LANES, wide), FULL)], relayout(bundles, back=True),
    )

    small = jnp.concatenate([small, swap(small, "row", 1)], 0)
    pieces = []
    for d in range(dp_count):
        for far in range(2):
            count = dp_count * grid.rows
            pairs = [(i, i ^ (d * grid.rows + 2 * far)) for i in range(count)]
            pieces.append(lax.ppermute(small, ("dp", "row"), pairs) if d or far else small)
    seq_total = grid.cols * dp_count
    vector = shape((width_local,), FULL)
    embed_tile = shape((seq_total * SLOTS, cond_width), FULL)
    weight_out, bias_out, gain_one_out, gain_two_out, down_bias_out, stats, embed = run(
        functools.partial(modulation_back, grid, slot_count, dp_count), "modulation_back",
        [
            shape((6, width_local, cond_width), FULL), shape((6, width_local), FULL),
            vector, vector, vector, shape((3,), FULL), embed_tile,
        ],
        times + [time_table, mod_weight] + pieces,
        [pltpu.VMEM((seq_total * SLOTS, cond_width), FULL),
         pltpu.VMEM((6, seq_total * SLOTS, width_local), FULL)],
        smem=dp_count,
    )
    [table_out] = run(
        functools.partial(table_sum, grid, slot_count, dp_count), "table_sum",
        [shape(time_table.shape, FULL)],
        times + [embed] + [swap(embed, "col", j) for j in range(1, grid.cols)],
        [pltpu.VMEM((seq_total * SLOTS, cond_width), FULL)], smem=dp_count,
    )

    def all_dp(part):
        return [part] + [swap(part, "dp", d) for d in range(1, dp_count)]

    attn_grads = attn_grads[:1] + [swap(attn_grads[j], "col", j) for j in range(1, grid.cols)]
    [attn_sum] = run(
        block_sum, "block_sum", [shape((width_local, 4 * head_width), LOW)], attn_grads
    )
    up_out, up_bias_out, down_out = run(
        feed_weight_out, "feed_weight_out",
        [shape(up_weight.shape, FULL), shape(up_bias.shape, FULL), shape(down_weight.shape, FULL)],
        all_dp(feed_grads),
    )
    qkv_out, proj_out = run(
        attn_weight_out, "attn_weight_out",
        [shape((3, width_local, head_width), FULL), shape(proj_weight.shape, FULL)],
        all_dp(attn_sum),
    )
    return (
        block_output,
        tokens_grad,
        table_out,
        gain_one_out,
        gain_two_out,
        weight_out,
        bias_out,
        qkv_out.transpose(1, 0, 2),
        proj_out,
        up_out,
        up_bias_out,
        down_out,
        down_bias_out,
        stats,
    )


def solution(mesh):
    return jax.shard_map(
        per_device,
        mesh=mesh,
        in_specs=(
            P("col", ("dp", "row")),
            P("col", ("dp", "row")),
            P("dp"),
            P("dp", None),
            P(),
            P("col"),
            P("col"),
            P(None, "col", None),
            P(None, "col"),
            P("col", None, "row"),
            P("row", "col"),
            P("col", "row"),
            P("row"),
            P("col", "row"),
            P("col"),
        ),
        out_specs=(
            P("col", ("dp", "row")),
            P("col", ("dp", "row")),
            P(),
            P("col"),
            P("col"),
            P(None, "col", None),
            P(None, "col"),
            P("col", None, "row"),
            P("row", "col"),
            P("col", "row"),
            P("row"),
            P("col", "row"),
            P("col"),
            P(),
        ),
        check_vma=False,
    )
```

```python
import functools

import jax
import jax.numpy as jnp
from jax import lax
from jax.experimental import pallas as pl
from jax.experimental.pallas import tpu as pltpu
from jax.sharding import PartitionSpec as P

HEAD_DIM = 64
SEQ = 1024

PRECISE = lax.Precision.HIGHEST
EPSILON = 1e-05
MASK_FILL = -1e30
MASK_FLOOR = -1e29
LOW = jnp.bfloat16
FULL = jnp.float32
SLOTS = 8
LANES = 64
GAIN_ONE, GAIN_TWO, DOWN_BIAS = 48, 49, 50
STATS = 51
VMEM_LIMIT = 56 * 1024 * 1024
NEAR = {'unbundle': 12, 'modulation_back': 12, 'table_sum': 12, 'attn_weight_out': 12, 'feed_weight_out': 12, 'pair_sum': 12, 'block_sum': 12, 'join': 12, 'finish_forward': 12, 'finish_backward': 12, 'feed_first': 56, 'attend_back_first': 56, 'attend_back_last': 56, 'second_norm': 56, 'middle_grad': 56, 'branch_grad': 56, 'first_norm': 56, 'attend': 40}


def swap(values, axis, bit):
    count = lax.axis_size(axis)
    return lax.ppermute(values, axis, [(i, i ^ bit) for i in range(count)])


def gather_rows(values, filler=None, deps=()):
    far = swap(values, "row", 2)
    near = swap(values, "row", 1)
    filled = None
    if filler is not None:
        filled = filler(near)
        deps = list(deps) + list(filled[:1])
    if deps:
        [far] = after(deps, [far])
    last = swap(far, "row", 1)
    pieces = [values, near, far, last]
    return pieces if filler is None else (pieces, after([last], filled))


def scatter_rows(parts, filler=None, hold=False):
    width = parts[0].shape[0]
    near = swap(parts[2], "row", 1)
    total = (parts[1].astype(FULL) + near[width:].astype(FULL)).astype(LOW)
    far = swap(total, "row", 2)
    if filler is None:
        return [parts[0], near, far]
    filled = filler(total)
    [far] = after(filled[:1], [far])
    return [parts[0], near, far], after([far], filled) if hold else filled


def scatter_near(parts):
    near = swap(parts[2], "row", 1)
    total = (parts[1].astype(FULL) + near[parts[0].shape[0] :].astype(FULL)).astype(LOW)
    return near, total


def col_of_row(row_count):
    if row_count == 4:
        return [0, 2, 1, 3]
    return list(range(row_count))


def relayout_pairs(step):
    row_count = lax.axis_size("row")
    col_count = lax.axis_size("col")
    per_row = col_count // row_count
    table = col_of_row(row_count)
    pairs = []
    for r in range(row_count):
        for c in range(col_count):
            j, q = divmod((c + step) % col_count, row_count)
            pairs.append((r * col_count + c, q * col_count + table[r] * per_row + j))
    return pairs


def relayout(pieces, back=False):
    got = []
    for step, piece in enumerate(pieces):
        pairs = relayout_pairs(step)
        if back:
            pairs = [(b, a) for a, b in pairs]
        got.append(lax.ppermute(piece, ("row", "col"), pairs))
    return got


def after(deps, values):
    return lax.optimization_barrier((list(values), list(deps)))[0]


class Grid:
    def __init__(self):
        self.rows = lax.axis_size("row")
        self.cols = lax.axis_size("col")
        self.per_row = self.cols // self.rows
        table = col_of_row(self.rows)
        self.seq_of_col = [0] * self.cols
        for r in range(self.rows):
            for j in range(self.per_row):
                self.seq_of_col[table[r] * self.per_row + j] = r * self.per_row + j

    def row(self):
        return lax.axis_index("row")

    def col(self):
        return lax.axis_index("col")

    def sequence(self):
        return sum(jnp.where(self.col() == c, s, 0) for c, s in enumerate(self.seq_of_col))

    def half(self):
        return lax.axis_index("dp") % 2

    def half_start(self, block, which, size):
        return pl.multiple_of((2 * block + which) * size, size)

    def source(self, step):
        mine = self.col() % self.per_row * self.rows + self.row()
        return (mine + self.cols - step) % self.cols

    def place(self, step):
        return (self.col() + step) % self.cols


def whole(memory_space=pltpu.VMEM):
    return pl.BlockSpec(memory_space=memory_space)


class Joined:
    def __init__(self, values):
        self.values = values


class FarIn:
    def __init__(self, sources, buffer, sems):
        self.buffer, self.waiting = buffer, True
        if len(sources) == 1:
            places = [buffer]
        else:
            count = sources[0].shape[1]
            places = [buffer.at[:, i * count : (i + 1) * count] for i in range(len(sources))]
        self.copies = [
            pltpu.make_async_copy(source, place, sem)
            for source, place, sem in zip(sources, places, sems)
        ]
        for copy in self.copies:
            copy.start()

    @property
    def shape(self):
        return self.buffer.shape

    @property
    def ref(self):
        if self.waiting:
            for copy in self.copies:
                copy.wait()
            self.waiting = False
        return self.buffer

    @property
    def at(self):
        return self.ref.at

    def __getitem__(self, index):
        return self.ref[index]


class FarOut:
    def __init__(self, buffer, target, sem):
        self.copy = pltpu.make_async_copy(buffer, target, sem)
        self.ref, self.shipped = buffer, False

    @property
    def shape(self):
        return self.ref.shape

    @property
    def at(self):
        return self.ref.at

    def __getitem__(self, index):
        return self.ref[index]

    def __setitem__(self, index, value):
        self.ref[index] = value

    def ship(self):
        if not self.shipped:
            self.copy.start()
            self.shipped = True


def ship(*refs):
    for ref in refs:
        if isinstance(ref, FarOut):
            ref.ship()


def run(body, name, outs, args, scratch=(), smem=0, flops=0):
    if name in NEAR:
        moved = sum(a.size * a.dtype.itemsize for a in list(args) + list(outs))
        found = pl.pallas_call(
            body,
            out_shape=list(outs),
            in_specs=[whole(pltpu.SMEM)] * smem + [whole() for _ in args[smem:]],
            out_specs=[whole() for _ in outs],
            scratch_shapes=list(scratch),
            compiler_params=pltpu.CompilerParams(vmem_limit_bytes=NEAR[name] * 1024 * 1024),
            cost_estimate=pl.CostEstimate(flops=flops, bytes_accessed=moved, transcendentals=0),
            name=name,
        )(*args)
        return list(found)
    groups = [a.values if isinstance(a, Joined) else [a] for a in args[smem:]]
    flat = [a for group in groups for a in group]
    outs = list(outs)
    buffers = [
        pltpu.VMEM((*group[0].shape[:-1], sum(a.shape[-1] for a in group)), group[0].dtype)
        for group in groups
    ] + [pltpu.VMEM(o.shape, o.dtype) for o in outs]
    moved = sum(a.size * a.dtype.itemsize for a in flat + outs)

    def kernel(*refs):
        scalars, rest = list(refs[:smem]), list(refs[smem:])
        sources, rest = rest[: len(flat)], rest[len(flat) :]
        targets, rest = rest[: len(outs)], rest[len(outs) :]
        own, rest = rest[: len(scratch)], rest[len(scratch) :]
        spaces, sems = rest[:-1], rest[-1]
        ins, count = [], 0
        for group, space in zip(groups, spaces):
            span = range(count, count + len(group))
            ins.append(FarIn([sources[i] for i in span], space, [sems.at[i] for i in span]))
            count += len(group)
        results = [
            FarOut(space, target, sems.at[count + i])
            for i, (space, target) in enumerate(zip(spaces[len(groups) :], targets))
        ]
        body(*scalars, *ins, *results, *own)
        ship(*results)
        for ref in ins:
            ref.ref
        for ref in results:
            ref.copy.wait()

    found = pl.pallas_call(
        kernel,
        out_shape=outs,
        in_specs=[whole(pltpu.SMEM)] * smem + [whole(pl.ANY) for _ in flat],
        out_specs=[whole(pl.ANY) for _ in outs],
        scratch_shapes=list(scratch) + buffers
        + [pltpu.SemaphoreType.DMA((len(flat) + len(outs),))],
        compiler_params=pltpu.CompilerParams(vmem_limit_bytes=VMEM_LIMIT),
        cost_estimate=pl.CostEstimate(flops=flops, bytes_accessed=moved, transcendentals=0),
        name=name,
    )(*args[:smem], *flat)
    return list(found)


def shape(dims, dtype):
    return jax.ShapeDtypeStruct(dims, dtype)


def dot(left, right, dims, precision=None):
    return lax.dot_general(
        left, right, (((dims[0],), (dims[1],)), ((), ())),
        preferred_element_type=FULL, precision=precision,
    )


def split(values, terms):
    found = []
    for _ in range(terms):
        term = values.astype(LOW).astype(FULL)
        found.append(term)
        values = values - term
    return found


def block_start(index, size):
    return pl.multiple_of(index * size, size)


def token_mods_of(mods, segs):
    rows = lax.broadcasted_iota(jnp.int32, (2 * LANES, segs.shape[1]), 0) % LANES

    def pick(k):
        chosen = (rows == segs + k * SLOTS).astype(LOW)
        return dot(mods, chosen, (1, 0))

    return pick


def part_of(parts, e):
    if e % 2 == 0:
        return parts[e // 2]
    width = parts[0].shape[0]
    return parts[2].at[(e // 2) * width : (e // 2 + 1) * width]


def ship_part(parts, e):
    if e != 3:
        ship({1: parts[2], 2: parts[1], 0: parts[0]}[e])


def three_terms(part, near, far):
    return (
        part[...].astype(FULL) + near[: part.shape[0], :].astype(FULL) + far[...].astype(FULL)
    )


def column_of(mods, lane):
    return mods[:, lane : lane + 1].astype(FULL) + mods[:, LANES + lane : LANES + lane + 1].astype(FULL)


def normalize(stream):
    count = 1.0 / stream.shape[0]
    center = jnp.sum(stream, axis=0, keepdims=True) * count
    offset = stream - center
    inverse = lax.rsqrt(jnp.sum(offset * offset, axis=0, keepdims=True) * count + EPSILON)
    return offset * inverse, inverse


def normalize_back(grad_normed, normed, inverse):
    count = 1.0 / normed.shape[0]
    center = jnp.sum(grad_normed, axis=0, keepdims=True) * count
    along = jnp.sum(grad_normed * normed, axis=0, keepdims=True) * count
    return inverse * (grad_normed - center - normed * along)


def prepare(grid, slot_count, times, table, weight, bias, gain_one, gain_two, down_bias, tokens, cot, *rest):
    outs, (embed, rows, blocks) = rest[: grid.cols], rest[grid.cols :]
    own = (outs[0].shape[1] - 2 * LANES) // 2
    rows[...] = jnp.zeros(rows.shape, FULL)
    for k in range(6):
        rows[k * SLOTS : (k + 1) * SLOTS, :] = jnp.broadcast_to(
            bias[k : k + 1, :].astype(FULL), (SLOTS, rows.shape[1])
        )
    rows[GAIN_ONE : GAIN_ONE + 1, :] = gain_one[...].astype(FULL)[None]
    rows[GAIN_TWO : GAIN_TWO + 1, :] = gain_two[...].astype(FULL)[None]
    rows[DOWN_BIAS : DOWN_BIAS + 1, :] = down_bias[...].astype(FULL)[None]
    fixed = rows[...].T
    cond = weight.shape[2]
    flat = jnp.concatenate([weight[k] for k in range(6)], 1)
    row = lax.broadcasted_iota(jnp.int32, (LANES, 6 * cond), 0)
    lane = lax.broadcasted_iota(jnp.int32, (LANES, 6 * cond), 1)
    match = row // SLOTS == lane // cond
    for j in range(grid.per_row):
        embed[...] = jnp.zeros(embed.shape, FULL)
        for slot in range(slot_count):
            time = times[grid.row() * grid.per_row + j, slot]
            embed[slot : slot + 1, :] = table[pl.ds(time, 1), :]
        tiled = jnp.concatenate([embed[...]] * (LANES // SLOTS), 0)
        tiled = jnp.concatenate([tiled] * 6, 1)
        total = fixed
        for term in split(jnp.where(match, tiled, 0.0), 3):
            total = total + dot(flat, term.astype(LOW), (1, 1))
        blocks[j] = jnp.concatenate(split(total, 2), 1).astype(LOW)
    for step in range(grid.cols):
        place = grid.place(step)
        outs[step][:, :own] = tokens[:, pl.ds(block_start(place, own), own)]
        outs[step][:, own : 2 * own] = cot[:, pl.ds(block_start(place, own), own)]
        outs[step][:, 2 * own :] = blocks[place // grid.rows]


def unbundle(grid, *rest):
    bundles, (grad_out, small_out) = rest[: grid.cols], rest[grid.cols :]
    own = grad_out.shape[1] // grid.cols
    small_out[...] = jnp.zeros(small_out.shape, FULL)
    for step in range(grid.cols):
        place = grid.place(step)
        grad_out[:, pl.ds(block_start(place, own), own)] = bundles[step][:, :own]
        terms = bundles[step][:, own:].astype(FULL)
        small_out[place // grid.rows] += (terms[:, :LANES] + terms[:, LANES:]).T


def join(grid, *rest):
    pieces, out = rest[: grid.cols], rest[-1]
    own = pieces[0].shape[1]
    for step in range(grid.cols):
        out[:, pl.ds(block_start(grid.place(step), own), own)] = pieces[step][...]


def pack(qkv, proj, attn_out):
    width = qkv.shape[2]
    for i in range(3):
        attn_out[:, i * width : (i + 1) * width] = qkv[i]
    attn_out[:, 3 * width :] = proj[...].T


def places(grid, slot_count, segs, segs_row, segs_col, segs_own, cosine, sine):
    own = segs_own.shape[1]
    base = grid.sequence() * grid.rows
    lane = lax.broadcasted_iota(jnp.int32, (1, own), 1)

    def segs_of(q):
        return segs[pl.ds(base + q, 1), :]

    starts = []
    for slot in range(slot_count):
        start = jnp.full((1, 1), SEQ, jnp.int32)
        for q in range(grid.rows):
            there = jnp.where(segs_of(q) == slot, lane + q * own, SEQ)
            start = jnp.minimum(start, jnp.min(there, axis=1, keepdims=True))
        starts.append(start)
    half = cosine.shape[0]
    step = lax.broadcasted_iota(jnp.int32, (half, own), 0).astype(FULL)
    inverse_freq = 1.0 / jnp.exp(step * (2.0 / HEAD_DIM) * jnp.log(FULL(10000.0)))
    for e in range(grid.rows):
        q = grid.row() ^ e
        span = slice(e * own, (e + 1) * own)
        row = segs_of(q)
        position = lane + q * own
        for slot in range(slot_count):
            position = position - jnp.where(row == slot, starts[slot], 0)
        angle = position.astype(FULL) * inverse_freq
        cosine[:, span] = jnp.cos(angle)
        sine[:, span] = jnp.sin(angle)
        segs_row[:, span] = row
        segs_col[span, :] = jnp.broadcast_to(row.astype(FULL), (8, own)).T[:, :1].astype(jnp.int32)
    segs_own[...] = segs_row[:, :own]


def first_norm(grid, segs, *rest):
    bundles, (input_out, stream_out, cot_out, mods_out) = rest[: grid.cols], rest[grid.cols :]
    size, own = bundles[0].shape[0], input_out.shape[1]
    for step in range(grid.cols):
        place = pl.ds(block_start(grid.source(step), size), size)
        stream_out[place, :] = bundles[step][:, :own]
        cot_out[place, :] = bundles[step][:, own : 2 * own]
        mods_out[place, :] = bundles[step][:, 2 * own :]
    stream = stream_out[...].astype(FULL)
    mods = mods_out[...]
    pick = token_mods_of(mods, segs[...])
    normed, _ = normalize(stream)
    scaled = normed * column_of(mods, GAIN_ONE)
    input_out[...] = (scaled * (1.0 + pick(1)) + pick(0)).astype(LOW)


def branch_grad(segs, mods, cot, branch_out):
    pick = token_mods_of(mods[...], segs[...])
    branch_out[...] = (cot[...].astype(FULL) * pick(5)).astype(LOW)


def attend(weight_all, cosine, sine, *rest):
    pieces, (segs_row, segs_col), outs = rest[:4], rest[4:6], rest[6:]
    parts, (query, key, value, mixed, logsum, key_rows) = outs[:3], outs[3:]
    own = pieces[0].shape[1]
    head_width = query.shape[0]
    weight, proj = weight_all[:, : 3 * head_width], weight_all[:, 3 * head_width :]
    half = HEAD_DIM // 2
    scale = HEAD_DIM ** (-0.5)
    for e in range(4):
        span = slice(e * own, (e + 1) * own)
        cos, sin = cosine[:, span], sine[:, span]
        found = dot(weight, pieces[e][...], (0, 0))
        for h in range(head_width // HEAD_DIM):
            for out, base, factor in ((query, 0, scale), (key, head_width, 1.0)):
                at = h * HEAD_DIM
                one = found[base + at : base + at + half]
                two = found[base + at + half : base + at + HEAD_DIM]
                out[at : at + half, span] = ((one * cos - two * sin) * factor).astype(LOW)
                out[at + half : at + HEAD_DIM, span] = ((two * cos + one * sin) * factor).astype(LOW)
        value[:, span] = found[2 * head_width :].astype(LOW)
    ship(query, key, value)
    key_segs = jnp.where(segs_col[...] == 0, -1, segs_col[...])
    for h in range(head_width // HEAD_DIM):
        rows = slice(h * HEAD_DIM, (h + 1) * HEAD_DIM)
        key_rows[h] = key[rows, :].astype(FULL).T.astype(LOW)
    for e in (3, 1, 2, 0):
        span = slice(e * own, (e + 1) * own)
        query_segs = segs_row[:, span]
        allowed = key_segs == query_segs
        padding = (query_segs == 0).astype(FULL)
        for h in range(head_width // HEAD_DIM):
            rows = slice(h * HEAD_DIM, (h + 1) * HEAD_DIM)
            scores = dot(key_rows[h], query[rows, span], (1, 0))
            scores = jnp.where(allowed, scores, MASK_FILL)
            largest = jnp.maximum(jnp.max(scores, axis=0, keepdims=True), MASK_FLOOR)
            exponent = jnp.exp(scores - largest)
            total = jnp.sum(exponent, axis=0, keepdims=True) + padding
            found = dot(value[rows, :], exponent.astype(LOW), (1, 0))
            mixed[rows, span] = (found / total).astype(LOW)
            logsum[h : h + 1, span] = largest + jnp.log(total)
        part_of(parts, e)[...] = dot(proj, mixed[:, span], (1, 0)).astype(LOW)
        ship_part(parts, e)


def second_norm(segs, mods, stream, part, near, far, input_out, middle_out, attn_out):
    pick = token_mods_of(mods[...], segs[...])
    attn = three_terms(part, near, far)
    attn_out[...] = attn.astype(LOW)
    middle = stream[...].astype(FULL) + pick(2) * attn
    middle_out[...] = middle
    normed, _ = normalize(middle)
    scaled = normed * column_of(mods, GAIN_TWO)
    input_out[...] = (scaled * (1.0 + pick(4)) + pick(3)).astype(LOW)


GELU_SCALE = 0.7978845608028654
GELU_CUBE = 0.044715


FEED_ORDER = (0, 1, 2, 3)


def feed_first(weights, up_bias, *rest):
    sides, outs = rest[:8], rest[8:]
    parts, results, hidden, pre_grad = outs[:3], outs[3:6], outs[6:10], outs[10:14]
    count = hidden[0].shape[0]
    up, down = weights[:, :count], weights[:, count:]
    bias = jnp.broadcast_to(up_bias[...].astype(FULL)[None], (8, count)).T[:, :1]
    for i, e in enumerate(FEED_ORDER):
        piece, branch = sides[2 * i], sides[2 * i + 1]
        pre = dot(up, piece[...], (0, 0)) + bias
        square = pre * pre
        curve = jnp.tanh(GELU_SCALE * (pre + GELU_CUBE * square * pre))
        hidden[e][...] = (0.5 * pre * (1.0 + curve)).astype(LOW)
        slope = 0.5 * (1.0 + curve) + 0.5 * pre * (1.0 - curve * curve) * (
            GELU_SCALE * (1.0 + 3.0 * GELU_CUBE * square)
        )
        grad = dot(down, branch[...], (0, 0))
        pre_grad[e][...] = (grad * slope).astype(LOW)
        ship(hidden[e], pre_grad[e])
        part_of(parts, e)[...] = dot(up, pre_grad[e][...], (1, 0)).astype(LOW)
        part_of(results, e)[...] = dot(down, hidden[e][...], (1, 0)).astype(LOW)
        if e == 3:
            ship(parts[2], results[2])
        elif e != 1:
            ship(parts[e // 2], results[e // 2])


def feed_grads_of(pre_grad, inputs_all, hidden, branch_all, grads):
    count = hidden.shape[0]
    blocks = grads.shape[0]
    size = inputs_all.shape[0] // blocks
    ones = jnp.ones((16, hidden.shape[1]), LOW)
    bias = dot(ones, pre_grad[...], (1, 1)).astype(LOW)
    for j in range(blocks):
        grads[j, size:, :count] = bias
        grads[j, size:, count:] = jnp.zeros_like(bias)
    up_total = dot(inputs_all[...], pre_grad[...], (1, 1)).astype(LOW)
    for j in range(blocks):
        grads[j, :size, :count] = up_total[j * size : (j + 1) * size]
    down_total = dot(branch_all[...], hidden[...], (1, 1)).astype(LOW)
    for j in range(blocks):
        grads[j, :size, count:] = down_total[j * size : (j + 1) * size]


def middle_grad(segs, mods, middle, cot, part, near, far, grad_out, attn_grad_out, input_grad_out):
    pick = token_mods_of(mods[...], segs[...])
    input_grad = three_terms(part, near, far)
    input_grad_out[...] = input_grad.astype(LOW)
    normed, inverse = normalize(middle[...])
    grad_scaled = input_grad * (1.0 + pick(4)) * column_of(mods, GAIN_TWO)
    grad = cot[...].astype(FULL) + normalize_back(grad_scaled, normed, inverse)
    grad_out[...] = grad
    attn_grad_out[...] = (grad * pick(2)).astype(LOW)


def doc_sums(values, chosen):
    terms = jnp.concatenate(split(values, 2), 1).astype(LOW)
    return dot(jnp.concatenate([chosen, chosen], 1), terms, (1, 1))


def slot_rows(segs):
    return (lax.broadcasted_iota(jnp.int32, (16, segs.shape[1]), 0) == segs).astype(LOW)


def finish_forward(grid, segs, mods, middle, cot, attn, grad_middle, input_grad, part, near, far, *rest):
    outs, (small, result_low) = rest[: grid.cols], rest[grid.cols :]
    pick = token_mods_of(mods[...], segs[...])
    chosen = slot_rows(segs[...])
    ones = jnp.ones(chosen.shape, LOW)
    valid = (segs[...] != 0).astype(FULL)
    mlp = (
        three_terms(part, near, far)
        + column_of(mods, DOWN_BIAS)
    )
    gate = pick(5)
    mlp_term = gate * mlp
    result = middle[...] + mlp_term
    result_low[...] = result.astype(LOW)
    size = outs[0].shape[0]
    for step in range(grid.cols):
        outs[step][...] = result_low[pl.ds(block_start(grid.source(step), size), size), :]
    small[...] = jnp.zeros(small.shape, FULL)
    cot_full = cot[...].astype(FULL)
    attn_all = attn[...].astype(FULL)
    input_all = input_grad[...].astype(FULL)
    normed, _ = normalize(middle[...])
    along = input_all * normed
    terms = (
        (2, grad_middle[...] * attn_all),
        (3, input_all),
        (4, along * column_of(mods, GAIN_TWO)),
        (5, cot_full * mlp),
    )
    for k, values in terms:
        small[k * SLOTS : (k + 1) * SLOTS, :] = doc_sums(values, chosen)[:SLOTS]
    small[GAIN_TWO : GAIN_TWO + 1, :] = doc_sums(along * (1.0 + pick(4)), ones)[:1]
    branch = (cot_full * gate).astype(LOW)
    small[DOWN_BIAS : DOWN_BIAS + 1, :] = dot(ones, branch, (1, 1))[:1]
    attn_term = pick(2) * attn_all
    squares = [
        jnp.sum(jnp.sum(v * v, axis=0, keepdims=True) * valid, axis=1, keepdims=True)
        for v in (result, attn_term, mlp_term)
    ]
    squares.append(jnp.sum(valid, axis=1, keepdims=True) * middle.shape[0])
    lane = lax.broadcasted_iota(jnp.int32, (1, small.shape[1]), 1)
    total = jnp.zeros(lane.shape, FULL)
    for i, value in enumerate(squares):
        total = jnp.where(lane == i, value, total)
    small[STATS : STATS + 1, :] = total


def attend_back(pieces_of, key, value, weight_all, first, query, mixed, logsum, segs_row, segs_col, cosine, sine, *rest):
    last = pieces_of[0] != 0
    if last:
        second, key_in, value_in, query_in, rest = rest[0], rest[1], rest[2], rest[3], rest[4:]
        parts, (grads, key_rows, value_rows, out_grad, key_grad, value_grad) = rest[:3], rest[3:]
    else:
        second, (grads, key_grad, value_grad, key_rows, value_rows, out_grad) = rest[0], rest[1:]
    pieces = dict(zip(pieces_of, (first, second)))
    own = first.shape[1]
    head_width = query.shape[0]
    heads = head_width // HEAD_DIM
    weight, proj = weight_all[:, : 3 * head_width], weight_all[:, 3 * head_width :]
    half = HEAD_DIM // 2
    scale = HEAD_DIM ** (-0.5)
    for h in range(heads):
        rows = slice(h * HEAD_DIM, (h + 1) * HEAD_DIM)
        key_rows[h] = key[rows, :].astype(FULL).T.astype(LOW)
        value_rows[h] = value[rows, :].astype(FULL).T.astype(LOW)
    key_segs = jnp.where(segs_col[...] == 0, -1, segs_col[...])
    if last:
        grads[:head_width, : 2 * own] = query_in[...]
        key_grad[...] = key_in[...]
        value_grad[...] = value_in[...]
    else:
        key_grad[...] = jnp.zeros(key_grad.shape, FULL)
        value_grad[...] = jnp.zeros(value_grad.shape, FULL)

    def turn_back(grad, span, base, at):
        cos, sin = cosine[:, span], sine[:, span]
        one, two = grad[:half], grad[half:]
        grads[base + at : base + at + half, span] = (one * cos + two * sin).astype(LOW)
        grads[base + at + half : base + at + HEAD_DIM, span] = (two * cos - one * sin).astype(LOW)

    for e in pieces_of:
        span = slice(e * own, (e + 1) * own)
        allowed = key_segs == segs_row[:, span]
        out_grad[...] = dot(proj, pieces[e][...], (0, 0)).astype(LOW)
        for h in range(heads):
            rows = slice(h * HEAD_DIM, (h + 1) * HEAD_DIM)
            back = out_grad[rows, :]
            inner = jnp.sum(
                back.astype(FULL) * mixed[rows, span].astype(FULL), axis=0, keepdims=True
            )
            scores = dot(key_rows[h], query[rows, span], (1, 0))
            scores = jnp.where(allowed, scores, MASK_FILL)
            probability = jnp.exp(scores - logsum[h : h + 1, span])
            grad_probs = dot(value_rows[h], back, (1, 0))
            score_grad = (probability * (grad_probs - inner)).astype(LOW)
            value_grad[rows, :] += dot(back, probability.astype(LOW), (1, 1))
            key_grad[rows, :] += dot(query[rows, span], score_grad, (1, 1))
            turn_back(dot(key[rows, :], score_grad, (1, 0)) * scale, span, 0, h * HEAD_DIM)
    if not last:
        return
    for e in (3, 1, 2, 0):
        span = slice(e * own, (e + 1) * own)
        for h in range(heads):
            turn_back(key_grad[h * HEAD_DIM : (h + 1) * HEAD_DIM, span], span, head_width, h * HEAD_DIM)
        grads[2 * head_width :, span] = value_grad[:, span].astype(LOW)
        part_of(parts, e)[...] = dot(weight, grads[:, span], (1, 0)).astype(LOW)
        ship_part(parts, e)


def attend_weights(grid, grads, mixed, inputs_all, pieces_all, keep, send, total):
    count = grads.shape[0]
    total[:, :count] = dot(inputs_all[...], grads[...], (1, 1)).astype(LOW)
    total[:, count:] = dot(pieces_all[...], mixed[...], (1, 1)).astype(LOW)
    size = keep.shape[1]
    for j in range(grid.cols):
        send[j] = total[pl.ds(grid.half_start(grid.col() ^ j, 1 - grid.half(), size), size), :]
    ship(send)
    for j in range(grid.cols):
        keep[j] = total[pl.ds(grid.half_start(grid.col() ^ j, grid.half(), size), size), :]


def pair_sum(keep, got, *outs):
    for j, out in enumerate(outs):
        out[...] = (keep[j].astype(FULL) + got[j].astype(FULL)).astype(LOW)


def block_sum(*rest):
    total = rest[0][...].astype(FULL)
    for piece in rest[1:-1]:
        total = total + piece[...].astype(FULL)
    rest[-1][...] = total.astype(LOW)


def attn_weight_out(grid, own, other, qkv_out, proj_out, total):
    size = own.shape[0]
    total[pl.ds(grid.half_start(0, grid.half(), size), size), :] = own[...]
    total[pl.ds(grid.half_start(0, 1 - grid.half(), size), size), :] = other[...]
    width = qkv_out.shape[2]
    for i in range(3):
        qkv_out[i] = total[:, i * width : (i + 1) * width].astype(FULL)
    proj_out[...] = total[:, 3 * width :].astype(FULL).T


def feed_weight_out(*rest):
    parts, (up_out, bias_out, down_out) = rest[:-3], rest[-3:]
    total = parts[0][...].astype(FULL)
    for part in parts[1:]:
        total = total + part[...].astype(FULL)
    size, count = up_out.shape
    up_out[...] = total[:size, :count]
    down_out[...] = total[:size, count:]
    bias_out[...] = total[size, :count]


def finish_backward(grid, segs, mods, stream, grad_middle, small_in, part, near, far, *rest):
    outs, (grad_low, blocks) = rest[: grid.cols], rest[grid.cols :]
    pick = token_mods_of(mods[...], segs[...])
    chosen = slot_rows(segs[...])
    ones = jnp.ones(chosen.shape, LOW)
    input_grad = three_terms(part, near, far)
    normed, inverse = normalize(stream[...].astype(FULL))
    gain = column_of(mods, GAIN_ONE)
    grown = input_grad * (1.0 + pick(1))
    grad = grad_middle[...] + normalize_back(grown * gain, normed, inverse)
    grad_low[...] = grad.astype(LOW)
    size = grad.shape[0] // grid.cols
    own = grad.shape[1]
    for step in range(grid.cols):
        place = pl.ds(block_start(grid.source(step), size), size)
        outs[step][:, :own] = grad_low[place, :]
    shift = doc_sums(input_grad, chosen)[:SLOTS]
    scale = doc_sums(input_grad * normed * gain, chosen)[:SLOTS]
    norm_gain = doc_sums(grown * normed, ones)[:1]
    for c in range(grid.cols):
        span = slice(c * size, (c + 1) * size)
        blocks[c, :, :size] = small_in[:, span]
        blocks[c, :SLOTS, :size] = shift[:, span]
        blocks[c, SLOTS : 2 * SLOTS, :size] = scale[:, span]
        blocks[c, GAIN_ONE : GAIN_ONE + 1, :size] = norm_gain[:, span]
        blocks[c, STATS : STATS + 1, :size] = small_in[STATS : STATS + 1, :size]
    for step in range(grid.cols):
        terms = split(blocks[grid.source(step)].T, 2)
        outs[step][:, own:] = jnp.concatenate(terms, 1).astype(LOW)


def modulation_back(grid, slot_count, dp_count, *rest):
    times, (table, weight), rest = rest[:dp_count], rest[dp_count : dp_count + 2], rest[dp_count + 2 :]
    pieces, outs = rest[: 2 * dp_count], rest[2 * dp_count :]
    weight_out, bias_out, gain_one_out, gain_two_out, down_bias_out, stats_out, embed_out = outs[:7]
    embed, grads = outs[7:]
    per = grid.per_row
    embed[...] = jnp.zeros(embed.shape, FULL)
    size = grads.shape[2]
    total = jnp.zeros((LANES - 6 * SLOTS, size), FULL)
    for d in range(dp_count):
        for far in range(2):
            piece = pieces[2 * d + far]
            for s in range(2 * per):
                sequence = (grid.row() ^ (2 * far + s // per)) * per + s % per
                first = block_start(d * per * grid.rows + sequence, SLOTS)
                for slot in range(slot_count):
                    time = times[d][sequence, slot]
                    embed[pl.ds(first + slot, 1), :] = table[pl.ds(time, 1), :]
                for k in range(6):
                    grads[k, pl.ds(first, SLOTS), :] = piece[s, k * SLOTS : (k + 1) * SLOTS, :]
                total = total + piece[s, 6 * SLOTS :, :]
    for k in range(6):
        rows = grads[k]
        weight_out[k] = dot(rows, embed[...], (0, 0), PRECISE)
        bias_out[k : k + 1, :] = jnp.sum(rows, axis=0, keepdims=True)
        part = dot(rows, weight[k].astype(FULL), (1, 0), PRECISE)
        embed_out[...] = part if k == 0 else embed_out[...] + part
    gain_one_out[...] = total[GAIN_ONE - 6 * SLOTS]
    gain_two_out[...] = total[GAIN_TWO - 6 * SLOTS]
    down_bias_out[...] = total[DOWN_BIAS - 6 * SLOTS]
    squares = total[STATS - 6 * SLOTS : STATS - 6 * SLOTS + 1, :]
    stats_out[...] = jnp.sqrt(squares / squares[:, 3:4])[0, :3]


def table_sum(grid, slot_count, dp_count, *rest):
    times, parts, (table_out, total) = rest[:dp_count], rest[dp_count:-2], rest[-2:]
    found = parts[0][...]
    for part in parts[1:]:
        found = found + part[...]
    total[...] = found
    table_out[...] = jnp.zeros(table_out.shape, FULL)
    for d in range(dp_count):
        for sequence in range(grid.cols):
            for slot in range(slot_count):
                time = times[d][sequence, slot]
                at = (d * grid.cols + sequence) * SLOTS + slot
                table_out[pl.ds(time, 1), :] += total[at : at + 1, :]


def per_device(
    tokens,
    cotangent,
    segment_ids,
    doc_times,
    time_table,
    attn_gain,
    mlp_gain,
    mod_weight,
    mod_bias,
    qkv_weight,
    proj_weight,
    up_weight,
    up_bias,
    down_weight,
    down_bias,
):
    grid = Grid()
    dp_count = lax.axis_size("dp")
    width_local = tokens.shape[0]
    width = width_local * grid.cols
    own = tokens.shape[1] // grid.cols
    head_width = qkv_weight.shape[2]
    hidden_local = up_weight.shape[1]
    slot_count = doc_times.shape[1]
    cond_width = mod_weight.shape[2]
    if segment_ids.shape[0] != grid.cols * SEQ or own * grid.rows != SEQ or grid.rows != 4:
        raise ValueError("sequence split")
    low_tile = shape((width, own), LOW)
    full_tile = shape((width, own), FULL)
    low_piece = shape((width_local, own), LOW)
    part_tiles = [low_tile, low_tile, shape((2 * width, own), LOW)]

    part_rows = width_local // dp_count
    part_start = lax.axis_index("dp") * part_rows

    def gather_weight(parts):
        parts = [lax.dynamic_slice_in_dim(p, part_start, part_rows, 0) for p in parts]
        part = jnp.concatenate(parts, 1) if len(parts) > 1 else parts[0]
        return lax.all_gather(part, ("col", "dp"), axis=0, tiled=True)

    attn_block = run(
        pack, "pack", [shape((width_local, 4 * head_width), LOW)],
        [qkv_weight.transpose(1, 0, 2), proj_weight],
    )
    attn_weights = gather_weight(attn_block)

    bundles = run(
        functools.partial(prepare, grid, slot_count), "prepare",
        [shape((width_local, 2 * own + 2 * LANES), LOW)] * grid.cols,
        [doc_times, time_table, mod_weight, mod_bias, attn_gain, mlp_gain,
         down_bias, tokens, cotangent],
        [pltpu.VMEM((SLOTS, cond_width), FULL), pltpu.VMEM((LANES, width_local), FULL),
         pltpu.VMEM((grid.per_row, width_local, 2 * LANES), LOW)],
        smem=1,
    )
    bundles = relayout(bundles)
    segs_row, segs_col, segs_own, cosine, sine = run(
        functools.partial(places, grid, slot_count), "places",
        [shape((1, SEQ), jnp.int32), shape((SEQ, 1), jnp.int32), shape((1, own), jnp.int32)]
        + [shape((HEAD_DIM // 2, SEQ), FULL)] * 2,
        [segment_ids.reshape(-1, own)],
    )
    input_one, stream, cot, mods = run(
        functools.partial(first_norm, grid), "first_norm",
        [low_tile] * 3 + [shape((width, 2 * LANES), LOW)], [segs_own] + bundles,
    )

    def branch_filler(ready):
        [late] = after([ready], [cot])
        return run(branch_grad, "branch_grad", [low_tile], [segs_own, mods, late])

    rows_one, [branch] = gather_rows(input_one, branch_filler)
    branch_rows = gather_rows(branch)
    times = [doc_times] + [swap(doc_times, "dp", d) for d in range(1, dp_count)]
    rows_one[3:] = after([branch_rows[1]] + times[1:], rows_one[3:])

    feed_weights = gather_weight(after(rows_one[2:3] + [attn_weights], [up_weight, down_weight]))
    *parts, query, key, value, mixed, logsum = run(
        attend, "attend",
        part_tiles + [shape((head_width, SEQ), LOW)] * 4 + [shape((8, SEQ), FULL)],
        [attn_weights, cosine, sine] + rows_one + [segs_row, segs_col],
        [pltpu.VMEM((head_width // HEAD_DIM, SEQ, HEAD_DIM), LOW)],
    )
    attn_terms = scatter_rows(parts)
    input_two, middle, attn = run(
        second_norm, "second_norm", [low_tile, full_tile, low_tile],
        [segs_own, mods, stream] + attn_terms,
    )
    rows_two = gather_rows(input_two)
    hidden_tile = shape((hidden_local, own), LOW)
    sides = [side for e in FEED_ORDER for side in (rows_two[e], branch_rows[e])]
    found = run(
        feed_first, "feed_first", part_tiles * 2 + [hidden_tile] * 8, [feed_weights, up_bias] + sides
    )
    parts, results, hidden, pre_grad = found[:3], found[3:6], found[6:10], found[10:]

    def grads_filler(ready):
        late = after([ready], pre_grad)
        return run(
            feed_grads_of, "feed_grads",
            [shape((grid.cols, width_local + 16, 2 * hidden_local), LOW)],
            [Joined(late), Joined(rows_two), Joined(hidden), Joined(branch_rows)],
        )

    input_terms, [feed_grads] = scatter_rows(parts, grads_filler, True)
    feed_grads = lax.psum_scatter(
        feed_grads.reshape(-1, 2 * hidden_local), "col", scatter_dimension=0, tiled=True
    )
    grad_middle, grad_attn, input_grad = run(
        middle_grad, "middle_grad", [full_tile, low_tile, low_tile],
        [segs_own, mods, middle, cot] + input_terms,
    )

    mlp_near, mlp_total = scatter_near(results)
    head_tile = shape((head_width, SEQ), FULL)
    back_scratch = [pltpu.VMEM((head_width // HEAD_DIM, SEQ, HEAD_DIM), LOW)] * 2 + [
        pltpu.VMEM((head_width, own), LOW)
    ]
    saved = [query, mixed, logsum, segs_row, segs_col, cosine, sine]

    def first_filler(ready):
        return run(
            functools.partial(attend_back, (0, 1)), "attend_back_first",
            [shape((head_width, 2 * own), LOW), head_tile, head_tile],
            [key, value, attn_weights, grad_attn] + saved + [ready], back_scratch,
        )

    attn_rows, (query_grad, key_grad, value_grad) = gather_rows(grad_attn, first_filler)
    [mlp_total] = after(attn_rows[2:3], [mlp_total])
    mlp_terms = [results[0], mlp_near, swap(mlp_total, "row", 2)]
    *parts, qkv_grads = run(
        functools.partial(attend_back, (2, 3)), "attend_back_last",
        part_tiles + [shape((3 * head_width, SEQ), LOW)],
        [key, value, attn_weights, attn_rows[2]] + saved
        + [attn_rows[3], key_grad, value_grad, query_grad],
        back_scratch + [pltpu.VMEM((head_width, SEQ), FULL)] * 2,
    )

    def back_filler(ready):
        [late] = after([ready], [qkv_grads])
        blocks = run(
            functools.partial(attend_weights, grid), "attend_weights",
            [shape((grid.cols, width_local // 2, 4 * head_width), LOW)] * 2,
            [late, mixed, Joined(rows_one), Joined(attn_rows)], [pltpu.VMEM((width, 4 * head_width), LOW)],
        )
        [first] = after(blocks[:1], mlp_terms[:1])
        found = run(
            functools.partial(finish_forward, grid), "finish_forward",
            [low_piece] * grid.cols + [shape((LANES, width), FULL)],
            [segs_own, mods, middle, cot, attn, grad_middle, input_grad, first] + mlp_terms[1:],
            [pltpu.VMEM((width, own), LOW)],
        )
        return found + blocks

    parts[2:] = after(mlp_terms[2:], parts[2:])
    back_terms, found = scatter_rows(parts, back_filler)
    result_chunks, small, attn_grads = found[: grid.cols], found[grid.cols], found[grid.cols + 1 :]
    bundles = run(
        functools.partial(finish_backward, grid), "finish_backward",
        [shape((width_local, own + 2 * LANES), LOW)] * grid.cols,
        [segs_own, mods, stream, grad_middle, small] + back_terms,
        [pltpu.VMEM((width, own), LOW), pltpu.VMEM((grid.cols, LANES, width_local), FULL)],
    )
    out_tile = shape((width_local, grid.cols * own), LOW)
    bundles = relayout(bundles, back=True)
    tokens_grad, small = run(
        functools.partial(unbundle, grid), "unbundle",
        [out_tile, shape((grid.per_row, LANES, width_local), FULL)], bundles,
    )
    [block_output] = run(
        functools.partial(join, grid), "join", [out_tile],
        relayout(after(bundles, result_chunks), back=True),
    )

    small = jnp.concatenate([small, swap(small, "row", 1)], 0)
    pieces = []
    for d in range(dp_count):
        for far in range(2):
            count = dp_count * grid.rows
            pairs = [(i, i ^ (d * grid.rows + 2 * far)) for i in range(count)]
            pieces.append(lax.ppermute(small, ("dp", "row"), pairs) if d or far else small)
    seq_total = grid.cols * dp_count
    vector = shape((width_local,), FULL)
    embed_tile = shape((seq_total * SLOTS, cond_width), FULL)
    weight_out, bias_out, gain_one_out, gain_two_out, down_bias_out, stats, embed = run(
        functools.partial(modulation_back, grid, slot_count, dp_count), "modulation_back",
        [
            shape((6, width_local, cond_width), FULL), shape((6, width_local), FULL),
            vector, vector, vector, shape((3,), FULL), embed_tile,
        ],
        times + [time_table, mod_weight] + pieces,
        [pltpu.VMEM((seq_total * SLOTS, cond_width), FULL),
         pltpu.VMEM((6, seq_total * SLOTS, width_local), FULL)],
        smem=dp_count,
    )
    [table_out] = run(
        functools.partial(table_sum, grid, slot_count, dp_count), "table_sum",
        [shape(time_table.shape, FULL)],
        times + [embed] + [swap(embed, "col", j) for j in range(1, grid.cols)],
        [pltpu.VMEM((seq_total * SLOTS, cond_width), FULL)], smem=dp_count,
    )

    def all_dp(part):
        return [part] + [swap(part, "dp", d) for d in range(1, dp_count)]

    half_tile = shape((width_local // 2, 4 * head_width), LOW)
    pieces = run(pair_sum, "pair_sum", [half_tile] * grid.cols, [attn_grads[0], swap(attn_grads[1], "dp", 1)])
    pieces = pieces[:1] + [swap(pieces[j], "col", j) for j in range(1, grid.cols)]
    [attn_half] = run(block_sum, "block_sum", [half_tile], pieces)
    bit = 2
    while bit < dp_count:
        attn_half = (attn_half.astype(FULL) + swap(attn_half, "dp", bit).astype(FULL)).astype(LOW)
        bit *= 2
    up_out, up_bias_out, down_out = run(
        feed_weight_out, "feed_weight_out",
        [shape(up_weight.shape, FULL), shape(up_bias.shape, FULL), shape(down_weight.shape, FULL)],
        all_dp(feed_grads),
    )
    qkv_out, proj_out = run(
        functools.partial(attn_weight_out, grid), "attn_weight_out",
        [shape((3, width_local, head_width), FULL), shape(proj_weight.shape, FULL)],
        [attn_half, swap(attn_half, "dp", 1)], [pltpu.VMEM((width_local, 4 * head_width), LOW)],
    )
    return (
        block_output,
        tokens_grad,
        table_out,
        gain_one_out,
        gain_two_out,
        weight_out,
        bias_out,
        qkv_out.transpose(1, 0, 2),
        proj_out,
        up_out,
        up_bias_out,
        down_out,
        down_bias_out,
        stats,
    )


def solution(mesh):
    return jax.shard_map(
        per_device,
        mesh=mesh,
        in_specs=(
            P("col", ("dp", "row")),
            P("col", ("dp", "row")),
            P("dp"),
            P("dp", None),
            P(),
            P("col"),
            P("col"),
            P(None, "col", None),
            P(None, "col"),
            P("col", None, "row"),
            P("row", "col"),
            P("col", "row"),
            P("row"),
            P("col", "row"),
            P("col"),
        ),
        out_specs=(
            P("col", ("dp", "row")),
            P("col", ("dp", "row")),
            P(),
            P("col"),
            P("col"),
            P(None, "col", None),
            P(None, "col"),
            P("col", None, "row"),
            P("row", "col"),
            P("col", "row"),
            P("row"),
            P("col", "row"),
            P("col"),
            P(),
        ),
        check_vma=False,
    )
```

```python
import functools

import jax
import jax.numpy as jnp
from jax import lax
from jax.experimental import pallas as pl
from jax.experimental.pallas import tpu as pltpu
from jax.sharding import PartitionSpec as P

HEAD_DIM = 64
SEQ = 1024

PRECISE = lax.Precision.HIGHEST
EPSILON = 1e-05
MASK_FILL = -1e30
MASK_FLOOR = -1e29
LOW = jnp.bfloat16
FULL = jnp.float32
SLOTS = 8
LANES = 64
GAIN_ONE, GAIN_TWO, DOWN_BIAS = 48, 49, 50
STATS = 51
VMEM_LIMIT = 56 * 1024 * 1024
NEAR = {'unbundle': 12, 'modulation_back': 12, 'table_sum': 12, 'attn_weight_out': 12, 'feed_weight_out': 12, 'pair_sum': 12, 'block_sum': 12, 'join': 12, 'finish_forward': 12, 'finish_backward': 12, 'feed_first': 56, 'attend_back_first': 56, 'attend_back_last': 56, 'second_norm': 12, 'middle_grad': 12, 'branch_grad': 12, 'first_norm': 12, 'attend': 40}


def swap(values, axis, bit):
    count = lax.axis_size(axis)
    return lax.ppermute(values, axis, [(i, i ^ bit) for i in range(count)])


def gather_rows(values, filler=None, deps=()):
    far = swap(values, "row", 2)
    near = swap(values, "row", 1)
    filled = None
    if filler is not None:
        filled = filler(near)
        deps = list(deps) + list(filled[:1])
    if deps:
        [far] = after(deps, [far])
    last = swap(far, "row", 1)
    pieces = [values, near, far, last]
    return pieces if filler is None else (pieces, after([last], filled))


def scatter_rows(parts, filler=None, hold=False):
    width = parts[0].shape[0]
    near = swap(parts[2], "row", 1)
    total = (parts[1].astype(FULL) + near[width:].astype(FULL)).astype(LOW)
    far = swap(total, "row", 2)
    if filler is None:
        return [parts[0], near, far]
    filled = filler(total)
    [far] = after(filled[:1], [far])
    return [parts[0], near, far], after([far], filled) if hold else filled


def scatter_near(parts):
    near = swap(parts[2], "row", 1)
    total = (parts[1].astype(FULL) + near[parts[0].shape[0] :].astype(FULL)).astype(LOW)
    return near, total


def col_of_row(row_count):
    if row_count == 4:
        return [0, 2, 1, 3]
    return list(range(row_count))


def relayout_pairs(step):
    row_count = lax.axis_size("row")
    col_count = lax.axis_size("col")
    per_row = col_count // row_count
    table = col_of_row(row_count)
    pairs = []
    for r in range(row_count):
        for c in range(col_count):
            j, q = divmod((c + step) % col_count, row_count)
            pairs.append((r * col_count + c, q * col_count + table[r] * per_row + j))
    return pairs


def relayout(pieces, back=False):
    got = []
    for step, piece in enumerate(pieces):
        pairs = relayout_pairs(step)
        if back:
            pairs = [(b, a) for a, b in pairs]
        got.append(lax.ppermute(piece, ("row", "col"), pairs))
    return got


def after(deps, values):
    return lax.optimization_barrier((list(values), list(deps)))[0]


class Grid:
    def __init__(self):
        self.rows = lax.axis_size("row")
        self.cols = lax.axis_size("col")
        self.per_row = self.cols // self.rows
        table = col_of_row(self.rows)
        self.seq_of_col = [0] * self.cols
        for r in range(self.rows):
            for j in range(self.per_row):
                self.seq_of_col[table[r] * self.per_row + j] = r * self.per_row + j

    def row(self):
        return lax.axis_index("row")

    def col(self):
        return lax.axis_index("col")

    def sequence(self):
        return sum(jnp.where(self.col() == c, s, 0) for c, s in enumerate(self.seq_of_col))

    def half(self):
        return lax.axis_index("dp") % 2

    def half_start(self, block, which, size):
        return pl.multiple_of((2 * block + which) * size, size)

    def source(self, step):
        mine = self.col() % self.per_row * self.rows + self.row()
        return (mine + self.cols - step) % self.cols

    def place(self, step):
        return (self.col() + step) % self.cols


def whole(memory_space=pltpu.VMEM):
    return pl.BlockSpec(memory_space=memory_space)


class Joined:
    def __init__(self, values):
        self.values = values


class FarIn:
    def __init__(self, sources, buffer, sems):
        self.buffer, self.waiting = buffer, True
        if len(sources) == 1:
            places = [buffer]
        else:
            count = sources[0].shape[1]
            places = [buffer.at[:, i * count : (i + 1) * count] for i in range(len(sources))]
        self.copies = [
            pltpu.make_async_copy(source, place, sem)
            for source, place, sem in zip(sources, places, sems)
        ]
        for copy in self.copies:
            copy.start()

    @property
    def shape(self):
        return self.buffer.shape

    @property
    def ref(self):
        if self.waiting:
            for copy in self.copies:
                copy.wait()
            self.waiting = False
        return self.buffer

    @property
    def at(self):
        return self.ref.at

    def __getitem__(self, index):
        return self.ref[index]


class FarOut:
    def __init__(self, buffer, target, sem):
        self.copy = pltpu.make_async_copy(buffer, target, sem)
        self.ref, self.shipped = buffer, False

    @property
    def shape(self):
        return self.ref.shape

    @property
    def at(self):
        return self.ref.at

    def __getitem__(self, index):
        return self.ref[index]

    def __setitem__(self, index, value):
        self.ref[index] = value

    def ship(self):
        if not self.shipped:
            self.copy.start()
            self.shipped = True


def ship(*refs):
    for ref in refs:
        if isinstance(ref, FarOut):
            ref.ship()


def run(body, name, outs, args, scratch=(), smem=0, flops=0):
    if name in NEAR:
        moved = sum(a.size * a.dtype.itemsize for a in list(args) + list(outs))
        found = pl.pallas_call(
            body,
            out_shape=list(outs),
            in_specs=[whole(pltpu.SMEM)] * smem + [whole() for _ in args[smem:]],
            out_specs=[whole() for _ in outs],
            scratch_shapes=list(scratch),
            compiler_params=pltpu.CompilerParams(vmem_limit_bytes=NEAR[name] * 1024 * 1024),
            cost_estimate=pl.CostEstimate(flops=flops, bytes_accessed=moved, transcendentals=0),
            name=name,
        )(*args)
        return list(found)
    groups = [a.values if isinstance(a, Joined) else [a] for a in args[smem:]]
    flat = [a for group in groups for a in group]
    outs = list(outs)
    buffers = [
        pltpu.VMEM((*group[0].shape[:-1], sum(a.shape[-1] for a in group)), group[0].dtype)
        for group in groups
    ] + [pltpu.VMEM(o.shape, o.dtype) for o in outs]
    moved = sum(a.size * a.dtype.itemsize for a in flat + outs)

    def kernel(*refs):
        scalars, rest = list(refs[:smem]), list(refs[smem:])
        sources, rest = rest[: len(flat)], rest[len(flat) :]
        targets, rest = rest[: len(outs)], rest[len(outs) :]
        own, rest = rest[: len(scratch)], rest[len(scratch) :]
        spaces, sems = rest[:-1], rest[-1]
        ins, count = [], 0
        for group, space in zip(groups, spaces):
            span = range(count, count + len(group))
            ins.append(FarIn([sources[i] for i in span], space, [sems.at[i] for i in span]))
            count += len(group)
        results = [
            FarOut(space, target, sems.at[count + i])
            for i, (space, target) in enumerate(zip(spaces[len(groups) :], targets))
        ]
        body(*scalars, *ins, *results, *own)
        ship(*results)
        for ref in ins:
            ref.ref
        for ref in results:
            ref.copy.wait()

    found = pl.pallas_call(
        kernel,
        out_shape=outs,
        in_specs=[whole(pltpu.SMEM)] * smem + [whole(pl.ANY) for _ in flat],
        out_specs=[whole(pl.ANY) for _ in outs],
        scratch_shapes=list(scratch) + buffers
        + [pltpu.SemaphoreType.DMA((len(flat) + len(outs),))],
        compiler_params=pltpu.CompilerParams(vmem_limit_bytes=VMEM_LIMIT),
        cost_estimate=pl.CostEstimate(flops=flops, bytes_accessed=moved, transcendentals=0),
        name=name,
    )(*args[:smem], *flat)
    return list(found)


def shape(dims, dtype):
    return jax.ShapeDtypeStruct(dims, dtype)


def dot(left, right, dims, precision=None):
    return lax.dot_general(
        left, right, (((dims[0],), (dims[1],)), ((), ())),
        preferred_element_type=FULL, precision=precision,
    )


def split(values, terms):
    found = []
    for _ in range(terms):
        term = values.astype(LOW).astype(FULL)
        found.append(term)
        values = values - term
    return found


def block_start(index, size):
    return pl.multiple_of(index * size, size)


def token_mods_of(mods, segs):
    rows = lax.broadcasted_iota(jnp.int32, (2 * LANES, segs.shape[1]), 0) % LANES

    def pick(k):
        chosen = (rows == segs + k * SLOTS).astype(LOW)
        return dot(mods, chosen, (1, 0))

    return pick


def part_of(parts, e):
    if e % 2 == 0:
        return parts[e // 2]
    width = parts[0].shape[0]
    return parts[2].at[(e // 2) * width : (e // 2 + 1) * width]


def ship_part(parts, e):
    if e != 3:
        ship({1: parts[2], 2: parts[1], 0: parts[0]}[e])


def three_terms(part, near, far):
    return (
        part[...].astype(FULL) + near[: part.shape[0], :].astype(FULL) + far[...].astype(FULL)
    )


def column_of(mods, lane):
    return mods[:, lane : lane + 1].astype(FULL) + mods[:, LANES + lane : LANES + lane + 1].astype(FULL)


def normalize(stream):
    count = 1.0 / stream.shape[0]
    center = jnp.sum(stream, axis=0, keepdims=True) * count
    offset = stream - center
    inverse = lax.rsqrt(jnp.sum(offset * offset, axis=0, keepdims=True) * count + EPSILON)
    return offset * inverse, inverse


def normalize_back(grad_normed, normed, inverse):
    count = 1.0 / normed.shape[0]
    center = jnp.sum(grad_normed, axis=0, keepdims=True) * count
    along = jnp.sum(grad_normed * normed, axis=0, keepdims=True) * count
    return inverse * (grad_normed - center - normed * along)


def prepare(grid, slot_count, times, table, weight, bias, gain_one, gain_two, down_bias, tokens, cot, *rest):
    outs, (embed, rows, blocks) = rest[: grid.cols], rest[grid.cols :]
    own = (outs[0].shape[1] - 2 * LANES) // 2
    rows[...] = jnp.zeros(rows.shape, FULL)
    for k in range(6):
        rows[k * SLOTS : (k + 1) * SLOTS, :] = jnp.broadcast_to(
            bias[k : k + 1, :].astype(FULL), (SLOTS, rows.shape[1])
        )
    rows[GAIN_ONE : GAIN_ONE + 1, :] = gain_one[...].astype(FULL)[None]
    rows[GAIN_TWO : GAIN_TWO + 1, :] = gain_two[...].astype(FULL)[None]
    rows[DOWN_BIAS : DOWN_BIAS + 1, :] = down_bias[...].astype(FULL)[None]
    fixed = rows[...].T
    cond = weight.shape[2]
    flat = jnp.concatenate([weight[k] for k in range(6)], 1)
    row = lax.broadcasted_iota(jnp.int32, (LANES, 6 * cond), 0)
    lane = lax.broadcasted_iota(jnp.int32, (LANES, 6 * cond), 1)
    match = row // SLOTS == lane // cond
    for j in range(grid.per_row):
        embed[...] = jnp.zeros(embed.shape, FULL)
        for slot in range(slot_count):
            time = times[grid.row() * grid.per_row + j, slot]
            embed[slot : slot + 1, :] = table[pl.ds(time, 1), :]
        tiled = jnp.concatenate([embed[...]] * (LANES // SLOTS), 0)
        tiled = jnp.concatenate([tiled] * 6, 1)
        total = fixed
        for term in split(jnp.where(match, tiled, 0.0), 3):
            total = total + dot(flat, term.astype(LOW), (1, 1))
        blocks[j] = jnp.concatenate(split(total, 2), 1).astype(LOW)
    for step in range(grid.cols):
        place = grid.place(step)
        outs[step][:, :own] = tokens[:, pl.ds(block_start(place, own), own)]
        outs[step][:, own : 2 * own] = cot[:, pl.ds(block_start(place, own), own)]
        outs[step][:, 2 * own :] = blocks[place // grid.rows]


def unbundle(grid, *rest):
    bundles, (grad_out, small_out) = rest[: grid.cols], rest[grid.cols :]
    own = grad_out.shape[1] // grid.cols
    small_out[...] = jnp.zeros(small_out.shape, FULL)
    for step in range(grid.cols):
        place = grid.place(step)
        grad_out[:, pl.ds(block_start(place, own), own)] = bundles[step][:, :own]
        terms = bundles[step][:, own:].astype(FULL)
        small_out[place // grid.rows] += (terms[:, :LANES] + terms[:, LANES:]).T


def join(grid, *rest):
    pieces, out = rest[: grid.cols], rest[-1]
    own = pieces[0].shape[1]
    for step in range(grid.cols):
        out[:, pl.ds(block_start(grid.place(step), own), own)] = pieces[step][...]


def pack(qkv, proj, attn_out):
    width = qkv.shape[2]
    for i in range(3):
        attn_out[:, i * width : (i + 1) * width] = qkv[i]
    attn_out[:, 3 * width :] = proj[...].T


def places(grid, slot_count, segs, segs_row, segs_col, segs_own, cosine, sine):
    own = segs_own.shape[1]
    base = grid.sequence() * grid.rows
    lane = lax.broadcasted_iota(jnp.int32, (1, own), 1)

    def segs_of(q):
        return segs[pl.ds(base + q, 1), :]

    starts = []
    for slot in range(slot_count):
        start = jnp.full((1, 1), SEQ, jnp.int32)
        for q in range(grid.rows):
            there = jnp.where(segs_of(q) == slot, lane + q * own, SEQ)
            start = jnp.minimum(start, jnp.min(there, axis=1, keepdims=True))
        starts.append(start)
    half = cosine.shape[0]
    step = lax.broadcasted_iota(jnp.int32, (half, own), 0).astype(FULL)
    inverse_freq = 1.0 / jnp.exp(step * (2.0 / HEAD_DIM) * jnp.log(FULL(10000.0)))
    for e in range(grid.rows):
        q = grid.row() ^ e
        span = slice(e * own, (e + 1) * own)
        row = segs_of(q)
        position = lane + q * own
        for slot in range(slot_count):
            position = position - jnp.where(row == slot, starts[slot], 0)
        angle = position.astype(FULL) * inverse_freq
        cosine[:, span] = jnp.cos(angle)
        sine[:, span] = jnp.sin(angle)
        segs_row[:, span] = row
        segs_col[span, :] = jnp.broadcast_to(row.astype(FULL), (8, own)).T[:, :1].astype(jnp.int32)
    segs_own[...] = segs_row[:, :own]


def first_norm(grid, segs, *rest):
    bundles, (input_out, stream_out, cot_out, mods_out) = rest[: grid.cols], rest[grid.cols :]
    size, own = bundles[0].shape[0], input_out.shape[1]
    for step in range(grid.cols):
        place = pl.ds(block_start(grid.source(step), size), size)
        stream_out[place, :] = bundles[step][:, :own]
        cot_out[place, :] = bundles[step][:, own : 2 * own]
        mods_out[place, :] = bundles[step][:, 2 * own :]
    stream = stream_out[...].astype(FULL)
    mods = mods_out[...]
    pick = token_mods_of(mods, segs[...])
    normed, _ = normalize(stream)
    scaled = normed * column_of(mods, GAIN_ONE)
    input_out[...] = (scaled * (1.0 + pick(1)) + pick(0)).astype(LOW)


def branch_grad(segs, mods, cot, branch_out):
    pick = token_mods_of(mods[...], segs[...])
    branch_out[...] = (cot[...].astype(FULL) * pick(5)).astype(LOW)


def attend(weight_all, cosine, sine, *rest):
    pieces, (segs_row, segs_col), outs = rest[:4], rest[4:6], rest[6:]
    parts, (query, key, value, mixed, logsum, key_rows) = outs[:3], outs[3:]
    own = pieces[0].shape[1]
    head_width = query.shape[0]
    weight, proj = weight_all[:, : 3 * head_width], weight_all[:, 3 * head_width :]
    half = HEAD_DIM // 2
    scale = HEAD_DIM ** (-0.5)
    for e in range(4):
        span = slice(e * own, (e + 1) * own)
        cos, sin = cosine[:, span], sine[:, span]
        found = dot(weight, pieces[e][...], (0, 0))
        for h in range(head_width // HEAD_DIM):
            for out, base, factor in ((query, 0, scale), (key, head_width, 1.0)):
                at = h * HEAD_DIM
                one = found[base + at : base + at + half]
                two = found[base + at + half : base + at + HEAD_DIM]
                out[at : at + half, span] = ((one * cos - two * sin) * factor).astype(LOW)
                out[at + half : at + HEAD_DIM, span] = ((two * cos + one * sin) * factor).astype(LOW)
        value[:, span] = found[2 * head_width :].astype(LOW)
    ship(query, key, value)
    key_segs = jnp.where(segs_col[...] == 0, -1, segs_col[...])
    for h in range(head_width // HEAD_DIM):
        rows = slice(h * HEAD_DIM, (h + 1) * HEAD_DIM)
        key_rows[h] = key[rows, :].astype(FULL).T.astype(LOW)
    for e in (3, 1, 2, 0):
        span = slice(e * own, (e + 1) * own)
        query_segs = segs_row[:, span]
        allowed = key_segs == query_segs
        padding = (query_segs == 0).astype(FULL)
        for h in range(head_width // HEAD_DIM):
            rows = slice(h * HEAD_DIM, (h + 1) * HEAD_DIM)
            scores = dot(key_rows[h], query[rows, span], (1, 0))
            scores = jnp.where(allowed, scores, MASK_FILL)
            largest = jnp.maximum(jnp.max(scores, axis=0, keepdims=True), MASK_FLOOR)
            exponent = jnp.exp(scores - largest)
            total = jnp.sum(exponent, axis=0, keepdims=True) + padding
            found = dot(value[rows, :], exponent.astype(LOW), (1, 0))
            mixed[rows, span] = (found / total).astype(LOW)
            logsum[h : h + 1, span] = largest + jnp.log(total)
        part_of(parts, e)[...] = dot(proj, mixed[:, span], (1, 0)).astype(LOW)
        ship_part(parts, e)


def second_norm(segs, mods, stream, part, near, far, input_out, middle_out, attn_out):
    pick = token_mods_of(mods[...], segs[...])
    attn = three_terms(part, near, far)
    attn_out[...] = attn.astype(LOW)
    middle = stream[...].astype(FULL) + pick(2) * attn
    middle_out[...] = middle
    normed, _ = normalize(middle)
    scaled = normed * column_of(mods, GAIN_TWO)
    input_out[...] = (scaled * (1.0 + pick(4)) + pick(3)).astype(LOW)


GELU_SCALE = 0.7978845608028654
GELU_CUBE = 0.044715


FEED_ORDER = (0, 1, 2, 3)


def feed_first(weights, up_bias, *rest):
    sides, outs = rest[:8], rest[8:]
    parts, results, hidden, pre_grad = outs[:3], outs[3:6], outs[6:10], outs[10:14]
    count = hidden[0].shape[0]
    up, down = weights[:, :count], weights[:, count:]
    bias = jnp.broadcast_to(up_bias[...].astype(FULL)[None], (8, count)).T[:, :1]
    for i, e in enumerate(FEED_ORDER):
        piece, branch = sides[2 * i], sides[2 * i + 1]
        pre = dot(up, piece[...], (0, 0)) + bias
        square = pre * pre
        curve = jnp.tanh(GELU_SCALE * (pre + GELU_CUBE * square * pre))
        hidden[e][...] = (0.5 * pre * (1.0 + curve)).astype(LOW)
        slope = 0.5 * (1.0 + curve) + 0.5 * pre * (1.0 - curve * curve) * (
            GELU_SCALE * (1.0 + 3.0 * GELU_CUBE * square)
        )
        grad = dot(down, branch[...], (0, 0))
        pre_grad[e][...] = (grad * slope).astype(LOW)
        ship(hidden[e], pre_grad[e])
        part_of(parts, e)[...] = dot(up, pre_grad[e][...], (1, 0)).astype(LOW)
        part_of(results, e)[...] = dot(down, hidden[e][...], (1, 0)).astype(LOW)
        if e == 3:
            ship(parts[2], results[2])
        elif e != 1:
            ship(parts[e // 2], results[e // 2])


def feed_grads_of(pre_grad, inputs_all, hidden, branch_all, grads):
    count = hidden.shape[0]
    blocks = grads.shape[0]
    size = inputs_all.shape[0] // blocks
    ones = jnp.ones((16, hidden.shape[1]), LOW)
    bias = dot(ones, pre_grad[...], (1, 1)).astype(LOW)
    for j in range(blocks):
        grads[j, size:, :count] = bias
        grads[j, size:, count:] = jnp.zeros_like(bias)
    up_total = dot(inputs_all[...], pre_grad[...], (1, 1)).astype(LOW)
    for j in range(blocks):
        grads[j, :size, :count] = up_total[j * size : (j + 1) * size]
    down_total = dot(branch_all[...], hidden[...], (1, 1)).astype(LOW)
    for j in range(blocks):
        grads[j, :size, count:] = down_total[j * size : (j + 1) * size]


def middle_grad(segs, mods, middle, cot, part, near, far, grad_out, attn_grad_out, input_grad_out):
    pick = token_mods_of(mods[...], segs[...])
    input_grad = three_terms(part, near, far)
    input_grad_out[...] = input_grad.astype(LOW)
    normed, inverse = normalize(middle[...])
    grad_scaled = input_grad * (1.0 + pick(4)) * column_of(mods, GAIN_TWO)
    grad = cot[...].astype(FULL) + normalize_back(grad_scaled, normed, inverse)
    grad_out[...] = grad
    attn_grad_out[...] = (grad * pick(2)).astype(LOW)


def doc_sums(values, chosen):
    terms = jnp.concatenate(split(values, 2), 1).astype(LOW)
    return dot(jnp.concatenate([chosen, chosen], 1), terms, (1, 1))


def slot_rows(segs):
    return (lax.broadcasted_iota(jnp.int32, (16, segs.shape[1]), 0) == segs).astype(LOW)


def finish_forward(grid, segs, mods, middle, cot, attn, grad_middle, input_grad, part, near, far, *rest):
    outs, (small, result_low) = rest[: grid.cols], rest[grid.cols :]
    pick = token_mods_of(mods[...], segs[...])
    chosen = slot_rows(segs[...])
    ones = jnp.ones(chosen.shape, LOW)
    valid = (segs[...] != 0).astype(FULL)
    mlp = (
        three_terms(part, near, far)
        + column_of(mods, DOWN_BIAS)
    )
    gate = pick(5)
    mlp_term = gate * mlp
    result = middle[...] + mlp_term
    result_low[...] = result.astype(LOW)
    size = outs[0].shape[0]
    for step in range(grid.cols):
        outs[step][...] = result_low[pl.ds(block_start(grid.source(step), size), size), :]
    small[...] = jnp.zeros(small.shape, FULL)
    cot_full = cot[...].astype(FULL)
    attn_all = attn[...].astype(FULL)
    input_all = input_grad[...].astype(FULL)
    normed, _ = normalize(middle[...])
    along = input_all * normed
    terms = (
        (2, grad_middle[...] * attn_all),
        (3, input_all),
        (4, along * column_of(mods, GAIN_TWO)),
        (5, cot_full * mlp),
    )
    for k, values in terms:
        small[k * SLOTS : (k + 1) * SLOTS, :] = doc_sums(values, chosen)[:SLOTS]
    small[GAIN_TWO : GAIN_TWO + 1, :] = doc_sums(along * (1.0 + pick(4)), ones)[:1]
    branch = (cot_full * gate).astype(LOW)
    small[DOWN_BIAS : DOWN_BIAS + 1, :] = dot(ones, branch, (1, 1))[:1]
    attn_term = pick(2) * attn_all
    squares = [
        jnp.sum(jnp.sum(v * v, axis=0, keepdims=True) * valid, axis=1, keepdims=True)
        for v in (result, attn_term, mlp_term)
    ]
    squares.append(jnp.sum(valid, axis=1, keepdims=True) * middle.shape[0])
    lane = lax.broadcasted_iota(jnp.int32, (1, small.shape[1]), 1)
    total = jnp.zeros(lane.shape, FULL)
    for i, value in enumerate(squares):
        total = jnp.where(lane == i, value, total)
    small[STATS : STATS + 1, :] = total


def attend_back(pieces_of, key, value, weight_all, first, query, mixed, logsum, segs_row, segs_col, cosine, sine, *rest):
    last = pieces_of[0] != 0
    if last:
        second, key_in, value_in, query_in, rest = rest[0], rest[1], rest[2], rest[3], rest[4:]
        parts, (grads, key_rows, value_rows, out_grad, key_grad, value_grad) = rest[:3], rest[3:]
    else:
        second, (grads, key_grad, value_grad, key_rows, value_rows, out_grad) = rest[0], rest[1:]
    pieces = dict(zip(pieces_of, (first, second)))
    own = first.shape[1]
    head_width = query.shape[0]
    heads = head_width // HEAD_DIM
    weight, proj = weight_all[:, : 3 * head_width], weight_all[:, 3 * head_width :]
    half = HEAD_DIM // 2
    scale = HEAD_DIM ** (-0.5)
    for h in range(heads):
        rows = slice(h * HEAD_DIM, (h + 1) * HEAD_DIM)
        key_rows[h] = key[rows, :].astype(FULL).T.astype(LOW)
        value_rows[h] = value[rows, :].astype(FULL).T.astype(LOW)
    key_segs = jnp.where(segs_col[...] == 0, -1, segs_col[...])
    if last:
        grads[:head_width, : 2 * own] = query_in[...]
        key_grad[...] = key_in[...]
        value_grad[...] = value_in[...]
    else:
        key_grad[...] = jnp.zeros(key_grad.shape, FULL)
        value_grad[...] = jnp.zeros(value_grad.shape, FULL)

    def turn_back(grad, span, base, at):
        cos, sin = cosine[:, span], sine[:, span]
        one, two = grad[:half], grad[half:]
        grads[base + at : base + at + half, span] = (one * cos + two * sin).astype(LOW)
        grads[base + at + half : base + at + HEAD_DIM, span] = (two * cos - one * sin).astype(LOW)

    for e in pieces_of:
        span = slice(e * own, (e + 1) * own)
        allowed = key_segs == segs_row[:, span]
        out_grad[...] = dot(proj, pieces[e][...], (0, 0)).astype(LOW)
        for h in range(heads):
            rows = slice(h * HEAD_DIM, (h + 1) * HEAD_DIM)
            back = out_grad[rows, :]
            inner = jnp.sum(
                back.astype(FULL) * mixed[rows, span].astype(FULL), axis=0, keepdims=True
            )
            scores = dot(key_rows[h], query[rows, span], (1, 0))
            scores = jnp.where(allowed, scores, MASK_FILL)
            probability = jnp.exp(scores - logsum[h : h + 1, span])
            grad_probs = dot(value_rows[h], back, (1, 0))
            score_grad = (probability * (grad_probs - inner)).astype(LOW)
            value_grad[rows, :] += dot(back, probability.astype(LOW), (1, 1))
            key_grad[rows, :] += dot(query[rows, span], score_grad, (1, 1))
            turn_back(dot(key[rows, :], score_grad, (1, 0)) * scale, span, 0, h * HEAD_DIM)
    if not last:
        return
    for e in (3, 1, 2, 0):
        span = slice(e * own, (e + 1) * own)
        for h in range(heads):
            turn_back(key_grad[h * HEAD_DIM : (h + 1) * HEAD_DIM, span], span, head_width, h * HEAD_DIM)
        grads[2 * head_width :, span] = value_grad[:, span].astype(LOW)
        part_of(parts, e)[...] = dot(weight, grads[:, span], (1, 0)).astype(LOW)
        ship_part(parts, e)


def attend_weights(grid, grads, mixed, inputs_all, pieces_all, keep, send, total):
    count = grads.shape[0]
    total[:, :count] = dot(inputs_all[...], grads[...], (1, 1)).astype(LOW)
    total[:, count:] = dot(pieces_all[...], mixed[...], (1, 1)).astype(LOW)
    size = keep.shape[1]
    for j in range(grid.cols):
        send[j] = total[pl.ds(grid.half_start(grid.col() ^ j, 1 - grid.half(), size), size), :]
    ship(send)
    for j in range(grid.cols):
        keep[j] = total[pl.ds(grid.half_start(grid.col() ^ j, grid.half(), size), size), :]


def pair_sum(keep, got, *outs):
    for j, out in enumerate(outs):
        out[...] = (keep[j].astype(FULL) + got[j].astype(FULL)).astype(LOW)


def block_sum(*rest):
    total = rest[0][...].astype(FULL)
    for piece in rest[1:-1]:
        total = total + piece[...].astype(FULL)
    rest[-1][...] = total.astype(LOW)


def attn_weight_out(grid, own, other, qkv_out, proj_out, total):
    size = own.shape[0]
    total[pl.ds(grid.half_start(0, grid.half(), size), size), :] = own[...]
    total[pl.ds(grid.half_start(0, 1 - grid.half(), size), size), :] = other[...]
    width = qkv_out.shape[2]
    for i in range(3):
        qkv_out[i] = total[:, i * width : (i + 1) * width].astype(FULL)
    proj_out[...] = total[:, 3 * width :].astype(FULL).T


def feed_weight_out(*rest):
    parts, (up_out, bias_out, down_out) = rest[:-3], rest[-3:]
    total = parts[0][...].astype(FULL)
    for part in parts[1:]:
        total = total + part[...].astype(FULL)
    size, count = up_out.shape
    up_out[...] = total[:size, :count]
    down_out[...] = total[:size, count:]
    bias_out[...] = total[size, :count]


def finish_backward(grid, segs, mods, stream, grad_middle, small_in, part, near, far, *rest):
    outs, (grad_low, blocks) = rest[: grid.cols], rest[grid.cols :]
    pick = token_mods_of(mods[...], segs[...])
    chosen = slot_rows(segs[...])
    ones = jnp.ones(chosen.shape, LOW)
    input_grad = three_terms(part, near, far)
    normed, inverse = normalize(stream[...].astype(FULL))
    gain = column_of(mods, GAIN_ONE)
    grown = input_grad * (1.0 + pick(1))
    grad = grad_middle[...] + normalize_back(grown * gain, normed, inverse)
    grad_low[...] = grad.astype(LOW)
    size = grad.shape[0] // grid.cols
    own = grad.shape[1]
    for step in range(grid.cols):
        place = pl.ds(block_start(grid.source(step), size), size)
        outs[step][:, :own] = grad_low[place, :]
    shift = doc_sums(input_grad, chosen)[:SLOTS]
    scale = doc_sums(input_grad * normed * gain, chosen)[:SLOTS]
    norm_gain = doc_sums(grown * normed, ones)[:1]
    for c in range(grid.cols):
        span = slice(c * size, (c + 1) * size)
        blocks[c, :, :size] = small_in[:, span]
        blocks[c, :SLOTS, :size] = shift[:, span]
        blocks[c, SLOTS : 2 * SLOTS, :size] = scale[:, span]
        blocks[c, GAIN_ONE : GAIN_ONE + 1, :size] = norm_gain[:, span]
        blocks[c, STATS : STATS + 1, :size] = small_in[STATS : STATS + 1, :size]
    for step in range(grid.cols):
        terms = split(blocks[grid.source(step)].T, 2)
        outs[step][:, own:] = jnp.concatenate(terms, 1).astype(LOW)


def modulation_back(grid, slot_count, dp_count, *rest):
    times, (table, weight), rest = rest[:dp_count], rest[dp_count : dp_count + 2], rest[dp_count + 2 :]
    pieces, outs = rest[: 2 * dp_count], rest[2 * dp_count :]
    weight_out, bias_out, gain_one_out, gain_two_out, down_bias_out, stats_out, embed_out = outs[:7]
    embed, grads = outs[7:]
    per = grid.per_row
    embed[...] = jnp.zeros(embed.shape, FULL)
    size = grads.shape[2]
    total = jnp.zeros((LANES - 6 * SLOTS, size), FULL)
    for d in range(dp_count):
        for far in range(2):
            piece = pieces[2 * d + far]
            for s in range(2 * per):
                sequence = (grid.row() ^ (2 * far + s // per)) * per + s % per
                first = block_start(d * per * grid.rows + sequence, SLOTS)
                for slot in range(slot_count):
                    time = times[d][sequence, slot]
                    embed[pl.ds(first + slot, 1), :] = table[pl.ds(time, 1), :]
                for k in range(6):
                    grads[k, pl.ds(first, SLOTS), :] = piece[s, k * SLOTS : (k + 1) * SLOTS, :]
                total = total + piece[s, 6 * SLOTS :, :]
    for k in range(6):
        rows = grads[k]
        weight_out[k] = dot(rows, embed[...], (0, 0), PRECISE)
        bias_out[k : k + 1, :] = jnp.sum(rows, axis=0, keepdims=True)
        part = dot(rows, weight[k].astype(FULL), (1, 0), PRECISE)
        embed_out[...] = part if k == 0 else embed_out[...] + part
    gain_one_out[...] = total[GAIN_ONE - 6 * SLOTS]
    gain_two_out[...] = total[GAIN_TWO - 6 * SLOTS]
    down_bias_out[...] = total[DOWN_BIAS - 6 * SLOTS]
    squares = total[STATS - 6 * SLOTS : STATS - 6 * SLOTS + 1, :]
    stats_out[...] = jnp.sqrt(squares / squares[:, 3:4])[0, :3]


def table_sum(grid, slot_count, dp_count, *rest):
    times, parts, (table_out, total) = rest[:dp_count], rest[dp_count:-2], rest[-2:]
    found = parts[0][...]
    for part in parts[1:]:
        found = found + part[...]
    total[...] = found
    table_out[...] = jnp.zeros(table_out.shape, FULL)
    for d in range(dp_count):
        for sequence in range(grid.cols):
            for slot in range(slot_count):
                time = times[d][sequence, slot]
                at = (d * grid.cols + sequence) * SLOTS + slot
                table_out[pl.ds(time, 1), :] += total[at : at + 1, :]


def per_device(
    tokens,
    cotangent,
    segment_ids,
    doc_times,
    time_table,
    attn_gain,
    mlp_gain,
    mod_weight,
    mod_bias,
    qkv_weight,
    proj_weight,
    up_weight,
    up_bias,
    down_weight,
    down_bias,
):
    grid = Grid()
    dp_count = lax.axis_size("dp")
    width_local = tokens.shape[0]
    width = width_local * grid.cols
    own = tokens.shape[1] // grid.cols
    head_width = qkv_weight.shape[2]
    hidden_local = up_weight.shape[1]
    slot_count = doc_times.shape[1]
    cond_width = mod_weight.shape[2]
    if segment_ids.shape[0] != grid.cols * SEQ or own * grid.rows != SEQ or grid.rows != 4:
        raise ValueError("sequence split")
    low_tile = shape((width, own), LOW)
    full_tile = shape((width, own), FULL)
    low_piece = shape((width_local, own), LOW)
    part_tiles = [low_tile, low_tile, shape((2 * width, own), LOW)]

    part_rows = width_local // dp_count
    part_start = lax.axis_index("dp") * part_rows

    def gather_weight(parts):
        parts = [lax.dynamic_slice_in_dim(p, part_start, part_rows, 0) for p in parts]
        part = jnp.concatenate(parts, 1) if len(parts) > 1 else parts[0]
        return lax.all_gather(part, ("col", "dp"), axis=0, tiled=True)

    bundles = run(
        functools.partial(prepare, grid, slot_count), "prepare",
        [shape((width_local, 2 * own + 2 * LANES), LOW)] * grid.cols,
        [doc_times, time_table, mod_weight, mod_bias, attn_gain, mlp_gain,
         down_bias, tokens, cotangent],
        [pltpu.VMEM((SLOTS, cond_width), FULL), pltpu.VMEM((LANES, width_local), FULL),
         pltpu.VMEM((grid.per_row, width_local, 2 * LANES), LOW)],
        smem=1,
    )
    attn_block = run(
        pack, "pack", [shape((width_local, 4 * head_width), LOW)],
        after(bundles[:1], [qkv_weight.transpose(1, 0, 2), proj_weight]),
    )
    attn_weights = gather_weight(attn_block)

    bundles = relayout(bundles)
    segs_row, segs_col, segs_own, cosine, sine = run(
        functools.partial(places, grid, slot_count), "places",
        [shape((1, SEQ), jnp.int32), shape((SEQ, 1), jnp.int32), shape((1, own), jnp.int32)]
        + [shape((HEAD_DIM // 2, SEQ), FULL)] * 2,
        [segment_ids.reshape(-1, own)],
    )
    input_one, stream, cot, mods = run(
        functools.partial(first_norm, grid), "first_norm",
        [low_tile] * 3 + [shape((width, 2 * LANES), LOW)], [segs_own] + bundles,
    )

    def branch_filler(ready):
        [late] = after([ready], [cot])
        return run(branch_grad, "branch_grad", [low_tile], [segs_own, mods, late])

    rows_one, [branch] = gather_rows(input_one, branch_filler)
    branch_rows = gather_rows(branch)
    times = [doc_times] + [swap(doc_times, "dp", d) for d in range(1, dp_count)]
    rows_one[3:] = after([branch_rows[1]] + times[1:], rows_one[3:])

    feed_weights = gather_weight(after(rows_one[2:3] + [attn_weights], [up_weight, down_weight]))
    *parts, query, key, value, mixed, logsum = run(
        attend, "attend",
        part_tiles + [shape((head_width, SEQ), LOW)] * 4 + [shape((8, SEQ), FULL)],
        [attn_weights, cosine, sine] + rows_one + [segs_row, segs_col],
        [pltpu.VMEM((head_width // HEAD_DIM, SEQ, HEAD_DIM), LOW)],
    )
    attn_terms = scatter_rows(parts)
    input_two, middle, attn = run(
        second_norm, "second_norm", [low_tile, full_tile, low_tile],
        [segs_own, mods, stream] + attn_terms,
    )
    rows_two = gather_rows(input_two)
    hidden_tile = shape((hidden_local, own), LOW)
    sides = [side for e in FEED_ORDER for side in (rows_two[e], branch_rows[e])]
    found = run(
        feed_first, "feed_first", part_tiles * 2 + [hidden_tile] * 8, [feed_weights, up_bias] + sides
    )
    parts, results, hidden, pre_grad = found[:3], found[3:6], found[6:10], found[10:]

    def grads_filler(ready):
        late = after([ready], pre_grad)
        return run(
            feed_grads_of, "feed_grads",
            [shape((grid.cols, width_local + 16, 2 * hidden_local), LOW)],
            [Joined(late), Joined(rows_two), Joined(hidden), Joined(branch_rows)],
        )

    input_terms, [feed_grads] = scatter_rows(parts, grads_filler, True)
    feed_grads = lax.psum_scatter(
        feed_grads.reshape(-1, 2 * hidden_local), "col", scatter_dimension=0, tiled=True
    )
    grad_middle, grad_attn, input_grad = run(
        middle_grad, "middle_grad", [full_tile, low_tile, low_tile],
        [segs_own, mods, middle, cot] + input_terms,
    )

    mlp_near, mlp_total = scatter_near(results)
    head_tile = shape((head_width, SEQ), FULL)
    back_scratch = [pltpu.VMEM((head_width // HEAD_DIM, SEQ, HEAD_DIM), LOW)] * 2 + [
        pltpu.VMEM((head_width, own), LOW)
    ]
    saved = [query, mixed, logsum, segs_row, segs_col, cosine, sine]

    def first_filler(ready):
        return run(
            functools.partial(attend_back, (0, 1)), "attend_back_first",
            [shape((head_width, 2 * own), LOW), head_tile, head_tile],
            [key, value, attn_weights, grad_attn] + saved + [ready], back_scratch,
        )

    attn_rows, (query_grad, key_grad, value_grad) = gather_rows(grad_attn, first_filler)
    [mlp_total] = after(attn_rows[2:3], [mlp_total])
    mlp_terms = [results[0], mlp_near, swap(mlp_total, "row", 2)]
    *parts, qkv_grads = run(
        functools.partial(attend_back, (2, 3)), "attend_back_last",
        part_tiles + [shape((3 * head_width, SEQ), LOW)],
        [key, value, attn_weights, attn_rows[2]] + saved
        + [attn_rows[3], key_grad, value_grad, query_grad],
        back_scratch + [pltpu.VMEM((head_width, SEQ), FULL)] * 2,
    )

    def back_filler(ready):
        [late] = after([ready], [qkv_grads])
        blocks = run(
            functools.partial(attend_weights, grid), "attend_weights",
            [shape((grid.cols, width_local // 2, 4 * head_width), LOW)] * 2,
            [late, mixed, Joined(rows_one), Joined(attn_rows)], [pltpu.VMEM((width, 4 * head_width), LOW)],
        )
        [first] = after(blocks[:1], mlp_terms[:1])
        found = run(
            functools.partial(finish_forward, grid), "finish_forward",
            [low_piece] * grid.cols + [shape((LANES, width), FULL)],
            [segs_own, mods, middle, cot, attn, grad_middle, input_grad, first] + mlp_terms[1:],
            [pltpu.VMEM((width, own), LOW)],
        )
        return found + blocks

    parts[2:] = after(mlp_terms[2:], parts[2:])
    back_terms, found = scatter_rows(parts, back_filler, True)
    result_chunks, small, attn_grads = found[: grid.cols], found[grid.cols], found[grid.cols + 1 :]
    bundles = run(
        functools.partial(finish_backward, grid), "finish_backward",
        [shape((width_local, own + 2 * LANES), LOW)] * grid.cols,
        [segs_own, mods, stream, grad_middle, small] + back_terms,
        [pltpu.VMEM((width, own), LOW), pltpu.VMEM((grid.cols, LANES, width_local), FULL)],
    )
    out_tile = shape((width_local, grid.cols * own), LOW)
    bundles = relayout(bundles, back=True)
    tokens_grad, small = run(
        functools.partial(unbundle, grid), "unbundle",
        [out_tile, shape((grid.per_row, LANES, width_local), FULL)], bundles,
    )
    [block_output] = run(
        functools.partial(join, grid), "join", [out_tile],
        relayout(after(bundles, result_chunks), back=True),
    )

    small = jnp.concatenate([small, swap(small, "row", 1)], 0)
    pieces = []
    for d in range(dp_count):
        for far in range(2):
            count = dp_count * grid.rows
            pairs = [(i, i ^ (d * grid.rows + 2 * far)) for i in range(count)]
            pieces.append(lax.ppermute(small, ("dp", "row"), pairs) if d or far else small)
    seq_total = grid.cols * dp_count
    vector = shape((width_local,), FULL)
    embed_tile = shape((seq_total * SLOTS, cond_width), FULL)
    weight_out, bias_out, gain_one_out, gain_two_out, down_bias_out, stats, embed = run(
        functools.partial(modulation_back, grid, slot_count, dp_count), "modulation_back",
        [
            shape((6, width_local, cond_width), FULL), shape((6, width_local), FULL),
            vector, vector, vector, shape((3,), FULL), embed_tile,
        ],
        times + [time_table, mod_weight] + pieces,
        [pltpu.VMEM((seq_total * SLOTS, cond_width), FULL),
         pltpu.VMEM((6, seq_total * SLOTS, width_local), FULL)],
        smem=dp_count,
    )
    [table_out] = run(
        functools.partial(table_sum, grid, slot_count, dp_count), "table_sum",
        [shape(time_table.shape, FULL)],
        times + [embed] + [swap(embed, "col", j) for j in range(1, grid.cols)],
        [pltpu.VMEM((seq_total * SLOTS, cond_width), FULL)], smem=dp_count,
    )

    def all_dp(part):
        return [part] + [swap(part, "dp", d) for d in range(1, dp_count)]

    half_tile = shape((width_local // 2, 4 * head_width), LOW)
    pieces = run(pair_sum, "pair_sum", [half_tile] * grid.cols, [attn_grads[0], swap(attn_grads[1], "dp", 1)])
    pieces = pieces[:1] + [swap(pieces[j], "col", j) for j in range(1, grid.cols)]
    [attn_half] = run(block_sum, "block_sum", [half_tile], pieces)
    bit = 2
    while bit < dp_count:
        attn_half = (attn_half.astype(FULL) + swap(attn_half, "dp", bit).astype(FULL)).astype(LOW)
        bit *= 2
    up_out, up_bias_out, down_out = run(
        feed_weight_out, "feed_weight_out",
        [shape(up_weight.shape, FULL), shape(up_bias.shape, FULL), shape(down_weight.shape, FULL)],
        all_dp(after(bundles, [feed_grads])[0]),
    )
    qkv_out, proj_out = run(
        functools.partial(attn_weight_out, grid), "attn_weight_out",
        [shape((3, width_local, head_width), FULL), shape(proj_weight.shape, FULL)],
        [attn_half, swap(attn_half, "dp", 1)], [pltpu.VMEM((width_local, 4 * head_width), LOW)],
    )
    return (
        block_output,
        tokens_grad,
        table_out,
        gain_one_out,
        gain_two_out,
        weight_out,
        bias_out,
        qkv_out.transpose(1, 0, 2),
        proj_out,
        up_out,
        up_bias_out,
        down_out,
        down_bias_out,
        stats,
    )


def solution(mesh):
    return jax.shard_map(
        per_device,
        mesh=mesh,
        in_specs=(
            P("col", ("dp", "row")),
            P("col", ("dp", "row")),
            P("dp"),
            P("dp", None),
            P(),
            P("col"),
            P("col"),
            P(None, "col", None),
            P(None, "col"),
            P("col", None, "row"),
            P("row", "col"),
            P("col", "row"),
            P("row"),
            P("col", "row"),
            P("col"),
        ),
        out_specs=(
            P("col", ("dp", "row")),
            P("col", ("dp", "row")),
            P(),
            P("col"),
            P("col"),
            P(None, "col", None),
            P(None, "col"),
            P("col", None, "row"),
            P("row", "col"),
            P("col", "row"),
            P("row"),
            P("col", "row"),
            P("col"),
            P(),
        ),
        check_vma=False,
    )
```

```python
import functools

import jax
import jax.numpy as jnp
from jax import lax
from jax.experimental import pallas as pl
from jax.experimental.pallas import tpu as pltpu
from jax.sharding import PartitionSpec as P

HEAD_DIM = 64
SEQ = 1024

PRECISE = lax.Precision.HIGHEST
EPSILON = 1e-05
MASK_FILL = -1e30
MASK_FLOOR = -1e29
LOW = jnp.bfloat16
FULL = jnp.float32
SLOTS = 8
LANES = 64
GAIN_ONE, GAIN_TWO, DOWN_BIAS = 48, 49, 50
STATS = 51
VMEM_LIMIT = 56 * 1024 * 1024
NEAR = {'unbundle': 12, 'modulation_back': 12, 'table_sum': 12, 'attn_weight_out': 12, 'feed_weight_out': 12, 'pair_sum': 12, 'block_sum': 12, 'join': 12, 'finish_forward': 12, 'finish_backward': 12, 'feed_first': 56, 'attend_back_first': 56, 'attend_back_last': 56, 'second_norm': 20, 'middle_grad': 20, 'branch_grad': 12, 'first_norm': 12, 'attend': 44}


def swap(values, axis, bit):
    count = lax.axis_size(axis)
    return lax.ppermute(values, axis, [(i, i ^ bit) for i in range(count)])


def gather_rows(values, filler=None, deps=()):
    far = swap(values, "row", 2)
    near = swap(values, "row", 1)
    filled = None
    if filler is not None:
        filled = filler(near)
        deps = list(deps) + list(filled[:1])
    if deps:
        [far] = after(deps, [far])
    last = swap(far, "row", 1)
    pieces = [values, near, far, last]
    return pieces if filler is None else (pieces, after([last], filled))


def scatter_rows(parts, filler=None, hold=False):
    width = parts[0].shape[0]
    near = swap(parts[2], "row", 1)
    total = (parts[1].astype(FULL) + near[width:].astype(FULL)).astype(LOW)
    far = swap(total, "row", 2)
    if filler is None:
        return [parts[0], near, far]
    filled = filler(total)
    [far] = after(filled[:1], [far])
    return [parts[0], near, far], after([far], filled) if hold else filled


def scatter_near(parts):
    near = swap(parts[2], "row", 1)
    total = (parts[1].astype(FULL) + near[parts[0].shape[0] :].astype(FULL)).astype(LOW)
    return near, total


def col_of_row(row_count):
    if row_count == 4:
        return [0, 2, 1, 3]
    return list(range(row_count))


def relayout_pairs(step):
    row_count = lax.axis_size("row")
    col_count = lax.axis_size("col")
    per_row = col_count // row_count
    table = col_of_row(row_count)
    pairs = []
    for r in range(row_count):
        for c in range(col_count):
            j, q = divmod((c + step) % col_count, row_count)
            pairs.append((r * col_count + c, q * col_count + table[r] * per_row + j))
    return pairs


def relayout(pieces, back=False):
    got = []
    for step, piece in enumerate(pieces):
        pairs = relayout_pairs(step)
        if back:
            pairs = [(b, a) for a, b in pairs]
        got.append(lax.ppermute(piece, ("row", "col"), pairs))
    return got


def after(deps, values):
    return lax.optimization_barrier((list(values), list(deps)))[0]


class Grid:
    def __init__(self):
        self.rows = lax.axis_size("row")
        self.cols = lax.axis_size("col")
        self.per_row = self.cols // self.rows
        table = col_of_row(self.rows)
        self.seq_of_col = [0] * self.cols
        for r in range(self.rows):
            for j in range(self.per_row):
                self.seq_of_col[table[r] * self.per_row + j] = r * self.per_row + j

    def row(self):
        return lax.axis_index("row")

    def col(self):
        return lax.axis_index("col")

    def sequence(self):
        return sum(jnp.where(self.col() == c, s, 0) for c, s in enumerate(self.seq_of_col))

    def half(self):
        return lax.axis_index("dp") % 2

    def half_start(self, block, which, size):
        return pl.multiple_of((2 * block + which) * size, size)

    def source(self, step):
        mine = self.col() % self.per_row * self.rows + self.row()
        return (mine + self.cols - step) % self.cols

    def place(self, step):
        return (self.col() + step) % self.cols


def whole(memory_space=pltpu.VMEM):
    return pl.BlockSpec(memory_space=memory_space)


class Joined:
    def __init__(self, values):
        self.values = values


class FarIn:
    def __init__(self, sources, buffer, sems):
        self.buffer, self.waiting = buffer, True
        if len(sources) == 1:
            places = [buffer]
        else:
            count = sources[0].shape[1]
            places = [buffer.at[:, i * count : (i + 1) * count] for i in range(len(sources))]
        self.copies = [
            pltpu.make_async_copy(source, place, sem)
            for source, place, sem in zip(sources, places, sems)
        ]
        for copy in self.copies:
            copy.start()

    @property
    def shape(self):
        return self.buffer.shape

    @property
    def ref(self):
        if self.waiting:
            for copy in self.copies:
                copy.wait()
            self.waiting = False
        return self.buffer

    @property
    def at(self):
        return self.ref.at

    def __getitem__(self, index):
        return self.ref[index]


class FarOut:
    def __init__(self, buffer, target, sem):
        self.copy = pltpu.make_async_copy(buffer, target, sem)
        self.ref, self.shipped = buffer, False

    @property
    def shape(self):
        return self.ref.shape

    @property
    def at(self):
        return self.ref.at

    def __getitem__(self, index):
        return self.ref[index]

    def __setitem__(self, index, value):
        self.ref[index] = value

    def ship(self):
        if not self.shipped:
            self.copy.start()
            self.shipped = True


def ship(*refs):
    for ref in refs:
        if isinstance(ref, FarOut):
            ref.ship()


def run(body, name, outs, args, scratch=(), smem=0, flops=0):
    if name in NEAR:
        moved = sum(a.size * a.dtype.itemsize for a in list(args) + list(outs))
        found = pl.pallas_call(
            body,
            out_shape=list(outs),
            in_specs=[whole(pltpu.SMEM)] * smem + [whole() for _ in args[smem:]],
            out_specs=[whole() for _ in outs],
            scratch_shapes=list(scratch),
            compiler_params=pltpu.CompilerParams(vmem_limit_bytes=NEAR[name] * 1024 * 1024),
            cost_estimate=pl.CostEstimate(flops=flops, bytes_accessed=moved, transcendentals=0),
            name=name,
        )(*args)
        return list(found)
    groups = [a.values if isinstance(a, Joined) else [a] for a in args[smem:]]
    flat = [a for group in groups for a in group]
    outs = list(outs)
    buffers = [
        pltpu.VMEM((*group[0].shape[:-1], sum(a.shape[-1] for a in group)), group[0].dtype)
        for group in groups
    ] + [pltpu.VMEM(o.shape, o.dtype) for o in outs]
    moved = sum(a.size * a.dtype.itemsize for a in flat + outs)

    def kernel(*refs):
        scalars, rest = list(refs[:smem]), list(refs[smem:])
        sources, rest = rest[: len(flat)], rest[len(flat) :]
        targets, rest = rest[: len(outs)], rest[len(outs) :]
        own, rest = rest[: len(scratch)], rest[len(scratch) :]
        spaces, sems = rest[:-1], rest[-1]
        ins, count = [], 0
        for group, space in zip(groups, spaces):
            span = range(count, count + len(group))
            ins.append(FarIn([sources[i] for i in span], space, [sems.at[i] for i in span]))
            count += len(group)
        results = [
            FarOut(space, target, sems.at[count + i])
            for i, (space, target) in enumerate(zip(spaces[len(groups) :], targets))
        ]
        body(*scalars, *ins, *results, *own)
        ship(*results)
        for ref in ins:
            ref.ref
        for ref in results:
            ref.copy.wait()

    found = pl.pallas_call(
        kernel,
        out_shape=outs,
        in_specs=[whole(pltpu.SMEM)] * smem + [whole(pl.ANY) for _ in flat],
        out_specs=[whole(pl.ANY) for _ in outs],
        scratch_shapes=list(scratch) + buffers
        + [pltpu.SemaphoreType.DMA((len(flat) + len(outs),))],
        compiler_params=pltpu.CompilerParams(vmem_limit_bytes=VMEM_LIMIT),
        cost_estimate=pl.CostEstimate(flops=flops, bytes_accessed=moved, transcendentals=0),
        name=name,
    )(*args[:smem], *flat)
    return list(found)


def shape(dims, dtype):
    return jax.ShapeDtypeStruct(dims, dtype)


def dot(left, right, dims, precision=None):
    return lax.dot_general(
        left, right, (((dims[0],), (dims[1],)), ((), ())),
        preferred_element_type=FULL, precision=precision,
    )


def split(values, terms):
    found = []
    for _ in range(terms):
        term = values.astype(LOW).astype(FULL)
        found.append(term)
        values = values - term
    return found


def block_start(index, size):
    return pl.multiple_of(index * size, size)


def token_mods_of(mods, segs):
    rows = lax.broadcasted_iota(jnp.int32, (2 * LANES, segs.shape[1]), 0) % LANES

    def pick(k):
        chosen = (rows == segs + k * SLOTS).astype(LOW)
        return dot(mods, chosen, (1, 0))

    return pick


def part_of(parts, e):
    if e % 2 == 0:
        return parts[e // 2]
    width = parts[0].shape[0]
    return parts[2].at[(e // 2) * width : (e // 2 + 1) * width]


def ship_part(parts, e):
    if e != 3:
        ship({1: parts[2], 2: parts[1], 0: parts[0]}[e])


def three_terms(part, near, far):
    return (
        part[...].astype(FULL) + near[: part.shape[0], :].astype(FULL) + far[...].astype(FULL)
    )


def column_of(mods, lane):
    return mods[:, lane : lane + 1].astype(FULL) + mods[:, LANES + lane : LANES + lane + 1].astype(FULL)


def normalize(stream):
    count = 1.0 / stream.shape[0]
    center = jnp.sum(stream, axis=0, keepdims=True) * count
    offset = stream - center
    inverse = lax.rsqrt(jnp.sum(offset * offset, axis=0, keepdims=True) * count + EPSILON)
    return offset * inverse, inverse


def normalize_back(grad_normed, normed, inverse):
    count = 1.0 / normed.shape[0]
    center = jnp.sum(grad_normed, axis=0, keepdims=True) * count
    along = jnp.sum(grad_normed * normed, axis=0, keepdims=True) * count
    return inverse * (grad_normed - center - normed * along)


def prepare(grid, slot_count, times, table, weight, bias, gain_one, gain_two, down_bias, tokens, cot, *rest):
    outs, (embed, rows, blocks) = rest[: grid.cols], rest[grid.cols :]
    own = (outs[0].shape[1] - 2 * LANES) // 2
    rows[...] = jnp.zeros(rows.shape, FULL)
    for k in range(6):
        rows[k * SLOTS : (k + 1) * SLOTS, :] = jnp.broadcast_to(
            bias[k : k + 1, :].astype(FULL), (SLOTS, rows.shape[1])
        )
    rows[GAIN_ONE : GAIN_ONE + 1, :] = gain_one[...].astype(FULL)[None]
    rows[GAIN_TWO : GAIN_TWO + 1, :] = gain_two[...].astype(FULL)[None]
    rows[DOWN_BIAS : DOWN_BIAS + 1, :] = down_bias[...].astype(FULL)[None]
    fixed = rows[...].T
    cond = weight.shape[2]
    flat = jnp.concatenate([weight[k] for k in range(6)], 1)
    row = lax.broadcasted_iota(jnp.int32, (LANES, 6 * cond), 0)
    lane = lax.broadcasted_iota(jnp.int32, (LANES, 6 * cond), 1)
    match = row // SLOTS == lane // cond
    for j in range(grid.per_row):
        embed[...] = jnp.zeros(embed.shape, FULL)
        for slot in range(slot_count):
            time = times[grid.row() * grid.per_row + j, slot]
            embed[slot : slot + 1, :] = table[pl.ds(time, 1), :]
        tiled = jnp.concatenate([embed[...]] * (LANES // SLOTS), 0)
        tiled = jnp.concatenate([tiled] * 6, 1)
        total = fixed
        for term in split(jnp.where(match, tiled, 0.0), 3):
            total = total + dot(flat, term.astype(LOW), (1, 1))
        blocks[j] = jnp.concatenate(split(total, 2), 1).astype(LOW)
    for step in range(grid.cols):
        place = grid.place(step)
        outs[step][:, :own] = tokens[:, pl.ds(block_start(place, own), own)]
        outs[step][:, own : 2 * own] = cot[:, pl.ds(block_start(place, own), own)]
        outs[step][:, 2 * own :] = blocks[place // grid.rows]


def unbundle(grid, *rest):
    bundles, (grad_out, small_out) = rest[: grid.cols], rest[grid.cols :]
    own = grad_out.shape[1] // grid.cols
    small_out[...] = jnp.zeros(small_out.shape, FULL)
    for step in range(grid.cols):
        place = grid.place(step)
        grad_out[:, pl.ds(block_start(place, own), own)] = bundles[step][:, :own]
        terms = bundles[step][:, own:].astype(FULL)
        small_out[place // grid.rows] += (terms[:, :LANES] + terms[:, LANES:]).T


def join(grid, *rest):
    pieces, out = rest[: grid.cols], rest[-1]
    own = pieces[0].shape[1]
    for step in range(grid.cols):
        out[:, pl.ds(block_start(grid.place(step), own), own)] = pieces[step][...]


def pack(qkv, proj, attn_out):
    width = qkv.shape[2]
    for i in range(3):
        attn_out[:, i * width : (i + 1) * width] = qkv[i]
    attn_out[:, 3 * width :] = proj[...].T


def places(grid, slot_count, segs, segs_row, segs_col, segs_own, cosine, sine):
    own = segs_own.shape[1]
    base = grid.sequence() * grid.rows
    lane = lax.broadcasted_iota(jnp.int32, (1, own), 1)

    def segs_of(q):
        return segs[pl.ds(base + q, 1), :]

    starts = []
    for slot in range(slot_count):
        start = jnp.full((1, 1), SEQ, jnp.int32)
        for q in range(grid.rows):
            there = jnp.where(segs_of(q) == slot, lane + q * own, SEQ)
            start = jnp.minimum(start, jnp.min(there, axis=1, keepdims=True))
        starts.append(start)
    half = cosine.shape[0]
    step = lax.broadcasted_iota(jnp.int32, (half, own), 0).astype(FULL)
    inverse_freq = 1.0 / jnp.exp(step * (2.0 / HEAD_DIM) * jnp.log(FULL(10000.0)))
    for e in range(grid.rows):
        q = grid.row() ^ e
        span = slice(e * own, (e + 1) * own)
        row = segs_of(q)
        position = lane + q * own
        for slot in range(slot_count):
            position = position - jnp.where(row == slot, starts[slot], 0)
        angle = position.astype(FULL) * inverse_freq
        cosine[:, span] = jnp.cos(angle)
        sine[:, span] = jnp.sin(angle)
        segs_row[:, span] = row
        segs_col[span, :] = jnp.broadcast_to(row.astype(FULL), (8, own)).T[:, :1].astype(jnp.int32)
    segs_own[...] = segs_row[:, :own]


def first_norm(grid, segs, *rest):
    bundles, (input_out, stream_out, cot_out, mods_out) = rest[: grid.cols], rest[grid.cols :]
    size, own = bundles[0].shape[0], input_out.shape[1]
    for step in range(grid.cols):
        place = pl.ds(block_start(grid.source(step), size), size)
        stream_out[place, :] = bundles[step][:, :own]
        cot_out[place, :] = bundles[step][:, own : 2 * own]
        mods_out[place, :] = bundles[step][:, 2 * own :]
    stream = stream_out[...].astype(FULL)
    mods = mods_out[...]
    pick = token_mods_of(mods, segs[...])
    normed, _ = normalize(stream)
    scaled = normed * column_of(mods, GAIN_ONE)
    input_out[...] = (scaled * (1.0 + pick(1)) + pick(0)).astype(LOW)


def branch_grad(segs, mods, cot, branch_out):
    pick = token_mods_of(mods[...], segs[...])
    branch_out[...] = (cot[...].astype(FULL) * pick(5)).astype(LOW)


def attend(weight_all, cosine, sine, *rest):
    pieces, (segs_row, segs_col), outs = rest[:4], rest[4:6], rest[6:]
    parts, (query, key, value, mixed, logsum, key_rows) = outs[:3], outs[3:]
    own = pieces[0].shape[1]
    head_width = query.shape[0]
    weight, proj = weight_all[:, : 3 * head_width], weight_all[:, 3 * head_width :]
    half = HEAD_DIM // 2
    scale = HEAD_DIM ** (-0.5)
    for e in range(4):
        span = slice(e * own, (e + 1) * own)
        cos, sin = cosine[:, span], sine[:, span]
        found = dot(weight, pieces[e][...], (0, 0))
        for h in range(head_width // HEAD_DIM):
            for out, base, factor in ((query, 0, scale), (key, head_width, 1.0)):
                at = h * HEAD_DIM
                one = found[base + at : base + at + half]
                two = found[base + at + half : base + at + HEAD_DIM]
                out[at : at + half, span] = ((one * cos - two * sin) * factor).astype(LOW)
                out[at + half : at + HEAD_DIM, span] = ((two * cos + one * sin) * factor).astype(LOW)
        value[:, span] = found[2 * head_width :].astype(LOW)
    ship(query, key, value)
    key_segs = jnp.where(segs_col[...] == 0, -1, segs_col[...])
    for h in range(head_width // HEAD_DIM):
        rows = slice(h * HEAD_DIM, (h + 1) * HEAD_DIM)
        key_rows[h] = key[rows, :].astype(FULL).T.astype(LOW)
    for e in (3, 1, 2, 0):
        span = slice(e * own, (e + 1) * own)
        query_segs = segs_row[:, span]
        allowed = key_segs == query_segs
        padding = (query_segs == 0).astype(FULL)
        for h in range(head_width // HEAD_DIM):
            rows = slice(h * HEAD_DIM, (h + 1) * HEAD_DIM)
            scores = dot(key_rows[h], query[rows, span], (1, 0))
            scores = jnp.where(allowed, scores, MASK_FILL)
            largest = jnp.maximum(jnp.max(scores, axis=0, keepdims=True), MASK_FLOOR)
            exponent = jnp.exp(scores - largest)
            total = jnp.sum(exponent, axis=0, keepdims=True) + padding
            found = dot(value[rows, :], exponent.astype(LOW), (1, 0))
            mixed[rows, span] = (found / total).astype(LOW)
            logsum[h : h + 1, span] = largest + jnp.log(total)
        part_of(parts, e)[...] = dot(proj, mixed[:, span], (1, 0)).astype(LOW)
        ship_part(parts, e)


def second_norm(segs, mods, stream, part, near, far, input_out, middle_out, attn_out):
    pick = token_mods_of(mods[...], segs[...])
    attn = three_terms(part, near, far)
    attn_out[...] = attn.astype(LOW)
    middle = stream[...].astype(FULL) + pick(2) * attn
    middle_out[...] = middle
    normed, _ = normalize(middle)
    scaled = normed * column_of(mods, GAIN_TWO)
    input_out[...] = (scaled * (1.0 + pick(4)) + pick(3)).astype(LOW)


GELU_SCALE = 0.7978845608028654
GELU_CUBE = 0.044715


FEED_ORDER = (0, 1, 2, 3)


def feed_first(weights, up_bias, *rest):
    sides, outs = rest[:8], rest[8:]
    parts, results, hidden, pre_grad = outs[:3], outs[3:6], outs[6:10], outs[10:14]
    count = hidden[0].shape[0]
    up, down = weights[:, :count], weights[:, count:]
    bias = jnp.broadcast_to(up_bias[...].astype(FULL)[None], (8, count)).T[:, :1]
    for i, e in enumerate(FEED_ORDER):
        piece, branch = sides[2 * i], sides[2 * i + 1]
        pre = dot(up, piece[...], (0, 0)) + bias
        square = pre * pre
        curve = jnp.tanh(GELU_SCALE * (pre + GELU_CUBE * square * pre))
        hidden[e][...] = (0.5 * pre * (1.0 + curve)).astype(LOW)
        slope = 0.5 * (1.0 + curve) + 0.5 * pre * (1.0 - curve * curve) * (
            GELU_SCALE * (1.0 + 3.0 * GELU_CUBE * square)
        )
        grad = dot(down, branch[...], (0, 0))
        pre_grad[e][...] = (grad * slope).astype(LOW)
        ship(hidden[e], pre_grad[e])
        part_of(parts, e)[...] = dot(up, pre_grad[e][...], (1, 0)).astype(LOW)
        part_of(results, e)[...] = dot(down, hidden[e][...], (1, 0)).astype(LOW)
        if e == 3:
            ship(parts[2], results[2])
        elif e != 1:
            ship(parts[e // 2], results[e // 2])


def feed_grads_of(pre_grad, inputs_all, hidden, branch_all, grads):
    count = hidden.shape[0]
    blocks = grads.shape[0]
    size = inputs_all.shape[0] // blocks
    ones = jnp.ones((16, hidden.shape[1]), LOW)
    bias = dot(ones, pre_grad[...], (1, 1)).astype(LOW)
    for j in range(blocks):
        grads[j, size:, :count] = bias
        grads[j, size:, count:] = jnp.zeros_like(bias)
    up_total = dot(inputs_all[...], pre_grad[...], (1, 1)).astype(LOW)
    for j in range(blocks):
        grads[j, :size, :count] = up_total[j * size : (j + 1) * size]
    down_total = dot(branch_all[...], hidden[...], (1, 1)).astype(LOW)
    for j in range(blocks):
        grads[j, :size, count:] = down_total[j * size : (j + 1) * size]


def middle_grad(segs, mods, middle, cot, part, near, far, grad_out, attn_grad_out, input_grad_out):
    pick = token_mods_of(mods[...], segs[...])
    input_grad = three_terms(part, near, far)
    input_grad_out[...] = input_grad.astype(LOW)
    normed, inverse = normalize(middle[...])
    grad_scaled = input_grad * (1.0 + pick(4)) * column_of(mods, GAIN_TWO)
    grad = cot[...].astype(FULL) + normalize_back(grad_scaled, normed, inverse)
    grad_out[...] = grad
    attn_grad_out[...] = (grad * pick(2)).astype(LOW)


def doc_sums(values, chosen):
    terms = jnp.concatenate(split(values, 2), 1).astype(LOW)
    return dot(jnp.concatenate([chosen, chosen], 1), terms, (1, 1))


def slot_rows(segs):
    return (lax.broadcasted_iota(jnp.int32, (16, segs.shape[1]), 0) == segs).astype(LOW)


def finish_forward(grid, segs, mods, middle, cot, attn, grad_middle, input_grad, part, near, far, *rest):
    outs, (small, result_low) = rest[: grid.cols], rest[grid.cols :]
    pick = token_mods_of(mods[...], segs[...])
    chosen = slot_rows(segs[...])
    ones = jnp.ones(chosen.shape, LOW)
    valid = (segs[...] != 0).astype(FULL)
    mlp = (
        three_terms(part, near, far)
        + column_of(mods, DOWN_BIAS)
    )
    gate = pick(5)
    mlp_term = gate * mlp
    result = middle[...] + mlp_term
    result_low[...] = result.astype(LOW)
    size = outs[0].shape[0]
    for step in range(grid.cols):
        outs[step][...] = result_low[pl.ds(block_start(grid.source(step), size), size), :]
    small[...] = jnp.zeros(small.shape, FULL)
    cot_full = cot[...].astype(FULL)
    attn_all = attn[...].astype(FULL)
    input_all = input_grad[...].astype(FULL)
    normed, _ = normalize(middle[...])
    along = input_all * normed
    terms = (
        (2, grad_middle[...] * attn_all),
        (3, input_all),
        (4, along * column_of(mods, GAIN_TWO)),
        (5, cot_full * mlp),
    )
    for k, values in terms:
        small[k * SLOTS : (k + 1) * SLOTS, :] = doc_sums(values, chosen)[:SLOTS]
    small[GAIN_TWO : GAIN_TWO + 1, :] = doc_sums(along * (1.0 + pick(4)), ones)[:1]
    branch = (cot_full * gate).astype(LOW)
    small[DOWN_BIAS : DOWN_BIAS + 1, :] = dot(ones, branch, (1, 1))[:1]
    attn_term = pick(2) * attn_all
    squares = [
        jnp.sum(jnp.sum(v * v, axis=0, keepdims=True) * valid, axis=1, keepdims=True)
        for v in (result, attn_term, mlp_term)
    ]
    squares.append(jnp.sum(valid, axis=1, keepdims=True) * middle.shape[0])
    lane = lax.broadcasted_iota(jnp.int32, (1, small.shape[1]), 1)
    total = jnp.zeros(lane.shape, FULL)
    for i, value in enumerate(squares):
        total = jnp.where(lane == i, value, total)
    small[STATS : STATS + 1, :] = total


def attend_back(pieces_of, key, value, weight_all, first, query, mixed, logsum, segs_row, segs_col, cosine, sine, *rest):
    last = pieces_of[0] != 0
    if last:
        second, key_in, value_in, query_in, rest = rest[0], rest[1], rest[2], rest[3], rest[4:]
        parts, (grads, key_rows, value_rows, out_grad, key_grad, value_grad) = rest[:3], rest[3:]
    else:
        second, (grads, key_grad, value_grad, key_rows, value_rows, out_grad) = rest[0], rest[1:]
    pieces = dict(zip(pieces_of, (first, second)))
    own = first.shape[1]
    head_width = query.shape[0]
    heads = head_width // HEAD_DIM
    weight, proj = weight_all[:, : 3 * head_width], weight_all[:, 3 * head_width :]
    half = HEAD_DIM // 2
    scale = HEAD_DIM ** (-0.5)
    for h in range(heads):
        rows = slice(h * HEAD_DIM, (h + 1) * HEAD_DIM)
        key_rows[h] = key[rows, :].astype(FULL).T.astype(LOW)
        value_rows[h] = value[rows, :].astype(FULL).T.astype(LOW)
    key_segs = jnp.where(segs_col[...] == 0, -1, segs_col[...])
    if last:
        grads[:head_width, : 2 * own] = query_in[...]
        key_grad[...] = key_in[...]
        value_grad[...] = value_in[...]
    else:
        key_grad[...] = jnp.zeros(key_grad.shape, FULL)
        value_grad[...] = jnp.zeros(value_grad.shape, FULL)

    def turn_back(grad, span, base, at):
        cos, sin = cosine[:, span], sine[:, span]
        one, two = grad[:half], grad[half:]
        grads[base + at : base + at + half, span] = (one * cos + two * sin).astype(LOW)
        grads[base + at + half : base + at + HEAD_DIM, span] = (two * cos - one * sin).astype(LOW)

    for e in pieces_of:
        span = slice(e * own, (e + 1) * own)
        allowed = key_segs == segs_row[:, span]
        out_grad[...] = dot(proj, pieces[e][...], (0, 0)).astype(LOW)
        for h in range(heads):
            rows = slice(h * HEAD_DIM, (h + 1) * HEAD_DIM)
            back = out_grad[rows, :]
            inner = jnp.sum(
                back.astype(FULL) * mixed[rows, span].astype(FULL), axis=0, keepdims=True
            )
            scores = dot(key_rows[h], query[rows, span], (1, 0))
            scores = jnp.where(allowed, scores, MASK_FILL)
            probability = jnp.exp(scores - logsum[h : h + 1, span])
            grad_probs = dot(value_rows[h], back, (1, 0))
            score_grad = (probability * (grad_probs - inner)).astype(LOW)
            value_grad[rows, :] += dot(back, probability.astype(LOW), (1, 1))
            key_grad[rows, :] += dot(query[rows, span], score_grad, (1, 1))
            turn_back(dot(key[rows, :], score_grad, (1, 0)) * scale, span, 0, h * HEAD_DIM)
    if not last:
        return
    for e in (3, 1, 2, 0):
        span = slice(e * own, (e + 1) * own)
        for h in range(heads):
            turn_back(key_grad[h * HEAD_DIM : (h + 1) * HEAD_DIM, span], span, head_width, h * HEAD_DIM)
        grads[2 * head_width :, span] = value_grad[:, span].astype(LOW)
        part_of(parts, e)[...] = dot(weight, grads[:, span], (1, 0)).astype(LOW)
        ship_part(parts, e)


def attend_weights(grid, grads, mixed, inputs_all, pieces_all, keep, send, total):
    count = grads.shape[0]
    total[:, :count] = dot(inputs_all[...], grads[...], (1, 1)).astype(LOW)
    total[:, count:] = dot(pieces_all[...], mixed[...], (1, 1)).astype(LOW)
    size = keep.shape[1]
    for j in range(grid.cols):
        send[j] = total[pl.ds(grid.half_start(grid.col() ^ j, 1 - grid.half(), size), size), :]
    ship(send)
    for j in range(grid.cols):
        keep[j] = total[pl.ds(grid.half_start(grid.col() ^ j, grid.half(), size), size), :]


def pair_sum(keep, got, *outs):
    for j, out in enumerate(outs):
        out[...] = (keep[j].astype(FULL) + got[j].astype(FULL)).astype(LOW)


def block_sum(*rest):
    total = rest[0][...].astype(FULL)
    for piece in rest[1:-1]:
        total = total + piece[...].astype(FULL)
    rest[-1][...] = total.astype(LOW)


def attn_weight_out(grid, own, other, qkv_out, proj_out, total):
    size = own.shape[0]
    total[pl.ds(grid.half_start(0, grid.half(), size), size), :] = own[...]
    total[pl.ds(grid.half_start(0, 1 - grid.half(), size), size), :] = other[...]
    width = qkv_out.shape[2]
    for i in range(3):
        qkv_out[i] = total[:, i * width : (i + 1) * width].astype(FULL)
    proj_out[...] = total[:, 3 * width :].astype(FULL).T


def feed_weight_out(*rest):
    parts, (up_out, bias_out, down_out) = rest[:-3], rest[-3:]
    total = parts[0][...].astype(FULL)
    for part in parts[1:]:
        total = total + part[...].astype(FULL)
    size, count = up_out.shape
    up_out[...] = total[:size, :count]
    down_out[...] = total[:size, count:]
    bias_out[...] = total[size, :count]


def finish_backward(grid, segs, mods, stream, grad_middle, small_in, part, near, far, *rest):
    outs, (grad_low, blocks) = rest[: grid.cols], rest[grid.cols :]
    pick = token_mods_of(mods[...], segs[...])
    chosen = slot_rows(segs[...])
    ones = jnp.ones(chosen.shape, LOW)
    input_grad = three_terms(part, near, far)
    normed, inverse = normalize(stream[...].astype(FULL))
    gain = column_of(mods, GAIN_ONE)
    grown = input_grad * (1.0 + pick(1))
    grad = grad_middle[...] + normalize_back(grown * gain, normed, inverse)
    grad_low[...] = grad.astype(LOW)
    size = grad.shape[0] // grid.cols
    own = grad.shape[1]
    for step in range(grid.cols):
        place = pl.ds(block_start(grid.source(step), size), size)
        outs[step][:, :own] = grad_low[place, :]
    shift = doc_sums(input_grad, chosen)[:SLOTS]
    scale = doc_sums(input_grad * normed * gain, chosen)[:SLOTS]
    norm_gain = doc_sums(grown * normed, ones)[:1]
    for c in range(grid.cols):
        span = slice(c * size, (c + 1) * size)
        blocks[c, :, :size] = small_in[:, span]
        blocks[c, :SLOTS, :size] = shift[:, span]
        blocks[c, SLOTS : 2 * SLOTS, :size] = scale[:, span]
        blocks[c, GAIN_ONE : GAIN_ONE + 1, :size] = norm_gain[:, span]
        blocks[c, STATS : STATS + 1, :size] = small_in[STATS : STATS + 1, :size]
    for step in range(grid.cols):
        terms = split(blocks[grid.source(step)].T, 2)
        outs[step][:, own:] = jnp.concatenate(terms, 1).astype(LOW)


def modulation_back(grid, slot_count, dp_count, *rest):
    times, (table, weight), rest = rest[:dp_count], rest[dp_count : dp_count + 2], rest[dp_count + 2 :]
    pieces, outs = rest[: 2 * dp_count], rest[2 * dp_count :]
    weight_out, bias_out, gain_one_out, gain_two_out, down_bias_out, stats_out, embed_out = outs[:7]
    embed, grads = outs[7:]
    per = grid.per_row
    embed[...] = jnp.zeros(embed.shape, FULL)
    size = grads.shape[2]
    total = jnp.zeros((LANES - 6 * SLOTS, size), FULL)
    for d in range(dp_count):
        for far in range(2):
            piece = pieces[2 * d + far]
            for s in range(2 * per):
                sequence = (grid.row() ^ (2 * far + s // per)) * per + s % per
                first = block_start(d * per * grid.rows + sequence, SLOTS)
                for slot in range(slot_count):
                    time = times[d][sequence, slot]
                    embed[pl.ds(first + slot, 1), :] = table[pl.ds(time, 1), :]
                for k in range(6):
                    grads[k, pl.ds(first, SLOTS), :] = piece[s, k * SLOTS : (k + 1) * SLOTS, :]
                total = total + piece[s, 6 * SLOTS :, :]
    for k in range(6):
        rows = grads[k]
        weight_out[k] = dot(rows, embed[...], (0, 0), PRECISE)
        bias_out[k : k + 1, :] = jnp.sum(rows, axis=0, keepdims=True)
        part = dot(rows, weight[k].astype(FULL), (1, 0), PRECISE)
        embed_out[...] = part if k == 0 else embed_out[...] + part
    gain_one_out[...] = total[GAIN_ONE - 6 * SLOTS]
    gain_two_out[...] = total[GAIN_TWO - 6 * SLOTS]
    down_bias_out[...] = total[DOWN_BIAS - 6 * SLOTS]
    squares = total[STATS - 6 * SLOTS : STATS - 6 * SLOTS + 1, :]
    stats_out[...] = jnp.sqrt(squares / squares[:, 3:4])[0, :3]


def table_sum(grid, slot_count, dp_count, *rest):
    times, parts, (table_out, total) = rest[:dp_count], rest[dp_count:-2], rest[-2:]
    found = parts[0][...]
    for part in parts[1:]:
        found = found + part[...]
    total[...] = found
    table_out[...] = jnp.zeros(table_out.shape, FULL)
    for d in range(dp_count):
        for sequence in range(grid.cols):
            for slot in range(slot_count):
                time = times[d][sequence, slot]
                at = (d * grid.cols + sequence) * SLOTS + slot
                table_out[pl.ds(time, 1), :] += total[at : at + 1, :]


def per_device(
    tokens,
    cotangent,
    segment_ids,
    doc_times,
    time_table,
    attn_gain,
    mlp_gain,
    mod_weight,
    mod_bias,
    qkv_weight,
    proj_weight,
    up_weight,
    up_bias,
    down_weight,
    down_bias,
):
    grid = Grid()
    dp_count = lax.axis_size("dp")
    width_local = tokens.shape[0]
    width = width_local * grid.cols
    own = tokens.shape[1] // grid.cols
    head_width = qkv_weight.shape[2]
    hidden_local = up_weight.shape[1]
    slot_count = doc_times.shape[1]
    cond_width = mod_weight.shape[2]
    if segment_ids.shape[0] != grid.cols * SEQ or own * grid.rows != SEQ or grid.rows != 4:
        raise ValueError("sequence split")
    low_tile = shape((width, own), LOW)
    full_tile = shape((width, own), FULL)
    low_piece = shape((width_local, own), LOW)
    part_tiles = [low_tile, low_tile, shape((2 * width, own), LOW)]

    part_rows = width_local // dp_count
    part_start = lax.axis_index("dp") * part_rows

    def gather_weight(parts):
        parts = [lax.dynamic_slice_in_dim(p, part_start, part_rows, 0) for p in parts]
        part = jnp.concatenate(parts, 1) if len(parts) > 1 else parts[0]
        return lax.all_gather(part, ("col", "dp"), axis=0, tiled=True)

    bundles = run(
        functools.partial(prepare, grid, slot_count), "prepare",
        [shape((width_local, 2 * own + 2 * LANES), LOW)] * grid.cols,
        [doc_times, time_table, mod_weight, mod_bias, attn_gain, mlp_gain,
         down_bias, tokens, cotangent],
        [pltpu.VMEM((SLOTS, cond_width), FULL), pltpu.VMEM((LANES, width_local), FULL),
         pltpu.VMEM((grid.per_row, width_local, 2 * LANES), LOW)],
        smem=1,
    )
    attn_block = run(
        pack, "pack", [shape((width_local, 4 * head_width), LOW)],
        after(bundles[:1], [qkv_weight.transpose(1, 0, 2), proj_weight]),
    )
    attn_weights = gather_weight(attn_block)

    bundles = relayout(bundles)
    segs_row, segs_col, segs_own, cosine, sine = run(
        functools.partial(places, grid, slot_count), "places",
        [shape((1, SEQ), jnp.int32), shape((SEQ, 1), jnp.int32), shape((1, own), jnp.int32)]
        + [shape((HEAD_DIM // 2, SEQ), FULL)] * 2,
        [segment_ids.reshape(-1, own)],
    )
    input_one, stream, cot, mods = run(
        functools.partial(first_norm, grid), "first_norm",
        [low_tile] * 3 + [shape((width, 2 * LANES), LOW)], [segs_own] + bundles,
    )

    def branch_filler(ready):
        [late] = after([ready], [cot])
        return run(branch_grad, "branch_grad", [low_tile], [segs_own, mods, late])

    rows_one, [branch] = gather_rows(input_one, branch_filler)
    branch_rows = gather_rows(branch)
    times = [doc_times] + [swap(doc_times, "dp", d) for d in range(1, dp_count)]
    rows_one[3:] = after([branch_rows[1]] + times[1:], rows_one[3:])

    feed_weights = gather_weight(after(rows_one[2:3] + [attn_weights], [up_weight, down_weight]))
    *parts, query, key, value, mixed, logsum = run(
        attend, "attend",
        part_tiles + [shape((head_width, SEQ), LOW)] * 4 + [shape((8, SEQ), FULL)],
        [attn_weights, cosine, sine] + rows_one + [segs_row, segs_col],
        [pltpu.VMEM((head_width // HEAD_DIM, SEQ, HEAD_DIM), LOW)],
    )
    attn_terms = scatter_rows(parts)
    input_two, middle, attn = run(
        second_norm, "second_norm", [low_tile, full_tile, low_tile],
        [segs_own, mods, stream] + attn_terms,
    )
    rows_two = gather_rows(input_two)
    hidden_tile = shape((hidden_local, own), LOW)
    sides = [side for e in FEED_ORDER for side in (rows_two[e], branch_rows[e])]
    found = run(
        feed_first, "feed_first", part_tiles * 2 + [hidden_tile] * 8, [feed_weights, up_bias] + sides
    )
    parts, results, hidden, pre_grad = found[:3], found[3:6], found[6:10], found[10:]

    def grads_filler(ready):
        late = after([ready], pre_grad)
        return run(
            feed_grads_of, "feed_grads",
            [shape((grid.cols, width_local + 16, 2 * hidden_local), LOW)],
            [Joined(late), Joined(rows_two), Joined(hidden), Joined(branch_rows)],
        )

    input_terms, [feed_grads] = scatter_rows(parts, grads_filler, True)
    feed_grads = lax.psum_scatter(
        feed_grads.reshape(-1, 2 * hidden_local), "col", scatter_dimension=0, tiled=True
    )
    grad_middle, grad_attn, input_grad = run(
        middle_grad, "middle_grad", [full_tile, low_tile, low_tile],
        [segs_own, mods, middle, cot] + input_terms,
    )

    mlp_near, mlp_total = scatter_near(results)
    head_tile = shape((head_width, SEQ), FULL)
    back_scratch = [pltpu.VMEM((head_width // HEAD_DIM, SEQ, HEAD_DIM), LOW)] * 2 + [
        pltpu.VMEM((head_width, own), LOW)
    ]
    saved = [query, mixed, logsum, segs_row, segs_col, cosine, sine]

    def first_filler(ready):
        return run(
            functools.partial(attend_back, (0, 1)), "attend_back_first",
            [shape((head_width, 2 * own), LOW), head_tile, head_tile],
            [key, value, attn_weights, grad_attn] + saved + [ready], back_scratch,
        )

    attn_rows, (query_grad, key_grad, value_grad) = gather_rows(grad_attn, first_filler)
    [mlp_total] = after(attn_rows[2:3], [mlp_total])
    mlp_terms = [results[0], mlp_near, swap(mlp_total, "row", 2)]
    *parts, qkv_grads = run(
        functools.partial(attend_back, (2, 3)), "attend_back_last",
        part_tiles + [shape((3 * head_width, SEQ), LOW)],
        [key, value, attn_weights, attn_rows[2]] + saved
        + [attn_rows[3], key_grad, value_grad, query_grad],
        back_scratch + [pltpu.VMEM((head_width, SEQ), FULL)] * 2,
    )

    def back_filler(ready):
        [late] = after([ready], [qkv_grads])
        blocks = run(
            functools.partial(attend_weights, grid), "attend_weights",
            [shape((grid.cols, width_local // 2, 4 * head_width), LOW)] * 2,
            [late, mixed, Joined(rows_one), Joined(attn_rows)], [pltpu.VMEM((width, 4 * head_width), LOW)],
        )
        [first] = after(blocks[:1], mlp_terms[:1])
        found = run(
            functools.partial(finish_forward, grid), "finish_forward",
            [low_piece] * grid.cols + [shape((LANES, width), FULL)],
            [segs_own, mods, middle, cot, attn, grad_middle, input_grad, first] + mlp_terms[1:],
            [pltpu.VMEM((width, own), LOW)],
        )
        return found + blocks

    parts[2:] = after(mlp_terms[2:], parts[2:])
    back_terms, found = scatter_rows(parts, back_filler, True)
    result_chunks, small, attn_grads = found[: grid.cols], found[grid.cols], found[grid.cols + 1 :]
    bundles = run(
        functools.partial(finish_backward, grid), "finish_backward",
        [shape((width_local, own + 2 * LANES), LOW)] * grid.cols,
        [segs_own, mods, stream, grad_middle, small] + back_terms,
        [pltpu.VMEM((width, own), LOW), pltpu.VMEM((grid.cols, LANES, width_local), FULL)],
    )
    out_tile = shape((width_local, grid.cols * own), LOW)
    bundles = relayout(bundles, back=True)
    tokens_grad, small = run(
        functools.partial(unbundle, grid), "unbundle",
        [out_tile, shape((grid.per_row, LANES, width_local), FULL)], bundles,
    )
    [block_output] = run(
        functools.partial(join, grid), "join", [out_tile],
        relayout(after(bundles, result_chunks), back=True),
    )

    small = jnp.concatenate([small, swap(small, "row", 1)], 0)
    pieces = []
    for d in range(dp_count):
        for far in range(2):
            count = dp_count * grid.rows
            pairs = [(i, i ^ (d * grid.rows + 2 * far)) for i in range(count)]
            pieces.append(lax.ppermute(small, ("dp", "row"), pairs) if d or far else small)
    seq_total = grid.cols * dp_count
    vector = shape((width_local,), FULL)
    embed_tile = shape((seq_total * SLOTS, cond_width), FULL)
    weight_out, bias_out, gain_one_out, gain_two_out, down_bias_out, stats, embed = run(
        functools.partial(modulation_back, grid, slot_count, dp_count), "modulation_back",
        [
            shape((6, width_local, cond_width), FULL), shape((6, width_local), FULL),
            vector, vector, vector, shape((3,), FULL), embed_tile,
        ],
        times + [time_table, mod_weight] + pieces,
        [pltpu.VMEM((seq_total * SLOTS, cond_width), FULL),
         pltpu.VMEM((6, seq_total * SLOTS, width_local), FULL)],
        smem=dp_count,
    )
    [table_out] = run(
        functools.partial(table_sum, grid, slot_count, dp_count), "table_sum",
        [shape(time_table.shape, FULL)],
        times + [embed] + [swap(embed, "col", j) for j in range(1, grid.cols)],
        [pltpu.VMEM((seq_total * SLOTS, cond_width), FULL)], smem=dp_count,
    )

    def all_dp(part):
        return [part] + [swap(part, "dp", d) for d in range(1, dp_count)]

    half_tile = shape((width_local // 2, 4 * head_width), LOW)
    pieces = run(pair_sum, "pair_sum", [half_tile] * grid.cols, [attn_grads[0], swap(attn_grads[1], "dp", 1)])
    pieces = pieces[:1] + [swap(pieces[j], "col", j) for j in range(1, grid.cols)]
    [attn_half] = run(block_sum, "block_sum", [half_tile], pieces)
    bit = 2
    while bit < dp_count:
        attn_half = (attn_half.astype(FULL) + swap(attn_half, "dp", bit).astype(FULL)).astype(LOW)
        bit *= 2
    up_out, up_bias_out, down_out = run(
        feed_weight_out, "feed_weight_out",
        [shape(up_weight.shape, FULL), shape(up_bias.shape, FULL), shape(down_weight.shape, FULL)],
        all_dp(after(bundles, [feed_grads])[0]),
    )
    qkv_out, proj_out = run(
        functools.partial(attn_weight_out, grid), "attn_weight_out",
        [shape((3, width_local, head_width), FULL), shape(proj_weight.shape, FULL)],
        [attn_half, swap(attn_half, "dp", 1)], [pltpu.VMEM((width_local, 4 * head_width), LOW)],
    )
    return (
        block_output,
        tokens_grad,
        table_out,
        gain_one_out,
        gain_two_out,
        weight_out,
        bias_out,
        qkv_out.transpose(1, 0, 2),
        proj_out,
        up_out,
        up_bias_out,
        down_out,
        down_bias_out,
        stats,
    )


def solution(mesh):
    return jax.shard_map(
        per_device,
        mesh=mesh,
        in_specs=(
            P("col", ("dp", "row")),
            P("col", ("dp", "row")),
            P("dp"),
            P("dp", None),
            P(),
            P("col"),
            P("col"),
            P(None, "col", None),
            P(None, "col"),
            P("col", None, "row"),
            P("row", "col"),
            P("col", "row"),
            P("row"),
            P("col", "row"),
            P("col"),
        ),
        out_specs=(
            P("col", ("dp", "row")),
            P("col", ("dp", "row")),
            P(),
            P("col"),
            P("col"),
            P(None, "col", None),
            P(None, "col"),
            P("col", None, "row"),
            P("row", "col"),
            P("col", "row"),
            P("row"),
            P("col", "row"),
            P("col"),
            P(),
        ),
        check_vma=False,
    )
```
